32 devices in a mesh: group: 8 (over z, x), fsdp: 4 (over y, core).
Axes of the slice: x: 2, y: 2, z: 4, core: 2. Of those that a mesh axis runs over, the one named last changes fastest.
Arguments:
- mol_qkv: bfloat16 [64, 128, 3, 4096], P('group', None, None, 'fsdp'), may hold values from -12 to 12
- pair_list: int32 [128, 3], replicated, may hold values from 0 to 7, as said below
- head_proj: bfloat16 [32, 128, 256], P('fsdp'), may hold values from -0.5 to 0.5
- head_out: float32 [32, 256], P('fsdp'), may hold values from -0.375 to 0.375
- labels: int32 [128], P('group'), may hold values 0 or 1
Outputs:
- mol_grad: bfloat16 [64, 128, 3, 4096], P('group', None, None, 'fsdp')
- pair_logits: float32 [128], P('group')
- mean_loss: float32 [], replicated
The draws below stay inside these ranges and needn't reach their ends.
Inputs may be any that keep to these rules, and one draw needn't show every extreme that they name: `pair_list`: pair p belongs to owner p // 16; column 0 is the first molecule's index among the owner's 8 molecules, column 1 the group index that holds the second molecule, column 2 its index among that holder's 8 molecules; molecule m is held by group m // 8. `pair_list`: among one owner's pairs, at most 4 take their second molecule from any one holder, and those name at most 2 different molecules; every owner reaches both bounds.
All inputs are finite; a program needn't handle non-finite values. No bound on the sum of `labels` on one device may be relied on, other than what follows from the above.
Results may differ from the reference program's by a relative error of at most 0.0075.
Values may be sent and summed in bfloat16 or wider, within the bound.
A program may use at most 192 MiB of HBM per device.

```python
import jax
import jax.numpy as jnp
from jax import lax

HEADS = 32
HD = 128
R = 256
L = 128
MOL_DEV = 8
MOLS = 64
PAIR_DEV = 16
PAIRS = 128
CAP_PAIR = 4
CAP_MOL = 2


def draw_mol_qkv(key, part):
    keys = jax.random.split(jax.random.fold_in(key, 11), 1)
    shape = (MOLS, L, 3, HEADS * HD)
    values = jax.random.normal(keys[0], shape, jnp.float32)
    return jnp.clip(values, -6.0, 6.0).astype(jnp.bfloat16)


def draw_pair_list(key, part):
    keys = jax.random.split(jax.random.fold_in(key, 23), 7)
    owners = PAIRS // PAIR_DEV
    position = jnp.arange(PAIR_DEV, dtype=jnp.int32)[None, :]
    hub_holder = jax.random.randint(keys[0], (owners, 1), 0, owners)
    offset_base = jax.random.randint(keys[1], (owners, 1), 0, owners - 1)
    other_holder = (hub_holder + 1 + (position - CAP_PAIR + offset_base) % (owners - 1)) % owners
    holder = jnp.where(position < CAP_PAIR, hub_holder, other_holder)
    base_mol = jax.random.randint(keys[2], (owners, 1), 0, MOL_DEV)
    hub_member = (base_mol + position % CAP_MOL) % MOL_DEV
    random_member = jax.random.randint(keys[3], (owners, PAIR_DEV), 0, MOL_DEV)
    member = jnp.where(position < CAP_PAIR, hub_member, random_member)
    first_mol = jnp.minimum(jax.random.randint(keys[4], (owners, PAIR_DEV), 0, MOL_DEV), jax.random.randint(keys[5], (owners, PAIR_DEV), 0, MOL_DEV))
    shuffle_keys = jax.random.randint(keys[6], (owners, PAIR_DEV), 0, 4 * PAIR_DEV) * PAIR_DEV + position
    shuffle = jnp.argsort(shuffle_keys, axis=1, stable=True)
    table = jnp.stack([first_mol, holder, member], axis=2)
    table = jnp.take_along_axis(table, shuffle[:, :, None], axis=1)
    return table.reshape(PAIRS, 3).astype(jnp.int32)


def touch_ends(result, rng, low, high):
    longest = result.shape.index(max(result.shape))
    spots = []
    for shift in (0, 1):
        where = [jax.random.randint(jax.random.fold_in(rng, axis), (), 0, length) for axis, length in enumerate(result.shape)]
        where[longest] = (where[longest] + shift) % result.shape[longest]
        spots.append(tuple(where))
    return result.at[spots[0]].set(low).at[spots[1]].set(high)


def shard_levels(rng, dims, cuts, smallest, largest):
    def one(axis_at, parts):
        draws = jax.random.uniform(jax.random.fold_in(jax.random.fold_in(rng, 6), axis_at), (parts,), jnp.float32, smallest / len(cuts), largest / len(cuts))
        return jnp.repeat(jnp.exp(draws), dims[axis_at] // parts).reshape((-1,) + (1,) * (len(dims) - axis_at - 1))

    loudness = one(*cuts[0])
    for cut in cuts[1:]:
        loudness = loudness * one(*cut)
    return loudness


def scatter_about(key, extent, scale, reach, shards=(), kind=jnp.bfloat16):
    result = jax.random.normal(key, extent, jnp.float32) * scale
    if len(shards) > 0:
        result = shard_levels(key, extent, shards, -0.22, 0.18) * result
    return jnp.clip(result, min=-reach, max=reach).astype(kind)


def setup_inputs(seed: int = 0) -> dict:
    arg_keys = jax.random.split(jax.random.key(seed), 6)
    return {
        "mol_qkv": draw_mol_qkv(jax.random.fold_in(arg_keys[5], 71), 0),
        "pair_list": draw_pair_list(jax.random.fold_in(arg_keys[5], 71), 0),
        "head_proj": scatter_about(arg_keys[2], (HEADS, HD, R), HD ** -0.5, 0.5, ((0, 4),)),
        "head_out": scatter_about(arg_keys[3], (HEADS, R), R ** -0.5, 0.375, ((0, 4),), jnp.float32),
        "labels": touch_ends((jax.random.randint(arg_keys[4], (PAIRS,), 0, 2) < 1).astype(jnp.int32), jax.random.fold_in(arg_keys[4], 1), 0, 1),
    }


loss_scale = 8192.0


def split_heads(rows_in, component, heads, head_dim):
    return rows_in[:, :, component].reshape(rows_in.shape[0], rows_in.shape[1], heads, head_dim)


def forward(query_rows, key_rows, value_rows, head_proj, head_out, inv_root, length):
    scores = jnp.einsum("plhd,pmhd->phlm", query_rows.astype(jnp.float32), key_rows.astype(jnp.float32)) * inv_root
    row_max = jnp.max(scores, axis=-1, keepdims=True)
    lifted = jnp.exp(scores - row_max)
    attn_weights = lifted / jnp.sum(lifted, axis=-1, keepdims=True)
    weights_bf = attn_weights.astype(jnp.bfloat16)
    context = jnp.einsum("phlm,pmhd->plhd", weights_bf.astype(jnp.float32), value_rows.astype(jnp.float32)).astype(jnp.bfloat16)
    hidden = jnp.einsum("plhd,hdr->plhr", context.astype(jnp.float32), head_proj.astype(jnp.float32))
    partial_value = jnp.sum(jax.nn.silu(hidden) * head_out[None, None], axis=(1, 2, 3)) / length
    return partial_value, (attn_weights, weights_bf, hidden)


def backward(query_rows, key_rows, value_rows, head_proj, head_out, saved, grad_out, inv_root, length):
    attn_weights, weights_bf, hidden = saved
    sigmoid_h = jax.nn.sigmoid(hidden)
    silu_slope = sigmoid_h * (1.0 + hidden * (1.0 - sigmoid_h))
    dhidden = (grad_out[:, None, None, None] / length * head_out[None, None] * silu_slope).astype(jnp.bfloat16)
    dcontext = jnp.einsum("plhr,hdr->plhd", dhidden.astype(jnp.float32), head_proj.astype(jnp.float32)).astype(jnp.bfloat16)
    dvalues = jnp.einsum("phlm,plhd->pmhd", weights_bf.astype(jnp.float32), dcontext.astype(jnp.float32))
    dweights = jnp.einsum("plhd,pmhd->phlm", dcontext.astype(jnp.float32), value_rows.astype(jnp.float32))
    dscores = (attn_weights * (dweights - jnp.sum(dweights * attn_weights, axis=-1, keepdims=True)) * inv_root).astype(jnp.bfloat16)
    dqueries = jnp.einsum("phlm,pmhd->plhd", dscores.astype(jnp.float32), key_rows.astype(jnp.float32))
    dkey_rows = jnp.einsum("phlm,plhd->pmhd", dscores.astype(jnp.float32), query_rows.astype(jnp.float32))
    return dqueries, dkey_rows, dvalues


def reference(mol_qkv, pair_list, head_proj, head_out, labels):
    inv_root = HD ** -0.5
    owners = PAIRS // PAIR_DEV
    blocks = pair_list.reshape(owners, PAIR_DEV, 3)
    block_labels_all = labels.reshape(owners, PAIR_DEV)
    position = jnp.arange(PAIR_DEV, dtype=jnp.int32)

    def per_block(accum, inputs):
        block_rows, block_labels, owner = inputs
        first_mol = (owner * MOL_DEV + block_rows[:, 0]).astype(jnp.int32)
        second_mol = (block_rows[:, 1] * MOL_DEV + block_rows[:, 2]).astype(jnp.int32)
        own_rows = mol_qkv[first_mol]
        partner_rows = mol_qkv[second_mol]
        qa, ka, va = [split_heads(own_rows, c, HEADS, HD) for c in range(3)]
        qb, kb, vb = [split_heads(partner_rows, c, HEADS, HD) for c in range(3)]
        part_ab, saved_ab = forward(qa, kb, vb, head_proj, head_out, inv_root, L)
        part_ba, saved_ba = forward(qb, ka, va, head_proj, head_out, inv_root, L)
        logits = part_ab + part_ba
        targets = block_labels.astype(jnp.float32)
        loss_terms = jax.nn.softplus(logits) - targets * logits
        grad_out = (jax.nn.sigmoid(logits) - targets) * loss_scale
        dq_a, dk_b, dv_b = backward(qa, kb, vb, head_proj, head_out, saved_ab, grad_out, inv_root, L)
        dq_b, dk_a, dv_a = backward(qb, ka, va, head_proj, head_out, saved_ba, grad_out, inv_root, L)
        grad_first = jnp.stack([dq_a, dk_a, dv_a], axis=2).reshape(PAIR_DEV, L, 3, HEADS * HD)
        grad_second = jnp.stack([dq_b, dk_b, dv_b], axis=2).reshape(PAIR_DEV, L, 3, HEADS * HD)
        matches = second_mol[:, None] == second_mol[None, :]
        earlier = matches & (position[None, :] < position[:, None])
        leading = jnp.logical_not(jnp.any(earlier, axis=1))
        key_sums = jnp.einsum("pq,qlcz->plcz", matches.astype(jnp.float32), grad_second, precision=lax.Precision.HIGHEST)
        rounded = lax.optimization_barrier(key_sums.astype(jnp.bfloat16)).astype(jnp.float32)
        partner_term = jnp.where(leading[:, None, None, None], rounded, jnp.zeros_like(rounded))
        accum = accum.at[first_mol].add(grad_first)
        accum = accum.at[second_mol].add(partner_term)
        return accum, (logits, jnp.sum(loss_terms))

    accum0 = jnp.zeros((MOLS, L, 3, HEADS * HD), jnp.float32)
    accum, (logits_all, loss_sums) = lax.scan(per_block, accum0, (blocks, block_labels_all, jnp.arange(owners, dtype=jnp.int32)))
    return accum.astype(jnp.bfloat16), logits_all.reshape(PAIRS), jnp.sum(loss_sums) / PAIRS
```

```python
import functools

import jax
import jax.numpy as jnp
from jax import lax
from jax.experimental import pallas as pl
from jax.experimental.pallas import tpu as pltpu
from jax.sharding import PartitionSpec as P

MESH = pl.DeviceIdType.MESH
loss_scale = 8192.0
row_block = 16

NN = (((1,), (0,)), ((), ()))
NT = (((1,), (1,)), ((), ()))


def mm(a, b, dims=NN):
    return lax.dot_general(a, b, dims, preferred_element_type=jnp.float32)


def params(mib, **more):
    return pltpu.CompilerParams(vmem_limit_bytes=mib * 1024 * 1024, **more)


def ring_of(groups):
    return list(range(0, groups, 2)) + list(range(groups - 1, 0, -2))


def place_of(group, groups):
    return jnp.where(group % 2 == 0, group // 2, groups - 1 - group // 2)


def ahead_step(d, groups):
    return groups - 1 if 2 * d == groups else 2 * d


def behind_step(d, groups):
    return groups - 1 if 2 * d == groups else 2 * d - 1


def list_kernel(groups, slots, per_owner, me_ref, pairs_ref, x_ref, y_ref, p_ref, n_ref):
    me = me_ref[0]
    my_place = place_of(me, groups)
    total = pairs_ref.shape[0] // 3

    def clear(i, carry):
        x_ref[i] = 0
        y_ref[i] = 0
        p_ref[i] = -1
        return carry

    lax.fori_loop(0, groups * slots, clear, 0)
    for t in range(groups):
        n_ref[t] = 0

    def add(group, x, y, p):
        behind = lax.rem(my_place - place_of(group, groups) + groups, groups)
        step = jnp.where(behind * 2 < groups, 2 * behind - 1, 2 * (groups - behind))
        step = jnp.where(behind == 0, 0, jnp.where(behind * 2 == groups, groups - 1, step))
        at = n_ref[step]
        spot = step * slots + at
        x_ref[spot] = x
        y_ref[spot] = y
        p_ref[spot] = p
        n_ref[step] = at + 1

    def visit(p, carry):
        owner = p // per_owner
        first = pairs_ref[3 * p]
        holder = pairs_ref[3 * p + 1]
        member = pairs_ref[3 * p + 2]

        @pl.when(owner == me)
        def _():
            add(holder, member, first, p)

        @pl.when(holder == me)
        def _():
            add(owner, first, member, p)

        return carry

    lax.fori_loop(0, total, visit, 0)


def make_lists(me, pair_list, groups, slots, per_owner):
    smem = pl.BlockSpec(memory_space=pltpu.SMEM)
    table = jax.ShapeDtypeStruct((groups * slots,), jnp.int32)
    return pl.pallas_call(
        functools.partial(list_kernel, groups, slots, per_owner),
        in_specs=[smem, smem],
        out_specs=[smem] * 4,
        out_shape=[table, table, table, jax.ShapeDtypeStruct((groups,), jnp.int32)],
        cost_estimate=pl.CostEstimate(flops=1000, bytes_accessed=4000, transcendentals=0),
    )(me, pair_list.reshape(-1))


def turn_kernel(head_dim, k_ref, v_ref, kt_ref, vt_ref):
    for h in range(kt_ref.shape[1]):
        cols = slice(h * head_dim, (h + 1) * head_dim)
        kt_ref[0, h] = k_ref[0, 0, :, cols].T
        vt_ref[0, h] = v_ref[0, 0, :, cols].T


def turn(mols, heads, head_dim):
    count, _, length, width = mols.shape
    out = jax.ShapeDtypeStruct((count, heads, head_dim, length), jnp.bfloat16)
    out_spec = pl.BlockSpec((1, heads, head_dim, length), lambda i: (i, 0, 0, 0))
    return pl.pallas_call(
        functools.partial(turn_kernel, head_dim),
        grid=(count,),
        in_specs=[
            pl.BlockSpec((1, 1, length, width), lambda i: (i, 1, 0, 0)),
            pl.BlockSpec((1, 1, length, width), lambda i: (i, 2, 0, 0)),
        ],
        out_specs=[out_spec, out_spec],
        out_shape=[out, out],
        compiler_params=params(16),
        cost_estimate=pl.CostEstimate(
            flops=8 * count * length * width,
            bytes_accessed=8 * count * length * width,
            transcendentals=0,
        ),
    )(mols, mols)


def unit_kernel(head_dim, step, slots, half, *refs):
    x_ref, _, n_ref, q0_ref, q1_ref, k_ref, v_ref, kt_ref, vt_ref = refs[:9]
    proj_ref, turned_ref, out_ref = refs[9:12]
    part_ref, dq_ref, dk_ref, dv_ref = refs[-4:]
    coef = 1.4426950408889634 * head_dim ** (-0.5)
    heads = proj_ref.shape[0]
    length = k_ref.shape[2]
    u = pl.program_id(0)

    @pl.when(u < n_ref[step])
    def _():
        use_low = x_ref[step * slots + u] < half
        total = jnp.zeros((8, length), jnp.float32)
        hs = range(heads)

        def col(h):
            return slice(h * head_dim, (h + 1) * head_dim)

        q = [jnp.where(use_low, q0_ref[0, :, col(h)], q1_ref[0, :, col(h)]) for h in hs]
        s = [mm(k_ref[0, 0, :, col(h)], q[h], NT) for h in hs]
        w = [jnp.exp2((a - jnp.max(a, axis=0, keepdims=True)) * coef) for a in s]
        w = [a * (1.0 / jnp.sum(a, axis=0, keepdims=True)) for a in w]
        wb = [a.astype(jnp.bfloat16) for a in w]
        context = [mm(vt_ref[0, h], wb[h]).astype(jnp.bfloat16) for h in hs]
        dhidden = []
        for h in hs:
            hidden = mm(turned_ref[h], context[h])
            bend = jnp.tanh(hidden)
            first = (1.0 + bend) * out_ref[h]
            silu = hidden * first
            total += jnp.sum(silu.reshape(-1, 8, length), axis=0)
            dhidden.append((first + silu * (1.0 - bend)).astype(jnp.bfloat16))
        dcontext = [mm(proj_ref[h], dhidden[h]).astype(jnp.bfloat16) for h in hs]
        dw = [mm(v_ref[0, 0, :, col(h)], dcontext[h]) for h in hs]
        for h in hs:
            dv_ref[0, :, col(h)] = mm(wb[h], dcontext[h], NT).astype(jnp.bfloat16)
        ds = []
        for h in hs:
            inner = jnp.sum(dw[h] * w[h], axis=0, keepdims=True)
            ds.append((w[h] * (dw[h] - inner)).astype(jnp.bfloat16))
        for h in hs:
            dq_ref[0, h * head_dim : (h + 1) * head_dim] = mm(kt_ref[0, h], ds[h]).astype(
                jnp.bfloat16
            )
            dk_ref[0, :, col(h)] = mm(ds[h], q[h]).astype(jnp.bfloat16)
        part_ref[0] = total


def run_units(step, slots, lists, q0, q1, mols, turned_kv, weights, held):
    unit_x, unit_y, _, counts = lists
    proj, turned, readout = weights
    heads, head_dim, inner = proj.shape
    _, _, length, width = mols.shape
    all_units = unit_x.shape[0]
    base = step * slots
    half = q0.shape[0]

    def at(u, n):
        return base + jnp.maximum(jnp.minimum(u, n[step] - 1), 0)

    def whole(a):
        return pl.BlockSpec(a.shape, lambda u, x, y, n: (0,) * a.ndim)

    def row_map(u, x, y, n):
        return (at(u, n), 0, 0)

    rows = jax.ShapeDtypeStruct((all_units, length, width), jnp.bfloat16)
    row_spec = pl.BlockSpec((1, length, width), row_map)
    kv_t = pl.BlockSpec((1, heads, head_dim, length), lambda u, x, y, n: (y[at(u, n)], 0, 0, 0))
    out_shape = [
        jax.ShapeDtypeStruct((all_units, 8, length), jnp.float32),
        jax.ShapeDtypeStruct((all_units, width, length), jnp.bfloat16),
        rows,
        rows,
    ]
    in_specs = [
        pl.BlockSpec(
            (1, length, width), lambda u, x, y, n: (jnp.minimum(x[at(u, n)], half - 1), 0, 0)
        ),
        pl.BlockSpec(
            (1, length, width), lambda u, x, y, n: (jnp.maximum(x[at(u, n)] - half, 0), 0, 0)
        ),
        pl.BlockSpec((1, 1, length, width), lambda u, x, y, n: (y[at(u, n)], 1, 0, 0)),
        pl.BlockSpec((1, 1, length, width), lambda u, x, y, n: (y[at(u, n)], 2, 0, 0)),
        kv_t,
        kv_t,
        whole(proj),
        whole(turned),
        whole(readout),
    ]
    operands = [q0, q1, mols, mols, *turned_kv, proj, turned, readout]
    aliases = {}
    if held is not None:
        aliases = {3 + len(operands) + i: i for i in range(4)}
        in_specs += [pl.BlockSpec(memory_space=pl.ANY)] * 4
        operands += list(held)
    return pl.pallas_call(
        functools.partial(unit_kernel, head_dim, step, slots, half),
        grid_spec=pltpu.PrefetchScalarGridSpec(
            num_scalar_prefetch=3,
            grid=(slots,),
            in_specs=in_specs,
            out_specs=[
                pl.BlockSpec((1, 8, length), row_map),
                pl.BlockSpec((1, width, length), row_map),
                row_spec,
                row_spec,
            ],
        ),
        out_shape=out_shape,
        input_output_aliases=aliases,
        compiler_params=params(48, dimension_semantics=("arbitrary",)),
        cost_estimate=pl.CostEstimate(
            flops=10 * slots * heads * length * length * head_dim,
            bytes_accessed=6 * slots * length * width,
            transcendentals=slots * heads * length * (length + inner) // 2,
        ),
    )(unit_x, unit_y, counts, *operands)


def logit_kernel(length, groups, shards, part_ref, hot_ref, targets_ref, *refs):
    logits_ref, scale_ref, near, far, near_send, near_recv, far_send, far_recv = refs
    g = lax.axis_index("group")
    f = lax.axis_index("fsdp")
    barrier = pltpu.get_barrier_semaphore()
    for d in range(1, shards):
        other = lax.rem(f + d, shards)
        pl.semaphore_signal(barrier, inc=1, device_id=(g, other), device_id_type=MESH)
    for d in range(1, groups):
        other = lax.rem(g + d, groups)
        pl.semaphore_signal(barrier, inc=1, device_id=(other, f), device_id_type=MESH)

    hot = hot_ref[...]
    mine = jnp.sum(part_ref[...], axis=1)
    used = jnp.max(hot, axis=1, keepdims=True) > 0.0
    mine = jnp.sum(jnp.where(used, mine, 0.0), axis=1, keepdims=True)
    terms = jnp.sum(mine * hot, axis=0, keepdims=True) * (1.0 / length)
    pl.semaphore_wait(barrier, shards - 1 + groups - 1)

    near[f] = jnp.broadcast_to(terms, near.shape[1:])
    copies = []
    for d in range(1, shards):
        other = lax.rem(f + d, shards)
        copy = pltpu.make_async_remote_copy(
            src_ref=near.at[f],
            dst_ref=near.at[f],
            send_sem=near_send.at[d - 1],
            recv_sem=near_recv.at[d - 1],
            device_id=(g, other),
            device_id_type=MESH,
        )
        copy.start()
        copies.append(copy)
    for copy in copies:
        copy.wait()
    summed = near[0]
    for i in range(1, shards):
        summed = summed + near[i]
    row = lax.broadcasted_iota(jnp.int32, summed.shape, 0)
    far[g] = jnp.where(row == 0, summed, jnp.broadcast_to(targets_ref[...], summed.shape))
    copies = []
    for d in range(1, groups):
        other = lax.rem(g + d, groups)
        copy = pltpu.make_async_remote_copy(
            src_ref=far.at[g],
            dst_ref=far.at[g],
            send_sem=far_send.at[d - 1],
            recv_sem=far_recv.at[d - 1],
            device_id=(other, f),
            device_id_type=MESH,
        )
        copy.start()
        copies.append(copy)
    for copy in copies:
        copy.wait()
    both = far[0]
    for i in range(1, groups):
        both = both + far[i]
    logits_ref[...] = both
    logits, targets = both[0:1], both[1:2]
    grad = (jax.nn.sigmoid(logits) - targets) * (loss_scale / length)
    scale_ref[...] = jnp.broadcast_to(
        jnp.sum(hot * grad, axis=1, keepdims=True), scale_ref.shape
    )


def run_logits(length, part, hot, targets, groups, shards):
    units, total = hot.shape
    vmem = pl.BlockSpec(memory_space=pltpu.VMEM)
    return pl.pallas_call(
        functools.partial(logit_kernel, length, groups, shards),
        in_specs=[vmem] * 3,
        out_specs=[vmem] * 2,
        out_shape=[
            jax.ShapeDtypeStruct((8, total), jnp.float32),
            jax.ShapeDtypeStruct((units, length), jnp.float32),
        ],
        scratch_shapes=[
            pltpu.VMEM((shards, 8, total), jnp.float32),
            pltpu.VMEM((groups, 8, total), jnp.float32),
            pltpu.SemaphoreType.DMA((shards - 1,)),
            pltpu.SemaphoreType.DMA((shards - 1,)),
            pltpu.SemaphoreType.DMA((groups - 1,)),
            pltpu.SemaphoreType.DMA((groups - 1,)),
        ],
        compiler_params=params(16, collective_id=0, has_side_effects=True),
        cost_estimate=pl.CostEstimate(
            flops=20000, bytes_accessed=4 * part.size, transcendentals=1000
        ),
    )(part, hot, targets)


def hop_kernel(step, slots, low, factor, x_ref, n_ref, *refs):
    scale_ref, dq_ref = refs[:2]
    out_ref, acc = refs[-2:]
    mol = low + pl.program_id(0)
    if len(refs) == 5:
        acc[...] = refs[2][0].astype(jnp.float32)
    else:
        acc[...] = jnp.zeros_like(acc)

    def visit(u, carry):
        @pl.when(x_ref[step * slots + u] == mol)
        def _():
            g = scale_ref[pl.ds(step * slots + u, 1), :] * factor
            acc[...] += g * dq_ref[u].astype(jnp.float32)

        return carry

    lax.fori_loop(0, n_ref[step], visit, 0)
    out_ref[0] = acc[...].astype(jnp.bfloat16)


def run_hop(step, slots, low, mols, factor, unit_x, counts, scale, dq, arrived):
    _, width, length = dq.shape
    spec = pl.BlockSpec((1, width, length), lambda i, x, n: (i, 0, 0))
    more = [] if arrived is None else [arrived]
    return pl.pallas_call(
        functools.partial(hop_kernel, step, slots, low, factor),
        grid_spec=pltpu.PrefetchScalarGridSpec(
            num_scalar_prefetch=2,
            grid=(mols,),
            in_specs=[
                pl.BlockSpec(scale.shape, lambda i, x, n: (0, 0)),
                pl.BlockSpec((slots, width, length), lambda i, x, n: (step, 0, 0)),
            ]
            + [spec] * len(more),
            out_specs=spec,
            scratch_shapes=[pltpu.VMEM((width, length), jnp.float32)],
        ),
        out_shape=jax.ShapeDtypeStruct((mols, width, length), jnp.bfloat16),
        compiler_params=params(24, dimension_semantics=("arbitrary",)),
        cost_estimate=pl.CostEstimate(
            flops=4 * slots * width * length,
            bytes_accessed=2 * (slots + 2 * mols) * width * length,
            transcendentals=0,
        ),
    )(unit_x, counts, scale, dq, *more)


def sum_kernel(slots, factor, y_ref, n_ref, scale_ref, dk_ref, dv_ref, out_ref, sk, sv):
    sk[...] = jnp.zeros_like(sk)
    sv[...] = jnp.zeros_like(sv)
    repeat = dk_ref.shape[2] // scale_ref.shape[1]

    for t in range(n_ref.shape[0]):

        def visit(i, carry, base=t * slots):
            u = base + i
            y = y_ref[u]
            g = jnp.concatenate([scale_ref[pl.ds(u, 1), :]] * repeat, axis=1)
            sk[y] += (g * factor) * dk_ref[u].astype(jnp.float32)
            sv[y] += g * dv_ref[u].astype(jnp.float32)
            return carry

        lax.fori_loop(0, n_ref[t], visit, 0)
    out_ref[:, 1] = sk[...].astype(jnp.bfloat16)
    out_ref[:, 2] = sv[...].astype(jnp.bfloat16)


def run_sums(slots, mols, factor, unit_y, counts, scale, dk, dv):
    units, length, width = dk.shape
    in_spec = pl.BlockSpec((units, row_block, width), lambda i, y, n: (0, i, 0))
    return pl.pallas_call(
        functools.partial(sum_kernel, slots, factor),
        grid_spec=pltpu.PrefetchScalarGridSpec(
            num_scalar_prefetch=2,
            grid=(length // row_block,),
            in_specs=[pl.BlockSpec(scale.shape, lambda i, y, n: (0, 0)), in_spec, in_spec],
            out_specs=pl.BlockSpec((mols, 3, row_block, width), lambda i, y, n: (0, 0, i, 0)),
            scratch_shapes=[pltpu.VMEM((mols, row_block, width), jnp.float32)] * 2,
        ),
        out_shape=jax.ShapeDtypeStruct((mols, 3, length, width), jnp.bfloat16),
        compiler_params=params(40, dimension_semantics=("arbitrary",)),
        cost_estimate=pl.CostEstimate(
            flops=4 * units * length * width,
            bytes_accessed=2 * (2 * units + 3 * mols) * length * width,
            transcendentals=0,
        ),
    )(unit_y, counts, scale, dk, dv)


def final_kernel(slots, half, factor, head_dim, x_ref, n_ref, scale_ref, dq_ref, *refs):
    out_ref, acc = refs[-2:]
    mol = pl.program_id(0)
    low = mol < half
    ahead = jnp.where(low, refs[0][0], refs[1][0]).astype(jnp.float32)
    behind = jnp.where(low, refs[2][0], refs[3][0]).astype(jnp.float32)
    acc[...] = ahead + behind

    def visit(u, carry):
        @pl.when(x_ref[u] == mol)
        def _():
            acc[...] += (scale_ref[pl.ds(u, 1), :] * factor) * dq_ref[u].astype(jnp.float32)

        return carry

    lax.fori_loop(0, n_ref[0], visit, 0)
    for h in range(acc.shape[0] // head_dim):
        part = slice(h * head_dim, (h + 1) * head_dim)
        out_ref[0, 0, :, part] = acc[part].astype(jnp.bfloat16).T


def run_final(slots, half, factor, head_dim, unit_x, counts, scale, dq, arrived, grads):
    _, width, length = dq.shape
    mols = grads.shape[0]
    low = pl.BlockSpec((1, width, length), lambda i, x, n: (jnp.minimum(i, half - 1), 0, 0))
    high = pl.BlockSpec((1, width, length), lambda i, x, n: (jnp.maximum(i - half, 0), 0, 0))
    return pl.pallas_call(
        functools.partial(final_kernel, slots, half, factor, head_dim),
        grid_spec=pltpu.PrefetchScalarGridSpec(
            num_scalar_prefetch=2,
            grid=(mols,),
            in_specs=[
                pl.BlockSpec(scale.shape, lambda i, x, n: (0, 0)),
                pl.BlockSpec((slots, width, length), lambda i, x, n: (0, 0, 0)),
                low,
                high,
                low,
                high,
                pl.BlockSpec(memory_space=pl.ANY),
            ],
            out_specs=pl.BlockSpec((1, 1, length, width), lambda i, x, n: (i, 0, 0, 0)),
            scratch_shapes=[pltpu.VMEM((width, length), jnp.float32)],
        ),
        out_shape=jax.ShapeDtypeStruct(grads.shape, jnp.bfloat16),
        input_output_aliases={8: 0},
        compiler_params=params(24, dimension_semantics=("arbitrary",)),
        cost_estimate=pl.CostEstimate(
            flops=6 * mols * width * length,
            bytes_accessed=2 * (slots + 3 * mols) * width * length,
            transcendentals=0,
        ),
    )(unit_x, counts, scale, dq, *arrived, grads)


def local(mol_qkv, pair_list, head_proj, head_out, labels):
    groups = lax.axis_size("group")
    shards = lax.axis_size("fsdp")
    me = lax.axis_index("group")
    mols_here, length, _, _ = mol_qkv.shape
    heads, head_dim, inner = head_proj.shape
    total_pairs = pair_list.shape[0]
    per_owner = total_pairs // groups
    slots = 2 * (2 * per_owner // groups)
    half = mols_here // 2
    far = groups // 2
    factor = head_dim ** (-0.5)
    ring = ring_of(groups)
    forth = [(ring[i], ring[(i + 1) % groups]) for i in range(groups)]
    back = [(b, a) for a, b in forth]

    mols = jnp.transpose(mol_qkv, (0, 2, 1, 3))
    own = [mols[:half, 0], mols[half:, 0]]
    reach = (far, far - 1)

    lists = make_lists(me.reshape(1).astype(jnp.int32), pair_list, groups, slots, per_owner)
    unit_x, unit_y, unit_p, counts = lists
    turned_kv = turn(mols, heads, head_dim)
    proj = head_proj * jnp.bfloat16(0.5)
    weights = (
        proj,
        jnp.transpose(proj, (0, 2, 1)),
        jnp.broadcast_to(head_out[:, :, None], (heads, inner, length)),
    )
    pairs = jnp.arange(total_pairs, dtype=jnp.int32)
    hot = (unit_p[:, None] == pairs[None, :]).astype(jnp.float32)
    targets = lax.dynamic_update_slice_in_dim(
        jnp.zeros((1, total_pairs), jnp.float32),
        labels.astype(jnp.float32)[None, :],
        me * per_owner,
        1,
    )

    held = run_units(0, slots, lists, own[0], own[1], mols, turned_kv, weights, None)
    up, down = list(own), list(own)
    for d in range(1, far + 1):
        for c in range(2):
            if d <= reach[c]:
                up[c] = lax.ppermute(up[c], "group", forth)
            if d <= reach[1 - c]:
                down[c] = lax.ppermute(down[c], "group", back)
        if d < far:
            steps = [(behind_step(d, groups), up[0], up[1]), (ahead_step(d, groups), down[0], down[1])]
        else:
            steps = [(groups - 1, up[0], down[1])]
        for step, q0, q1 in steps:
            held = run_units(step, slots, lists, q0, q1, mols, turned_kv, weights, held)
    part, dq, dk, dv = held

    logits, scale = run_logits(length, part, hot, targets, groups, shards)

    def hop(step, c, arrived):
        return run_hop(
            step, slots, c * half, half, factor, unit_x, counts, scale, dq, arrived
        )

    streams = {}
    for d in range(far, 0, -1):
        for c in range(2):
            if d <= reach[c]:
                mine = hop(ahead_step(d, groups), c, streams.get(("up", c)))
                streams["up", c] = lax.ppermute(mine, "group", forth)
            if d <= reach[1 - c]:
                mine = hop(behind_step(d, groups), c, streams.get(("down", c)))
                streams["down", c] = lax.ppermute(mine, "group", back)
    grads = run_sums(slots, mols_here, factor, unit_y, counts, scale, dk, dv)
    arrived = [streams["up", 0], streams["up", 1], streams["down", 0], streams["down", 1]]
    grads = run_final(
        slots, half, factor, head_dim, unit_x, counts, scale, dq, arrived, grads
    )
    mol_grad = jnp.transpose(grads, (0, 2, 1, 3))

    rows = logits[0]
    answers = logits[1]
    mean_loss = jnp.sum(jax.nn.softplus(rows) - answers * rows) / total_pairs
    own_logits = lax.dynamic_slice_in_dim(rows, me * per_owner, per_owner)
    return (mol_grad, own_logits, mean_loss)


def solution(mesh):
    placed = (
        P("group", None, None, "fsdp"),
        P(),
        P("fsdp", None, None),
        P("fsdp", None),
        P("group"),
    )
    return jax.shard_map(
        local,
        mesh=mesh,
        in_specs=placed,
        out_specs=(P("group", None, None, "fsdp"), P("group"), P()),
        check_vma=False,
    )
```

```python
import functools

import jax
import jax.numpy as jnp
from jax import lax
from jax.experimental import pallas as pl
from jax.experimental.pallas import tpu as pltpu
from jax.sharding import PartitionSpec as P

MESH = pl.DeviceIdType.MESH
loss_scale = 8192.0
row_block = 16

NN = (((1,), (0,)), ((), ()))
NT = (((1,), (1,)), ((), ()))


def mm(a, b, dims=NN):
    return lax.dot_general(a, b, dims, preferred_element_type=jnp.float32)


def params(mib, **more):
    return pltpu.CompilerParams(vmem_limit_bytes=mib * 1024 * 1024, **more)


def ring_of(groups):
    return list(range(0, groups, 2)) + list(range(groups - 1, 0, -2))


def place_of(group, groups):
    return jnp.where(group % 2 == 0, group // 2, groups - 1 - group // 2)


def ahead_step(d, groups):
    return groups - 1 if 2 * d == groups else 2 * d


def behind_step(d, groups):
    return groups - 1 if 2 * d == groups else 2 * d - 1


def list_kernel(groups, slots, per_owner, me_ref, pairs_ref, x_ref, y_ref, p_ref, n_ref):
    me = me_ref[0]
    my_place = place_of(me, groups)
    total = pairs_ref.shape[0] // 3

    def clear(i, carry):
        x_ref[i] = 0
        y_ref[i] = 0
        p_ref[i] = -1
        return carry

    lax.fori_loop(0, groups * slots, clear, 0)
    for t in range(groups):
        n_ref[t] = 0

    def add(group, x, y, p):
        behind = lax.rem(my_place - place_of(group, groups) + groups, groups)
        step = jnp.where(behind * 2 < groups, 2 * behind - 1, 2 * (groups - behind))
        step = jnp.where(behind == 0, 0, jnp.where(behind * 2 == groups, groups - 1, step))
        at = n_ref[step]
        spot = step * slots + at
        x_ref[spot] = x
        y_ref[spot] = y
        p_ref[spot] = p
        n_ref[step] = at + 1

    def visit(p, carry):
        owner = p // per_owner
        first = pairs_ref[3 * p]
        holder = pairs_ref[3 * p + 1]
        member = pairs_ref[3 * p + 2]

        @pl.when(owner == me)
        def _():
            add(holder, member, first, p)

        @pl.when(holder == me)
        def _():
            add(owner, first, member, p)

        return carry

    lax.fori_loop(0, total, visit, 0)


def make_lists(me, pair_list, groups, slots, per_owner):
    smem = pl.BlockSpec(memory_space=pltpu.SMEM)
    table = jax.ShapeDtypeStruct((groups * slots,), jnp.int32)
    return pl.pallas_call(
        functools.partial(list_kernel, groups, slots, per_owner),
        in_specs=[smem, smem],
        out_specs=[smem] * 4,
        out_shape=[table, table, table, jax.ShapeDtypeStruct((groups,), jnp.int32)],
        cost_estimate=pl.CostEstimate(flops=1000, bytes_accessed=4000, transcendentals=0),
    )(me, pair_list.reshape(-1))


def turn_kernel(head_dim, k_ref, v_ref, kt_ref, vt_ref):
    for h in range(kt_ref.shape[1]):
        cols = slice(h * head_dim, (h + 1) * head_dim)
        kt_ref[0, h] = k_ref[0, 0, :, cols].T
        vt_ref[0, h] = v_ref[0, 0, :, cols].T


def turn(mols, heads, head_dim):
    count, _, length, width = mols.shape
    out = jax.ShapeDtypeStruct((count, heads, head_dim, length), jnp.bfloat16)
    out_spec = pl.BlockSpec((1, heads, head_dim, length), lambda i: (i, 0, 0, 0))
    return pl.pallas_call(
        functools.partial(turn_kernel, head_dim),
        grid=(count,),
        in_specs=[
            pl.BlockSpec((1, 1, length, width), lambda i: (i, 1, 0, 0)),
            pl.BlockSpec((1, 1, length, width), lambda i: (i, 2, 0, 0)),
        ],
        out_specs=[out_spec, out_spec],
        out_shape=[out, out],
        compiler_params=params(16),
        cost_estimate=pl.CostEstimate(
            flops=8 * count * length * width,
            bytes_accessed=8 * count * length * width,
            transcendentals=0,
        ),
    )(mols, mols)


def unit_kernel(head_dim, step, slots, half, *refs):
    x_ref, _, n_ref, q0_ref, q1_ref, k_ref, v_ref, kt_ref, vt_ref = refs[:9]
    proj_ref, turned_ref, out_ref = refs[9:12]
    part_ref, dq_ref, dk_ref, dv_ref = refs[-4:]
    coef = 1.4426950408889634 * head_dim ** (-0.5)
    heads = proj_ref.shape[0]
    length = k_ref.shape[2]
    u = pl.program_id(0)

    @pl.when(u < n_ref[step])
    def _():
        use_low = x_ref[step * slots + u] < half
        total = jnp.zeros((8, length), jnp.float32)
        hs = range(heads)

        def col(h):
            return slice(h * head_dim, (h + 1) * head_dim)

        q = [jnp.where(use_low, q0_ref[0, :, col(h)], q1_ref[0, :, col(h)]) for h in hs]
        s = [mm(k_ref[0, 0, :, col(h)], q[h], NT) for h in hs]
        w = [jnp.exp2((a - jnp.max(a, axis=0, keepdims=True)) * coef) for a in s]
        w = [a * (1.0 / jnp.sum(a, axis=0, keepdims=True)) for a in w]
        wb = [a.astype(jnp.bfloat16) for a in w]
        context = [mm(vt_ref[0, h], wb[h]).astype(jnp.bfloat16) for h in hs]
        dhidden = []
        for h in hs:
            hidden = mm(turned_ref[h], context[h])
            bend = jnp.tanh(hidden)
            first = (1.0 + bend) * out_ref[h]
            silu = hidden * first
            total += jnp.sum(silu.reshape(-1, 8, length), axis=0)
            dhidden.append((first + silu * (1.0 - bend)).astype(jnp.bfloat16))
        dcontext = [mm(proj_ref[h], dhidden[h]).astype(jnp.bfloat16) for h in hs]
        dw = [mm(v_ref[0, 0, :, col(h)], dcontext[h]) for h in hs]
        for h in hs:
            dv_ref[0, :, col(h)] = mm(wb[h], dcontext[h], NT).astype(jnp.bfloat16)
        ds = []
        for h in hs:
            inner = jnp.sum(dw[h] * w[h], axis=0, keepdims=True)
            ds.append((w[h] * (dw[h] - inner)).astype(jnp.bfloat16))
        for h in hs:
            dq_ref[0, h * head_dim : (h + 1) * head_dim] = mm(kt_ref[0, h], ds[h]).astype(
                jnp.bfloat16
            )
            dk_ref[0, :, col(h)] = mm(ds[h], q[h]).astype(jnp.bfloat16)
        part_ref[0] = total


def run_units(step, slots, lists, q0, q1, mols, turned_kv, weights, held):
    unit_x, unit_y, _, counts = lists
    proj, turned, readout = weights
    heads, head_dim, inner = proj.shape
    _, _, length, width = mols.shape
    all_units = unit_x.shape[0]
    base = step * slots
    half = q0.shape[0]

    def at(u, n):
        return base + jnp.maximum(jnp.minimum(u, n[step] - 1), 0)

    def whole(a):
        return pl.BlockSpec(a.shape, lambda u, x, y, n: (0,) * a.ndim)

    def row_map(u, x, y, n):
        return (at(u, n), 0, 0)

    rows = jax.ShapeDtypeStruct((all_units, length, width), jnp.bfloat16)
    row_spec = pl.BlockSpec((1, length, width), row_map)
    kv_t = pl.BlockSpec((1, heads, head_dim, length), lambda u, x, y, n: (y[at(u, n)], 0, 0, 0))
    out_shape = [
        jax.ShapeDtypeStruct((all_units, 8, length), jnp.float32),
        jax.ShapeDtypeStruct((all_units, width, length), jnp.bfloat16),
        rows,
        rows,
    ]
    in_specs = [
        pl.BlockSpec(
            (1, length, width), lambda u, x, y, n: (jnp.minimum(x[at(u, n)], half - 1), 0, 0)
        ),
        pl.BlockSpec(
            (1, length, width), lambda u, x, y, n: (jnp.maximum(x[at(u, n)] - half, 0), 0, 0)
        ),
        pl.BlockSpec((1, 1, length, width), lambda u, x, y, n: (y[at(u, n)], 1, 0, 0)),
        pl.BlockSpec((1, 1, length, width), lambda u, x, y, n: (y[at(u, n)], 2, 0, 0)),
        kv_t,
        kv_t,
        whole(proj),
        whole(turned),
        whole(readout),
    ]
    operands = [q0, q1, mols, mols, *turned_kv, proj, turned, readout]
    aliases = {}
    if held is not None:
        aliases = {3 + len(operands) + i: i for i in range(4)}
        in_specs += [pl.BlockSpec(memory_space=pl.ANY)] * 4
        operands += list(held)
    return pl.pallas_call(
        functools.partial(unit_kernel, head_dim, step, slots, half),
        grid_spec=pltpu.PrefetchScalarGridSpec(
            num_scalar_prefetch=3,
            grid=(slots,),
            in_specs=in_specs,
            out_specs=[
                pl.BlockSpec((1, 8, length), row_map),
                pl.BlockSpec((1, width, length), row_map),
                row_spec,
                row_spec,
            ],
        ),
        out_shape=out_shape,
        input_output_aliases=aliases,
        compiler_params=params(56, dimension_semantics=("arbitrary",)),
        cost_estimate=pl.CostEstimate(
            flops=80 * slots * heads * length * length * head_dim,
            bytes_accessed=6 * slots * length * width,
            transcendentals=slots * heads * length * (length + inner) // 2,
        ),
    )(unit_x, unit_y, counts, *operands)


def logit_kernel(length, groups, shards, part_ref, hot_ref, targets_ref, *refs):
    logits_ref, scale_ref, near, far, near_send, near_recv, far_send, far_recv = refs
    g = lax.axis_index("group")
    f = lax.axis_index("fsdp")
    barrier = pltpu.get_barrier_semaphore()
    for d in range(1, shards):
        other = lax.rem(f + d, shards)
        pl.semaphore_signal(barrier, inc=1, device_id=(g, other), device_id_type=MESH)
    for d in range(1, groups):
        other = lax.rem(g + d, groups)
        pl.semaphore_signal(barrier, inc=1, device_id=(other, f), device_id_type=MESH)

    hot = hot_ref[...]
    mine = jnp.sum(part_ref[...], axis=1)
    used = jnp.max(hot, axis=1, keepdims=True) > 0.0
    mine = jnp.sum(jnp.where(used, mine, 0.0), axis=1, keepdims=True)
    terms = jnp.sum(mine * hot, axis=0, keepdims=True) * (1.0 / length)
    pl.semaphore_wait(barrier, shards - 1 + groups - 1)

    near[f] = jnp.broadcast_to(terms, near.shape[1:])
    copies = []
    for d in range(1, shards):
        other = lax.rem(f + d, shards)
        copy = pltpu.make_async_remote_copy(
            src_ref=near.at[f],
            dst_ref=near.at[f],
            send_sem=near_send.at[d - 1],
            recv_sem=near_recv.at[d - 1],
            device_id=(g, other),
            device_id_type=MESH,
        )
        copy.start()
        copies.append(copy)
    for copy in copies:
        copy.wait()
    summed = near[0]
    for i in range(1, shards):
        summed = summed + near[i]
    row = lax.broadcasted_iota(jnp.int32, summed.shape, 0)
    far[g] = jnp.where(row == 0, summed, jnp.broadcast_to(targets_ref[...], summed.shape))
    copies = []
    for d in range(1, groups):
        other = lax.rem(g + d, groups)
        copy = pltpu.make_async_remote_copy(
            src_ref=far.at[g],
            dst_ref=far.at[g],
            send_sem=far_send.at[d - 1],
            recv_sem=far_recv.at[d - 1],
            device_id=(other, f),
            device_id_type=MESH,
        )
        copy.start()
        copies.append(copy)
    for copy in copies:
        copy.wait()
    both = far[0]
    for i in range(1, groups):
        both = both + far[i]
    logits_ref[...] = both
    logits, targets = both[0:1], both[1:2]
    grad = (jax.nn.sigmoid(logits) - targets) * (loss_scale / length)
    scale_ref[...] = jnp.broadcast_to(
        jnp.sum(hot * grad, axis=1, keepdims=True), scale_ref.shape
    )


def run_logits(length, part, hot, targets, groups, shards):
    units, total = hot.shape
    vmem = pl.BlockSpec(memory_space=pltpu.VMEM)
    return pl.pallas_call(
        functools.partial(logit_kernel, length, groups, shards),
        in_specs=[vmem] * 3,
        out_specs=[vmem] * 2,
        out_shape=[
            jax.ShapeDtypeStruct((8, total), jnp.float32),
            jax.ShapeDtypeStruct((units, length), jnp.float32),
        ],
        scratch_shapes=[
            pltpu.VMEM((shards, 8, total), jnp.float32),
            pltpu.VMEM((groups, 8, total), jnp.float32),
            pltpu.SemaphoreType.DMA((shards - 1,)),
            pltpu.SemaphoreType.DMA((shards - 1,)),
            pltpu.SemaphoreType.DMA((groups - 1,)),
            pltpu.SemaphoreType.DMA((groups - 1,)),
        ],
        compiler_params=params(16, collective_id=0, has_side_effects=True),
        cost_estimate=pl.CostEstimate(
            flops=20000, bytes_accessed=4 * part.size, transcendentals=1000
        ),
    )(part, hot, targets)


def hop_kernel(step, slots, low, factor, x_ref, n_ref, *refs):
    scale_ref, dq_ref = refs[:2]
    out_ref, acc = refs[-2:]
    mol = low + pl.program_id(0)
    if len(refs) == 5:
        acc[...] = refs[2][0].astype(jnp.float32)
    else:
        acc[...] = jnp.zeros_like(acc)

    def visit(u, carry):
        @pl.when(x_ref[step * slots + u] == mol)
        def _():
            g = scale_ref[pl.ds(step * slots + u, 1), :] * factor
            acc[...] += g * dq_ref[u].astype(jnp.float32)

        return carry

    lax.fori_loop(0, n_ref[step], visit, 0)
    out_ref[0] = acc[...].astype(jnp.bfloat16)


def run_hop(step, slots, low, mols, factor, unit_x, counts, scale, dq, arrived):
    _, width, length = dq.shape
    spec = pl.BlockSpec((1, width, length), lambda i, x, n: (i, 0, 0))
    more = [] if arrived is None else [arrived]
    return pl.pallas_call(
        functools.partial(hop_kernel, step, slots, low, factor),
        grid_spec=pltpu.PrefetchScalarGridSpec(
            num_scalar_prefetch=2,
            grid=(mols,),
            in_specs=[
                pl.BlockSpec(scale.shape, lambda i, x, n: (0, 0)),
                pl.BlockSpec((slots, width, length), lambda i, x, n: (step, 0, 0)),
            ]
            + [spec] * len(more),
            out_specs=spec,
            scratch_shapes=[pltpu.VMEM((width, length), jnp.float32)],
        ),
        out_shape=jax.ShapeDtypeStruct((mols, width, length), jnp.bfloat16),
        compiler_params=params(56, dimension_semantics=("arbitrary",)),
        cost_estimate=pl.CostEstimate(
            flops=4 * slots * width * length,
            bytes_accessed=2 * (slots + 2 * mols) * width * length,
            transcendentals=0,
        ),
    )(unit_x, counts, scale, dq, *more)


def sum_kernel(slots, factor, y_ref, n_ref, scale_ref, dk_ref, dv_ref, out_ref, sk, sv):
    sk[...] = jnp.zeros_like(sk)
    sv[...] = jnp.zeros_like(sv)
    repeat = dk_ref.shape[2] // scale_ref.shape[1]

    for t in range(n_ref.shape[0]):

        def visit(i, carry, base=t * slots):
            u = base + i
            y = y_ref[u]
            g = jnp.concatenate([scale_ref[pl.ds(u, 1), :]] * repeat, axis=1)
            sk[y] += (g * factor) * dk_ref[u].astype(jnp.float32)
            sv[y] += g * dv_ref[u].astype(jnp.float32)
            return carry

        lax.fori_loop(0, n_ref[t], visit, 0)
    out_ref[:, 1] = sk[...].astype(jnp.bfloat16)
    out_ref[:, 2] = sv[...].astype(jnp.bfloat16)


def run_sums(slots, mols, factor, unit_y, counts, scale, dk, dv):
    units, length, width = dk.shape
    in_spec = pl.BlockSpec((units, row_block, width), lambda i, y, n: (0, i, 0))
    return pl.pallas_call(
        functools.partial(sum_kernel, slots, factor),
        grid_spec=pltpu.PrefetchScalarGridSpec(
            num_scalar_prefetch=2,
            grid=(length // row_block,),
            in_specs=[pl.BlockSpec(scale.shape, lambda i, y, n: (0, 0)), in_spec, in_spec],
            out_specs=pl.BlockSpec((mols, 3, row_block, width), lambda i, y, n: (0, 0, i, 0)),
            scratch_shapes=[pltpu.VMEM((mols, row_block, width), jnp.float32)] * 2,
        ),
        out_shape=jax.ShapeDtypeStruct((mols, 3, length, width), jnp.bfloat16),
        compiler_params=params(56, dimension_semantics=("arbitrary",)),
        cost_estimate=pl.CostEstimate(
            flops=4 * units * length * width,
            bytes_accessed=2 * (2 * units + 3 * mols) * length * width,
            transcendentals=0,
        ),
    )(unit_y, counts, scale, dk, dv)


def final_kernel(slots, half, factor, head_dim, x_ref, n_ref, scale_ref, dq_ref, *refs):
    out_ref, acc = refs[-2:]
    mol = pl.program_id(0)
    low = mol < half
    ahead = jnp.where(low, refs[0][0], refs[1][0]).astype(jnp.float32)
    behind = jnp.where(low, refs[2][0], refs[3][0]).astype(jnp.float32)
    acc[...] = ahead + behind

    def visit(u, carry):
        @pl.when(x_ref[u] == mol)
        def _():
            acc[...] += (scale_ref[pl.ds(u, 1), :] * factor) * dq_ref[u].astype(jnp.float32)

        return carry

    lax.fori_loop(0, n_ref[0], visit, 0)
    for h in range(acc.shape[0] // head_dim):
        part = slice(h * head_dim, (h + 1) * head_dim)
        out_ref[0, 0, :, part] = acc[part].astype(jnp.bfloat16).T


def run_final(slots, half, factor, head_dim, unit_x, counts, scale, dq, arrived, grads):
    _, width, length = dq.shape
    mols = grads.shape[0]
    low = pl.BlockSpec((1, width, length), lambda i, x, n: (jnp.minimum(i, half - 1), 0, 0))
    high = pl.BlockSpec((1, width, length), lambda i, x, n: (jnp.maximum(i - half, 0), 0, 0))
    return pl.pallas_call(
        functools.partial(final_kernel, slots, half, factor, head_dim),
        grid_spec=pltpu.PrefetchScalarGridSpec(
            num_scalar_prefetch=2,
            grid=(mols,),
            in_specs=[
                pl.BlockSpec(scale.shape, lambda i, x, n: (0, 0)),
                pl.BlockSpec((slots, width, length), lambda i, x, n: (0, 0, 0)),
                low,
                high,
                low,
                high,
                pl.BlockSpec(memory_space=pl.ANY),
            ],
            out_specs=pl.BlockSpec((1, 1, length, width), lambda i, x, n: (i, 0, 0, 0)),
            scratch_shapes=[pltpu.VMEM((width, length), jnp.float32)],
        ),
        out_shape=jax.ShapeDtypeStruct(grads.shape, jnp.bfloat16),
        input_output_aliases={8: 0},
        compiler_params=params(56, dimension_semantics=("arbitrary",)),
        cost_estimate=pl.CostEstimate(
            flops=6 * mols * width * length,
            bytes_accessed=2 * (slots + 3 * mols) * width * length,
            transcendentals=0,
        ),
    )(unit_x, counts, scale, dq, *arrived, grads)


def local(mol_qkv, pair_list, head_proj, head_out, labels):
    groups = lax.axis_size("group")
    shards = lax.axis_size("fsdp")
    me = lax.axis_index("group")
    mols_here, length, _, _ = mol_qkv.shape
    heads, head_dim, inner = head_proj.shape
    total_pairs = pair_list.shape[0]
    per_owner = total_pairs // groups
    slots = 2 * (2 * per_owner // groups)
    half = mols_here // 2
    far = groups // 2
    factor = head_dim ** (-0.5)
    ring = ring_of(groups)
    forth = [(ring[i], ring[(i + 1) % groups]) for i in range(groups)]
    back = [(b, a) for a, b in forth]

    mols = jnp.transpose(mol_qkv, (0, 2, 1, 3))
    own = [mols[:half, 0], mols[half:, 0]]
    reach = (far, far - 1)

    lists = make_lists(me.reshape(1).astype(jnp.int32), pair_list, groups, slots, per_owner)
    unit_x, unit_y, unit_p, counts = lists
    turned_kv = turn(mols, heads, head_dim)
    proj = head_proj * jnp.bfloat16(0.5)
    weights = (
        proj,
        jnp.transpose(proj, (0, 2, 1)),
        jnp.broadcast_to(head_out[:, :, None], (heads, inner, length)),
    )
    pairs = jnp.arange(total_pairs, dtype=jnp.int32)
    hot = (unit_p[:, None] == pairs[None, :]).astype(jnp.float32)
    targets = lax.dynamic_update_slice_in_dim(
        jnp.zeros((1, total_pairs), jnp.float32),
        labels.astype(jnp.float32)[None, :],
        me * per_owner,
        1,
    )

    held = run_units(0, slots, lists, own[0], own[1], mols, turned_kv, weights, None)
    up, down = list(own), list(own)
    for d in range(1, far + 1):
        for c in range(2):
            if d <= reach[c]:
                up[c] = lax.ppermute(up[c], "group", forth)
            if d <= reach[1 - c]:
                down[c] = lax.ppermute(down[c], "group", back)
        if d < far:
            steps = [(behind_step(d, groups), up[0], up[1]), (ahead_step(d, groups), down[0], down[1])]
        else:
            steps = [(groups - 1, up[0], down[1])]
        for step, q0, q1 in steps:
            held = run_units(step, slots, lists, q0, q1, mols, turned_kv, weights, held)
    part, dq, dk, dv = held

    logits, scale = run_logits(length, part, hot, targets, groups, shards)

    def hop(step, c, arrived):
        return run_hop(
            step, slots, c * half, half, factor, unit_x, counts, scale, dq, arrived
        )

    streams = {}
    for d in range(far, 0, -1):
        for c in range(2):
            if d <= reach[c]:
                mine = hop(ahead_step(d, groups), c, streams.get(("up", c)))
                streams["up", c] = lax.ppermute(mine, "group", forth)
            if d <= reach[1 - c]:
                mine = hop(behind_step(d, groups), c, streams.get(("down", c)))
                streams["down", c] = lax.ppermute(mine, "group", back)
    grads = run_sums(slots, mols_here, factor, unit_y, counts, scale, dk, dv)
    arrived = [streams["up", 0], streams["up", 1], streams["down", 0], streams["down", 1]]
    grads = run_final(
        slots, half, factor, head_dim, unit_x, counts, scale, dq, arrived, grads
    )
    mol_grad = jnp.transpose(grads, (0, 2, 1, 3))

    rows = logits[0]
    answers = logits[1]
    mean_loss = jnp.sum(jax.nn.softplus(rows) - answers * rows) / total_pairs
    own_logits = lax.dynamic_slice_in_dim(rows, me * per_owner, per_owner)
    return (mol_grad, own_logits, mean_loss)


def solution(mesh):
    placed = (
        P("group", None, None, "fsdp"),
        P(),
        P("fsdp", None, None),
        P("fsdp", None),
        P("group"),
    )
    return jax.shard_map(
        local,
        mesh=mesh,
        in_specs=placed,
        out_specs=(P("group", None, None, "fsdp"), P("group"), P()),
        check_vma=False,
    )
```

```python
import functools

import jax
import jax.numpy as jnp
from jax import lax
from jax.experimental import pallas as pl
from jax.experimental.pallas import tpu as pltpu
from jax.sharding import PartitionSpec as P

MESH = pl.DeviceIdType.MESH
loss_scale = 8192.0
row_block = 16

NN = (((1,), (0,)), ((), ()))
NT = (((1,), (1,)), ((), ()))


def mm(a, b, dims=NN):
    return lax.dot_general(a, b, dims, preferred_element_type=jnp.float32)


def params(mib, **more):
    return pltpu.CompilerParams(vmem_limit_bytes=mib * 1024 * 1024, **more)


def ring_of(groups):
    return list(range(0, groups, 2)) + list(range(groups - 1, 0, -2))


def place_of(group, groups):
    return jnp.where(group % 2 == 0, group // 2, groups - 1 - group // 2)


def behind_list(d, c, groups):
    if 2 * d == groups:
        return 2 * (groups - 1) + c
    return 2 * (2 * d - 1 + c)


def ahead_list(d, c, groups):
    if 2 * d == groups:
        return 2 * (groups - 1) + c
    return 2 * (2 * d - c) + 1


def list_kernel(groups, half, base, per_owner, me_ref, pairs_ref, x_ref, y_ref, p_ref, s_ref, n_ref):
    me = me_ref[0]
    my_place = place_of(me, groups)
    total = pairs_ref.shape[0] // 3
    lists = 2 * groups

    def clear(i, carry):
        x_ref[i] = 0
        y_ref[i] = 0
        p_ref[i] = -1
        return carry

    lax.fori_loop(0, x_ref.shape[0], clear, 0)

    def list_of(group, x):
        c = (x >= half).astype(jnp.int32)
        behind = lax.rem(my_place - place_of(group, groups) + groups, groups)
        from_behind = 2 * (2 * behind - 1 + c)
        from_ahead = 2 * (2 * (groups - behind) - c) + 1
        at = jnp.where(behind * 2 < groups, from_behind, from_ahead)
        at = jnp.where(behind * 2 == groups, 2 * (groups - 1) + c, at)
        return jnp.where(behind == 0, c, at)

    def walk(visit):
        def body(p, carry):
            owner = p // per_owner
            first = pairs_ref[3 * p]
            holder = pairs_ref[3 * p + 1]
            member = pairs_ref[3 * p + 2]

            @pl.when(owner == me)
            def _():
                visit(list_of(holder, member), member, first, p)

            @pl.when(holder == me)
            def _():
                visit(list_of(owner, first), first, member, p)

            return carry

        lax.fori_loop(0, total, body, 0)

    def count(at, x, y, p):
        n_ref[at] = n_ref[at] + 1

    def fill(at, x, y, p):
        spot = s_ref[at] + n_ref[at]
        x_ref[spot] = jnp.where(x >= half, x - half, x)
        y_ref[spot] = y
        p_ref[spot] = p
        n_ref[at] = n_ref[at] + 1

    for i in range(lists):
        n_ref[i] = 0
    walk(count)
    here = jnp.int32(0)
    for i in range(lists):
        if i == lists - 2:
            here = jnp.int32(base)
        s_ref[i] = here
        here = here + n_ref[i]
        n_ref[i] = 0
    walk(fill)


def make_lists(me, pair_list, groups, half, base, size, per_owner):
    smem = pl.BlockSpec(memory_space=pltpu.SMEM)
    table = jax.ShapeDtypeStruct((size,), jnp.int32)
    short = jax.ShapeDtypeStruct((2 * groups,), jnp.int32)
    return pl.pallas_call(
        functools.partial(list_kernel, groups, half, base, per_owner),
        in_specs=[smem, smem],
        out_specs=[smem] * 5,
        out_shape=[table, table, table, short, short],
        cost_estimate=pl.CostEstimate(flops=1000, bytes_accessed=4000, transcendentals=0),
    )(me, pair_list.reshape(-1))


def turn_kernel(head_dim, k_ref, v_ref, kt_ref, vt_ref):
    for h in range(kt_ref.shape[1]):
        cols = slice(h * head_dim, (h + 1) * head_dim)
        kt_ref[0, h] = k_ref[0, 0, :, cols].T
        vt_ref[0, h] = v_ref[0, 0, :, cols].T


def turn(mols, heads, head_dim):
    count, _, length, width = mols.shape
    out = jax.ShapeDtypeStruct((count, heads, head_dim, length), jnp.bfloat16)
    out_spec = pl.BlockSpec((1, heads, head_dim, length), lambda i: (i, 0, 0, 0))
    return pl.pallas_call(
        functools.partial(turn_kernel, head_dim),
        grid=(count,),
        in_specs=[
            pl.BlockSpec((1, 1, length, width), lambda i: (i, 1, 0, 0)),
            pl.BlockSpec((1, 1, length, width), lambda i: (i, 2, 0, 0)),
        ],
        out_specs=[out_spec, out_spec],
        out_shape=[out, out],
        compiler_params=params(60),
        cost_estimate=pl.CostEstimate(
            flops=8 * count * length * width,
            bytes_accessed=8 * count * length * width,
            transcendentals=0,
        ),
    )(mols, mols)


def unit_body(head_dim, use_low, refs):
    q0_ref, q1_ref, k_ref, v_ref, kt_ref, vt_ref = refs[:6]
    proj_ref, turned_ref, out_ref = refs[6:9]
    part_ref, dq_ref, dk_ref, dv_ref = refs[9:]
    coef = 1.4426950408889634 * head_dim ** (-0.5)
    length = k_ref.shape[2]
    total = jnp.zeros((8, length), jnp.float32)
    hs = range(proj_ref.shape[0])

    def col(h):
        return slice(h * head_dim, (h + 1) * head_dim)

    q = [jnp.where(use_low, q0_ref[0, :, col(h)], q1_ref[0, :, col(h)]) for h in hs]
    s = [mm(k_ref[0, 0, :, col(h)], q[h], NT) for h in hs]
    w = [jnp.exp2((a - jnp.max(a, axis=0, keepdims=True)) * coef) for a in s]
    w = [a * (1.0 / jnp.sum(a, axis=0, keepdims=True)) for a in w]
    wb = [a.astype(jnp.bfloat16) for a in w]
    context = [mm(vt_ref[0, h], wb[h]).astype(jnp.bfloat16) for h in hs]
    dhidden = []
    for h in hs:
        hidden = mm(turned_ref[h], context[h])
        bend = jnp.tanh(hidden)
        first = (1.0 + bend) * out_ref[h]
        silu = hidden * first
        total += jnp.sum(silu.reshape(-1, 8, length), axis=0)
        dhidden.append((first + silu * (1.0 - bend)).astype(jnp.bfloat16))
    dcontext = [mm(proj_ref[h], dhidden[h]).astype(jnp.bfloat16) for h in hs]
    dw = [mm(v_ref[0, 0, :, col(h)], dcontext[h]) for h in hs]
    for h in hs:
        dv_ref[0, :, col(h)] = mm(wb[h], dcontext[h], NT).astype(jnp.bfloat16)
    ds = []
    for h in hs:
        inner = jnp.sum(dw[h] * w[h], axis=0, keepdims=True)
        ds.append((w[h] * (dw[h] - inner)).astype(jnp.bfloat16))
    for h in hs:
        dq_ref[0, col(h)] = mm(kt_ref[0, h], ds[h]).astype(jnp.bfloat16)
        dk_ref[0, :, col(h)] = mm(ds[h], q[h]).astype(jnp.bfloat16)
    part_ref[0] = total


def unit_kernel(head_dim, event, base, x_ref, y_ref, s_ref, n_ref, *refs):
    sources = refs[:5]
    weights = refs[5:8]
    results = refs[-5:-1]
    turns = refs[-1]
    heads = weights[0].shape[0]
    length, width = sources[0].shape[1:]
    low = n_ref[2 * event]
    total = low + n_ref[2 * event + 1]
    start = s_ref[2 * event]

    def low_map(u):
        return (x_ref[start + jnp.maximum(jnp.minimum(u, low - 1), 0)], 0, 0)

    def high_map(u):
        return (x_ref[start + jnp.minimum(jnp.maximum(u, low), total - 1)], 0, 0)

    def kv_map(u):
        return (y_ref[start + u], 0, 0, 0)

    def row_map(u):
        return (start - base + u, 0, 0)

    turns[0] = 0

    def step(*blocks):
        u = turns[0]
        turns[0] = u + 1
        unit_body(head_dim, u < low, (*blocks[:6], *weights, *blocks[6:]))

    kv_spec = pl.BlockSpec((1, heads, head_dim, length), kv_map)
    row_spec = pl.BlockSpec((1, length, width), row_map)

    @pl.when(total > 0)
    def _():
        pltpu.emit_pipeline(
            step,
            grid=(total,),
            in_specs=[
                pl.BlockSpec((1, length, width), low_map),
                pl.BlockSpec((1, length, width), high_map),
                pl.BlockSpec((1, 1, length, width), lambda u: (y_ref[start + u], 1, 0, 0)),
                pl.BlockSpec((1, 1, length, width), lambda u: (y_ref[start + u], 2, 0, 0)),
                kv_spec,
                kv_spec,
            ],
            out_specs=[
                pl.BlockSpec((1, 8, length), row_map),
                pl.BlockSpec((1, width, length), row_map),
                row_spec,
                row_spec,
            ],
        )(sources[0], sources[1], sources[2], sources[2], *sources[3:], *results)


def run_units(event, base, room, lists, q0, q1, mols, turned_kv, weights, held, after):
    unit_x, unit_y, _, starts, counts = lists
    proj, turned, readout = weights
    heads, head_dim, inner = proj.shape
    _, _, length, width = mols.shape
    rows = jax.ShapeDtypeStruct((room, length, width), jnp.bfloat16)
    hbm = pl.BlockSpec(memory_space=pltpu.HBM)
    vmem = pl.BlockSpec(memory_space=pltpu.VMEM)
    operands = [q0, q1, mols, *turned_kv, proj, turned, readout]
    in_specs = [hbm] * 5 + [vmem] * 3
    aliases = {}
    if held is not None:
        aliases = {4 + len(operands) + i: i for i in range(4)}
        in_specs += [hbm] * 4
        operands += list(held)
    in_specs += [hbm] * len(after)
    operands += list(after)
    return pl.pallas_call(
        functools.partial(unit_kernel, head_dim, event, base),
        grid_spec=pltpu.PrefetchScalarGridSpec(
            num_scalar_prefetch=4,
            in_specs=in_specs,
            out_specs=[hbm] * 4,
            scratch_shapes=[pltpu.SMEM((1,), jnp.int32)],
        ),
        out_shape=[
            jax.ShapeDtypeStruct((room, 8, length), jnp.float32),
            jax.ShapeDtypeStruct((room, width, length), jnp.bfloat16),
            rows,
            rows,
        ],
        input_output_aliases=aliases,
        compiler_params=params(60),
        cost_estimate=pl.CostEstimate(
            flops=(640 if held is not None or event == 0 else 4) * heads * length**2 * head_dim,
            bytes_accessed=48 * length * width,
            transcendentals=4 * heads * length * (length + inner),
        ),
    )(unit_x, unit_y, starts, counts, *operands)


def logit_kernel(length, groups, shards, part_ref, hot_ref, targets_ref, *refs):
    logits_ref, scale_ref, near, far, near_send, near_recv, far_send, far_recv = refs
    g = lax.axis_index("group")
    f = lax.axis_index("fsdp")
    barrier = pltpu.get_barrier_semaphore()
    for d in range(1, shards):
        other = lax.rem(f + d, shards)
        pl.semaphore_signal(barrier, inc=1, device_id=(g, other), device_id_type=MESH)
    for d in range(1, groups):
        other = lax.rem(g + d, groups)
        pl.semaphore_signal(barrier, inc=1, device_id=(other, f), device_id_type=MESH)

    hot = hot_ref[...]
    mine = jnp.sum(part_ref[...], axis=1)
    used = jnp.max(hot, axis=1, keepdims=True) > 0.0
    mine = jnp.sum(jnp.where(used, mine, 0.0), axis=1, keepdims=True)
    terms = jnp.sum(mine * hot, axis=0, keepdims=True) * (1.0 / length)
    pl.semaphore_wait(barrier, shards - 1 + groups - 1)

    near[f] = jnp.broadcast_to(terms, near.shape[1:])
    copies = []
    for d in range(1, shards):
        other = lax.rem(f + d, shards)
        copy = pltpu.make_async_remote_copy(
            src_ref=near.at[f],
            dst_ref=near.at[f],
            send_sem=near_send.at[d - 1],
            recv_sem=near_recv.at[d - 1],
            device_id=(g, other),
            device_id_type=MESH,
        )
        copy.start()
        copies.append(copy)
    for copy in copies:
        copy.wait()
    summed = near[0]
    for i in range(1, shards):
        summed = summed + near[i]
    row = lax.broadcasted_iota(jnp.int32, summed.shape, 0)
    far[g] = jnp.where(row == 0, summed, jnp.broadcast_to(targets_ref[...], summed.shape))
    copies = []
    for d in range(1, groups):
        other = lax.rem(g + d, groups)
        copy = pltpu.make_async_remote_copy(
            src_ref=far.at[g],
            dst_ref=far.at[g],
            send_sem=far_send.at[d - 1],
            recv_sem=far_recv.at[d - 1],
            device_id=(other, f),
            device_id_type=MESH,
        )
        copy.start()
        copies.append(copy)
    for copy in copies:
        copy.wait()
    both = far[0]
    for i in range(1, groups):
        both = both + far[i]
    logits_ref[...] = both
    logits, targets = both[0:1], both[1:2]
    grad = (jax.nn.sigmoid(logits) - targets) * (loss_scale / length)
    scale_ref[...] = jnp.broadcast_to(
        jnp.sum(hot * grad, axis=1, keepdims=True), scale_ref.shape
    )


def run_logits(which, length, part, hot, targets, groups, shards):
    units, total = hot.shape
    vmem = pl.BlockSpec(memory_space=pltpu.VMEM)
    return pl.pallas_call(
        functools.partial(logit_kernel, length, groups, shards),
        in_specs=[vmem] * 3,
        out_specs=[vmem] * 2,
        out_shape=[
            jax.ShapeDtypeStruct((8, total), jnp.float32),
            jax.ShapeDtypeStruct((units, length), jnp.float32),
        ],
        scratch_shapes=[
            pltpu.VMEM((shards, 8, total), jnp.float32),
            pltpu.VMEM((groups, 8, total), jnp.float32),
            pltpu.SemaphoreType.DMA((shards - 1,)),
            pltpu.SemaphoreType.DMA((shards - 1,)),
            pltpu.SemaphoreType.DMA((groups - 1,)),
            pltpu.SemaphoreType.DMA((groups - 1,)),
        ],
        compiler_params=params(60, collective_id=which, has_side_effects=True),
        cost_estimate=pl.CostEstimate(
            flops=(1 - which) * 6_000_000_000, bytes_accessed=4 * part.size, transcendentals=1000
        ),
    )(part, hot, targets)


def turn_heads(a, head_dim):
    return jnp.concatenate(
        [a[h : h + head_dim].T for h in range(0, a.shape[0], head_dim)], axis=1
    )


def hop_kernel(which, base, factor, head_dim, has_in, turn, turned_in, x_ref, s_ref, n_ref, *refs):
    scale_ref, dq_ref = refs[:2]
    out_ref, buf, acc, sems = refs[-4:]
    arrived = refs[2] if has_in else None
    count = n_ref[which]
    start = s_ref[which]

    def copy(i):
        return pltpu.make_async_copy(dq_ref.at[start - base + i], buf.at[i], sems.at[i])

    def begin(i, carry):
        copy(i).start()
        return carry

    lax.fori_loop(0, count, begin, 0)
    if arrived is None or turned_in:
        acc[...] = jnp.zeros_like(acc)
    else:
        acc[...] = arrived[...].astype(jnp.float32)

    def visit(i, carry):
        copy(i).wait()
        g = scale_ref[pl.ds(start - base + i, 1), :] * factor
        acc[x_ref[start + i]] += g * buf[i].astype(jnp.float32)
        return carry

    lax.fori_loop(0, count, visit, 0)
    if not turn:
        out_ref[...] = acc[...].astype(jnp.bfloat16)
        return
    for m in range(acc.shape[0]):
        if turned_in:
            for h in range(0, acc.shape[1], head_dim):
                cols = slice(h, h + head_dim)
                mine = acc[m, cols].T + arrived[m, :, cols].astype(jnp.float32)
                out_ref[m, :, cols] = mine.astype(jnp.bfloat16)
        else:
            out_ref[m] = turn_heads(acc[m].astype(jnp.bfloat16), head_dim)


def run_hop(which, base, cap, half, head_dim, lists, scale, dq, arrived, turn, turned_in, after):
    unit_x, _, _, starts, counts = lists
    _, width, length = dq.shape
    vmem = pl.BlockSpec(memory_space=pltpu.VMEM)
    hbm = pl.BlockSpec(memory_space=pltpu.HBM)
    more = [] if arrived is None else [arrived]
    out = (half, length, width) if turn else (half, width, length)
    return pl.pallas_call(
        functools.partial(
            hop_kernel, which, base, head_dim ** (-0.5), head_dim, bool(more), turn, turned_in
        ),
        grid_spec=pltpu.PrefetchScalarGridSpec(
            num_scalar_prefetch=3,
            in_specs=[vmem, hbm] + [vmem] * len(more) + [hbm] * len(after),
            out_specs=vmem,
            scratch_shapes=[
                pltpu.VMEM((cap, width, length), jnp.bfloat16),
                pltpu.VMEM((half, width, length), jnp.float32),
                pltpu.SemaphoreType.DMA((cap,)),
            ],
        ),
        out_shape=jax.ShapeDtypeStruct(out, jnp.bfloat16),
        compiler_params=params(60),
        cost_estimate=pl.CostEstimate(
            flops=4 * cap * width * length,
            bytes_accessed=2 * (cap + 3 * half) * width * length,
            transcendentals=0,
        ),
    )(unit_x, starts, counts, scale, dq, *more, *after)


def sum_kernel(base, factor, y_ref, s_ref, n_ref, *refs):
    scales, dks, dvs = refs[0:2], refs[2:4], refs[4:6]
    out_ref, sk, sv = refs[6:]
    sk[...] = jnp.zeros_like(sk)
    sv[...] = jnp.zeros_like(sv)
    lists = n_ref.shape[0]
    totals = (
        s_ref[lists - 3] + n_ref[lists - 3],
        n_ref[lists - 2] + n_ref[lists - 1],
    )
    for scale_ref, dk_ref, dv_ref, total, at in zip(scales, dks, dvs, totals, (0, base)):
        repeat = dk_ref.shape[2] // scale_ref.shape[1]

        def visit(u, carry):
            y = y_ref[at + u]
            g = jnp.concatenate([scale_ref[pl.ds(u, 1), :]] * repeat, axis=1)
            sk[y] += (g * factor) * dk_ref[u].astype(jnp.float32)
            sv[y] += g * dv_ref[u].astype(jnp.float32)
            return carry

        lax.fori_loop(0, total, visit, 0)
    out_ref[:, 1] = sk[...].astype(jnp.bfloat16)
    out_ref[:, 2] = sv[...].astype(jnp.bfloat16)


def run_sums(base, mols, factor, lists, scales, dks, dvs):
    _, unit_y, _, starts, counts = lists
    _, length, width = dks[0].shape
    units = dks[0].shape[0] + dks[1].shape[0]

    def rows(a):
        return pl.BlockSpec((a.shape[0], row_block, width), lambda i, y, s, n: (0, i, 0))

    def whole(a):
        return pl.BlockSpec(a.shape, lambda i, y, s, n: (0, 0))

    return pl.pallas_call(
        functools.partial(sum_kernel, base, factor),
        grid_spec=pltpu.PrefetchScalarGridSpec(
            num_scalar_prefetch=3,
            grid=(length // row_block,),
            in_specs=[whole(a) for a in scales] + [rows(a) for a in (*dks, *dvs)],
            out_specs=pl.BlockSpec((mols, 3, row_block, width), lambda i, y, s, n: (0, 0, i, 0)),
            scratch_shapes=[pltpu.VMEM((mols, row_block, width), jnp.float32)] * 2,
        ),
        out_shape=jax.ShapeDtypeStruct((mols, 3, length, width), jnp.bfloat16),
        compiler_params=params(60, dimension_semantics=("arbitrary",)),
        cost_estimate=pl.CostEstimate(
            flops=4 * units * length * width,
            bytes_accessed=4 * (2 * units + 3 * mols) * length * width,
            transcendentals=0,
        ),
    )(unit_y, starts, counts, *scales, *dks, *dvs)


def final_kernel(half, low_ref, high_ref, low_last_ref, high_last_ref, _, out_ref):
    low = pl.program_id(0) < half
    before = jnp.where(low, low_ref[0], high_ref[0]).astype(jnp.float32)
    last = jnp.where(low, low_last_ref[0], high_last_ref[0]).astype(jnp.float32)
    out_ref[0, 0] = (before + last).astype(jnp.bfloat16)


def run_final(half, before, last, grads):
    mols, _, length, width = grads.shape
    low = pl.BlockSpec((1, length, width), lambda i: (jnp.minimum(i, half - 1), 0, 0))
    high = pl.BlockSpec((1, length, width), lambda i: (jnp.maximum(i - half, 0), 0, 0))
    return pl.pallas_call(
        functools.partial(final_kernel, half),
        grid=(mols,),
        in_specs=[low, high, low, high, pl.BlockSpec(memory_space=pl.ANY)],
        out_specs=pl.BlockSpec((1, 1, length, width), lambda i: (i, 0, 0, 0)),
        out_shape=jax.ShapeDtypeStruct(grads.shape, jnp.bfloat16),
        input_output_aliases={4: 0},
        compiler_params=params(60, dimension_semantics=("arbitrary",)),
        cost_estimate=pl.CostEstimate(
            flops=mols * width * length, bytes_accessed=6 * mols * width * length, transcendentals=0
        ),
    )(*before, *last, grads)


def local(mol_qkv, pair_list, head_proj, head_out, labels):
    groups = lax.axis_size("group")
    shards = lax.axis_size("fsdp")
    me = lax.axis_index("group")
    mols_here, length, _, _ = mol_qkv.shape
    heads, head_dim, inner = head_proj.shape
    total_pairs = pair_list.shape[0]
    per_owner = total_pairs // groups
    cap_pair = 2 * per_owner // groups
    cap = 2 * cap_pair
    most = per_owner + groups * cap_pair + 1
    base = -(-most // 8) * 8
    extra = -(-(cap + 1) // 8) * 8
    half = mols_here // 2
    far = groups // 2
    factor = head_dim ** (-0.5)
    ring = ring_of(groups)
    forth = [(ring[i], ring[(i + 1) % groups]) for i in range(groups)]
    back = [(b, a) for a, b in forth]

    mols = jnp.transpose(mol_qkv, (0, 2, 1, 3))
    own = [mols[:half, 0], mols[half:, 0]]

    lists = make_lists(
        me.reshape(1).astype(jnp.int32), pair_list, groups, half, base, base + extra, per_owner
    )
    turned_kv = turn(mols, heads, head_dim)
    proj = head_proj * jnp.bfloat16(0.5)
    weights = (
        proj,
        jnp.transpose(proj, (0, 2, 1)),
        jnp.broadcast_to(head_out[:, :, None], (heads, inner, length)),
    )
    pairs = jnp.arange(total_pairs, dtype=jnp.int32)
    hot = (lists[2][:, None] == pairs[None, :]).astype(jnp.float32)
    targets = lax.dynamic_update_slice_in_dim(
        jnp.zeros((1, total_pairs), jnp.float32),
        labels.astype(jnp.float32)[None, :],
        me * per_owner,
        1,
    )

    def units(event, q0, q1, held, after=()):
        at, room = (base, extra) if event == groups - 1 else (0, base)
        return run_units(
            event, at, room, lists, q0, q1, mols, turned_kv, weights, held, after
        )

    held = units(0, own[0], own[1], None)
    up, down = list(own), list(own)
    for event in range(1, groups):
        c = (event + 1) % 2
        up[c] = lax.ppermute(up[c], "group", forth)
        down[1 - c] = lax.ppermute(down[1 - c], "group", back)
        if event < groups - 1:
            held = units(event, up[c], down[1 - c], held)
    part, dq, dk, dv = held
    logits, scale = run_logits(0, length, part, hot[:base], targets, groups, shards)

    def hop(which, scales, terms, arrived, turn=False, turned_in=False, after=()):
        at = base if which >= 2 * (groups - 1) else 0
        return run_hop(
            which, at, cap, half, head_dim, lists, scales, terms, arrived, turn, turned_in, after
        )

    early = [
        hop(ahead_list(far - 1, 1, groups), scale, dq, None, turn=far == 2),
        hop(behind_list(far - 1, 0, groups), scale, dq, None, turn=far == 2),
    ]
    streams = {
        ("up", 1): lax.ppermute(early[0], "group", forth),
        ("down", 0): lax.ppermute(early[1], "group", back),
    }
    last_part, last_dq, last_dk, last_dv = units(groups - 1, up[0], down[1], None, early)
    last_logits, last_scale = run_logits(
        1, length, last_part, hot[base:], targets, groups, shards
    )
    opposite = [
        hop(ahead_list(far, 0, groups), last_scale, last_dq, None, after=(streams["up", 1],)),
        hop(behind_list(far, 1, groups), last_scale, last_dq, None, after=(streams["down", 0],)),
    ]
    streams["up", 0] = lax.ppermute(opposite[0], "group", forth)
    streams["down", 1] = lax.ppermute(opposite[1], "group", back)

    latest = {"up": opposite[0], "down": opposite[1]}

    def send(way, c, d):
        find, perm = (ahead_list, forth) if way == "up" else (behind_list, back)
        mine = hop(
            find(d, c, groups), scale, dq, streams[way, c], turn=d == 1, after=(latest[way],)
        )
        latest[way] = mine
        streams[way, c] = lax.ppermute(mine, "group", perm)

    for d in range(far - 1, 0, -1):
        if d > 1:
            send("up", 1, d - 1)
            send("down", 0, d - 1)
        send("up", 0, d)
        send("down", 1, d)
    grads = run_sums(
        base, mols_here, factor, lists, (scale, last_scale), (dk, last_dk), (dv, last_dv)
    )
    before = [
        hop(0, scale, dq, streams["down", 0], turn=True, turned_in=True),
        hop(1, scale, dq, streams["up", 1], turn=True, turned_in=True),
    ]
    grads = run_final(half, before, [streams["up", 0], streams["down", 1]], grads)
    mol_grad = jnp.transpose(grads, (0, 2, 1, 3))

    rows = logits[0] + last_logits[0]
    answers = logits[1]
    mean_loss = jnp.sum(jax.nn.softplus(rows) - answers * rows) / total_pairs
    own_logits = lax.dynamic_slice_in_dim(rows, me * per_owner, per_owner)
    return (mol_grad, own_logits, mean_loss)


def solution(mesh):
    placed = (
        P("group", None, None, "fsdp"),
        P(),
        P("fsdp", None, None),
        P("fsdp", None),
        P("group"),
    )
    return jax.shard_map(
        local,
        mesh=mesh,
        in_specs=placed,
        out_specs=(P("group", None, None, "fsdp"), P("group"), P()),
        check_vma=False,
    )
```

```python
import functools

import jax
import jax.numpy as jnp
from jax import lax
from jax.experimental import pallas as pl
from jax.experimental.pallas import tpu as pltpu
from jax.sharding import PartitionSpec as P

MESH = pl.DeviceIdType.MESH
loss_scale = 8192.0
row_block = 16

NN = (((1,), (0,)), ((), ()))
NT = (((1,), (1,)), ((), ()))


def mm(a, b, dims=NN):
    return lax.dot_general(a, b, dims, preferred_element_type=jnp.float32)


def params(mib, **more):
    return pltpu.CompilerParams(vmem_limit_bytes=mib * 1024 * 1024, **more)


def ring_of(groups):
    return list(range(0, groups, 2)) + list(range(groups - 1, 0, -2))


def place_of(group, groups):
    return jnp.where(group % 2 == 0, group // 2, groups - 1 - group // 2)


def behind_list(d, c, groups):
    if 2 * d == groups:
        return 2 * (groups - 1) + c
    return 2 * (2 * d - 1 + c)


def ahead_list(d, c, groups):
    if 2 * d == groups:
        return 2 * (groups - 1) + c
    return 2 * (2 * d - c) + 1


def list_kernel(groups, half, base, per_owner, me_ref, pairs_ref, x_ref, y_ref, p_ref, s_ref, n_ref, found):
    me = me_ref[0]
    my_place = place_of(me, groups)
    lists = 2 * groups

    def clear(i, carry):
        x_ref[i] = 0
        y_ref[i] = 0
        p_ref[i] = -1
        return carry

    lax.fori_loop(0, x_ref.shape[0], clear, 0)
    for i in range(lists):
        n_ref[i] = 0

    def note(i, group, x, y, p):
        c = (x >= half).astype(jnp.int32)
        behind = my_place - place_of(group, groups)
        behind = jnp.where(behind < 0, behind + groups, behind)
        from_behind = 2 * (2 * behind - 1 + c)
        from_ahead = 2 * (2 * (groups - behind) - c) + 1
        at = jnp.where(behind * 2 < groups, from_behind, from_ahead)
        at = jnp.where(behind * 2 == groups, 2 * (groups - 1) + c, at)
        at = jnp.where(behind == 0, c, at)
        found[0, i] = at
        found[1, i] = x - half * c
        found[2, i] = y
        found[3, i] = p
        n_ref[at] = n_ref[at] + 1

    def mine(i, carry):
        p = me * per_owner + i
        note(i, pairs_ref[3 * p + 1], pairs_ref[3 * p + 2], pairs_ref[3 * p], p)
        return carry

    lax.fori_loop(0, per_owner, mine, 0)

    def theirs(group, many):
        def visit(i, many):
            p = group * per_owner + i
            here = pairs_ref[3 * p + 1] == me

            @pl.when(here)
            def _():
                note(many, group, pairs_ref[3 * p], pairs_ref[3 * p + 2], p)

            return many + here.astype(jnp.int32)

        return lax.fori_loop(0, per_owner, visit, many)

    many = lax.fori_loop(0, groups, theirs, jnp.int32(per_owner))
    here = jnp.int32(0)
    for i in range(lists):
        if i == lists - 2:
            here = jnp.int32(base)
        s_ref[i] = here
        here = here + n_ref[i]
        n_ref[i] = 0

    def fill(i, carry):
        at = found[0, i]
        spot = s_ref[at] + n_ref[at]
        x_ref[spot] = found[1, i]
        y_ref[spot] = found[2, i]
        p_ref[spot] = found[3, i]
        n_ref[at] = n_ref[at] + 1
        return carry

    lax.fori_loop(0, many, fill, 0)


def make_lists(me, pair_list, groups, half, base, size, per_owner):
    smem = pl.BlockSpec(memory_space=pltpu.SMEM)
    table = jax.ShapeDtypeStruct((size,), jnp.int32)
    short = jax.ShapeDtypeStruct((2 * groups,), jnp.int32)
    return pl.pallas_call(
        functools.partial(list_kernel, groups, half, base, per_owner),
        in_specs=[smem, smem],
        out_specs=[smem] * 5,
        out_shape=[table, table, table, short, short],
        scratch_shapes=[pltpu.SMEM((4, size), jnp.int32)],
        cost_estimate=pl.CostEstimate(flops=1000, bytes_accessed=4000, transcendentals=0),
    )(me, pair_list.reshape(-1))


def turn_kernel(head_dim, k_ref, v_ref, kt_ref, vt_ref):
    for h in range(kt_ref.shape[1]):
        cols = slice(h * head_dim, (h + 1) * head_dim)
        kt_ref[0, h] = k_ref[0, 0, :, cols].T
        vt_ref[0, h] = v_ref[0, 0, :, cols].T


def turn(mols, heads, head_dim):
    count, _, length, width = mols.shape
    out = jax.ShapeDtypeStruct((count, heads, head_dim, length), jnp.bfloat16)
    out_spec = pl.BlockSpec((1, heads, head_dim, length), lambda i: (i, 0, 0, 0))
    return pl.pallas_call(
        functools.partial(turn_kernel, head_dim),
        grid=(count,),
        in_specs=[
            pl.BlockSpec((1, 1, length, width), lambda i: (i, 1, 0, 0)),
            pl.BlockSpec((1, 1, length, width), lambda i: (i, 2, 0, 0)),
        ],
        out_specs=[out_spec, out_spec],
        out_shape=[out, out],
        compiler_params=params(56),
        cost_estimate=pl.CostEstimate(
            flops=8 * count * length * width,
            bytes_accessed=8 * count * length * width,
            transcendentals=0,
        ),
    )(mols, mols)


def unit_body(head_dim, use_low, refs):
    q0_ref, q1_ref, k_ref, v_ref, kt_ref, vt_ref = refs[:6]
    proj_ref, turned_ref, out_ref = refs[6:9]
    part_ref, dq_ref, dk_ref, dv_ref = refs[9:]
    coef = 1.4426950408889634 * head_dim ** (-0.5)
    length = k_ref.shape[2]
    total = jnp.zeros((8, length), jnp.float32)
    hs = range(proj_ref.shape[0])

    def col(h):
        return slice(h * head_dim, (h + 1) * head_dim)

    q = [jnp.where(use_low, q0_ref[0, :, col(h)], q1_ref[0, :, col(h)]) for h in hs]
    s = [mm(k_ref[0, 0, :, col(h)], q[h], NT) for h in hs]
    w = [jnp.exp2((a - jnp.max(a, axis=0, keepdims=True)) * coef) for a in s]
    w = [a * (1.0 / jnp.sum(a, axis=0, keepdims=True)) for a in w]
    wb = [a.astype(jnp.bfloat16) for a in w]
    context = [mm(vt_ref[0, h], wb[h]).astype(jnp.bfloat16) for h in hs]
    dhidden = []
    for h in hs:
        hidden = mm(turned_ref[h], context[h])
        bend = jnp.tanh(hidden)
        first = (1.0 + bend) * out_ref[h]
        silu = hidden * first
        total += jnp.sum(silu.reshape(-1, 8, length), axis=0)
        dhidden.append((first + silu * (1.0 - bend)).astype(jnp.bfloat16))
    dcontext = [mm(proj_ref[h], dhidden[h]).astype(jnp.bfloat16) for h in hs]
    dw = [mm(v_ref[0, 0, :, col(h)], dcontext[h]) for h in hs]
    for h in hs:
        dv_ref[0, :, col(h)] = mm(wb[h], dcontext[h], NT).astype(jnp.bfloat16)
    ds = []
    for h in hs:
        inner = jnp.sum(dw[h] * w[h], axis=0, keepdims=True)
        ds.append((w[h] * (dw[h] - inner)).astype(jnp.bfloat16))
    for h in hs:
        dq_ref[0, col(h)] = mm(kt_ref[0, h], ds[h]).astype(jnp.bfloat16)
        dk_ref[0, :, col(h)] = mm(ds[h], q[h]).astype(jnp.bfloat16)
    part_ref[0] = total


def unit_kernel(head_dim, event, base, x_ref, y_ref, s_ref, n_ref, *refs):
    sources = refs[:5]
    weights = refs[5:8]
    results = refs[-5:-1]
    turns = refs[-1]
    heads = weights[0].shape[0]
    length, width = sources[0].shape[1:]
    low = n_ref[2 * event]
    total = low + n_ref[2 * event + 1]
    start = s_ref[2 * event]

    def low_map(u):
        return (x_ref[start + jnp.maximum(jnp.minimum(u, low - 1), 0)], 0, 0)

    def high_map(u):
        return (x_ref[start + jnp.minimum(jnp.maximum(u, low), total - 1)], 0, 0)

    def kv_map(u):
        return (y_ref[start + u], 0, 0, 0)

    def row_map(u):
        return (start - base + u, 0, 0)

    turns[0] = 0

    def step(*blocks):
        u = turns[0]
        turns[0] = u + 1
        unit_body(head_dim, u < low, (*blocks[:6], *weights, *blocks[6:]))

    kv_spec = pl.BlockSpec((1, heads, head_dim, length), kv_map)
    row_spec = pl.BlockSpec((1, length, width), row_map)

    @pl.when(total > 0)
    def _():
        pltpu.emit_pipeline(
            step,
            grid=(total,),
            in_specs=[
                pl.BlockSpec((1, length, width), low_map),
                pl.BlockSpec((1, length, width), high_map),
                pl.BlockSpec((1, 1, length, width), lambda u: (y_ref[start + u], 1, 0, 0)),
                pl.BlockSpec((1, 1, length, width), lambda u: (y_ref[start + u], 2, 0, 0)),
                kv_spec,
                kv_spec,
            ],
            out_specs=[
                pl.BlockSpec((1, 8, length), row_map),
                pl.BlockSpec((1, width, length), row_map),
                row_spec,
                row_spec,
            ],
        )(sources[0], sources[1], sources[2], sources[2], *sources[3:], *results)


def run_units(event, base, room, lists, q0, q1, mols, turned_kv, weights, held, after):
    unit_x, unit_y, _, starts, counts = lists
    proj, turned, readout = weights
    heads, head_dim, inner = proj.shape
    _, _, length, width = mols.shape
    rows = jax.ShapeDtypeStruct((room, length, width), jnp.bfloat16)
    hbm = pl.BlockSpec(memory_space=pltpu.HBM)
    vmem = pl.BlockSpec(memory_space=pltpu.VMEM)
    operands = [q0, q1, mols, *turned_kv, proj, turned, readout]
    in_specs = [pl.BlockSpec(memory_space=pl.ANY)] * 2 + [hbm] * 3 + [vmem] * 3
    aliases = {}
    if held is not None:
        aliases = {4 + len(operands) + i: i for i in range(4)}
        in_specs += [hbm] * 4
        operands += list(held)
    in_specs += [pl.BlockSpec(memory_space=pl.ANY)] * len(after)
    operands += list(after)
    return pl.pallas_call(
        functools.partial(unit_kernel, head_dim, event, base),
        grid_spec=pltpu.PrefetchScalarGridSpec(
            num_scalar_prefetch=4,
            in_specs=in_specs,
            out_specs=[hbm] * 4,
            scratch_shapes=[pltpu.SMEM((1,), jnp.int32)],
        ),
        out_shape=[
            jax.ShapeDtypeStruct((room, 8, length), jnp.float32),
            jax.ShapeDtypeStruct((room, width, length), jnp.bfloat16),
            rows,
            rows,
        ],
        input_output_aliases=aliases,
        compiler_params=params(56),
        cost_estimate=pl.CostEstimate(
            flops=(640 if held is not None or event == 0 else 4) * heads * length**2 * head_dim,
            bytes_accessed=48 * length * width,
            transcendentals=4 * heads * length * (length + inner),
        ),
    )(unit_x, unit_y, starts, counts, *operands)


def logit_kernel(length, groups, shards, part_ref, hot_ref, targets_ref, *refs):
    logits_ref, scale_ref, rows, send_sem, recv_sem = refs
    me = lax.axis_index("group") * shards + lax.axis_index("fsdp")
    devices = groups * shards
    few = devices <= 32

    def each(visit):
        def body(d, carry):
            other = lax.rem(me + d, devices)
            visit(d - 1, {"group": other // shards, "fsdp": lax.rem(other, shards)})
            return carry

        lax.fori_loop(1, devices, body, 0, unroll=few)

    barrier = pltpu.get_barrier_semaphore()

    def greet(i, device):
        pl.semaphore_signal(barrier, inc=1, device_id=device, device_id_type=MESH)

    each(greet)
    hot = hot_ref[...]
    mine = jnp.sum(part_ref[...], axis=1)
    used = jnp.max(hot, axis=1, keepdims=True) > 0.0
    mine = jnp.sum(jnp.where(used, mine, 0.0), axis=1, keepdims=True)
    terms = jnp.sum(mine * hot, axis=0, keepdims=True) * (1.0 / length)
    row = lax.broadcasted_iota(jnp.int32, rows.shape[1:], 0)
    rows[me] = jnp.where(row == 0, terms, targets_ref[...])

    def copy(i, device):
        return pltpu.make_async_remote_copy(
            src_ref=rows.at[me],
            dst_ref=rows.at[me],
            send_sem=send_sem.at[i],
            recv_sem=recv_sem.at[i],
            device_id=device,
            device_id_type=MESH,
        )

    pl.semaphore_wait(barrier, devices - 1)
    each(lambda i, device: copy(i, device).start())
    each(lambda i, device: copy(i, device).wait())
    both = jnp.sum(rows[...], axis=0)
    logits_ref[...] = both
    logits, targets = both[0:1], both[1:2]
    grad = (jax.nn.sigmoid(logits) - targets) * (loss_scale / length)
    scale_ref[...] = jnp.broadcast_to(
        jnp.sum(hot * grad, axis=1, keepdims=True), scale_ref.shape
    )


def run_logits(which, length, part, hot, targets, groups, shards):
    units, total = hot.shape
    devices = groups * shards
    vmem = pl.BlockSpec(memory_space=pltpu.VMEM)
    return pl.pallas_call(
        functools.partial(logit_kernel, length, groups, shards),
        in_specs=[vmem] * 3,
        out_specs=[vmem] * 2,
        out_shape=[
            jax.ShapeDtypeStruct((8, total), jnp.float32),
            jax.ShapeDtypeStruct((units, length), jnp.float32),
        ],
        scratch_shapes=[
            pltpu.VMEM((devices, 8, total), jnp.float32),
            pltpu.SemaphoreType.DMA((devices - 1,)),
            pltpu.SemaphoreType.DMA((devices - 1,)),
        ],
        compiler_params=params(56, collective_id=which, has_side_effects=True),
        cost_estimate=pl.CostEstimate(
            flops=(1 - which) * 6_000_000_000, bytes_accessed=4 * part.size, transcendentals=1000
        ),
    )(part, hot, targets)


def turn_heads(a, head_dim):
    return jnp.concatenate(
        [a[h : h + head_dim].T for h in range(0, a.shape[0], head_dim)], axis=1
    )


def hop_kernel(which, base, factor, head_dim, has_in, turn, turned_in, x_ref, s_ref, n_ref, *refs):
    scale_ref, dq_ref = refs[:2]
    out_ref, buf, acc, sems = refs[-4:]
    arrived = refs[2] if has_in else None
    count = n_ref[which]
    start = s_ref[which]

    def copy(i):
        return pltpu.make_async_copy(dq_ref.at[start - base + i], buf.at[i], sems.at[i])

    def begin(i, carry):
        copy(i).start()
        return carry

    lax.fori_loop(0, count, begin, 0)
    if arrived is None or turned_in:
        acc[...] = jnp.zeros_like(acc)
    else:
        acc[...] = arrived[...].astype(jnp.float32)

    def visit(i, carry):
        copy(i).wait()
        g = scale_ref[pl.ds(start - base + i, 1), :] * factor
        acc[x_ref[start + i]] += g * buf[i].astype(jnp.float32)
        return carry

    lax.fori_loop(0, count, visit, 0)
    if not turn:
        out_ref[...] = acc[...].astype(jnp.bfloat16)
        return
    for m in range(acc.shape[0]):
        if turned_in:
            for h in range(0, acc.shape[1], head_dim):
                cols = slice(h, h + head_dim)
                mine = acc[m, cols].T + arrived[m, :, cols].astype(jnp.float32)
                out_ref[m, :, cols] = mine.astype(jnp.bfloat16)
        else:
            out_ref[m] = turn_heads(acc[m].astype(jnp.bfloat16), head_dim)


def run_hop(which, base, cap, half, head_dim, lists, scale, dq, arrived, turn, turned_in, after):
    unit_x, _, _, starts, counts = lists
    _, width, length = dq.shape
    vmem = pl.BlockSpec(memory_space=pltpu.VMEM)
    hbm = pl.BlockSpec(memory_space=pltpu.HBM)
    more = [] if arrived is None else [arrived]
    out = (half, length, width) if turn else (half, width, length)
    return pl.pallas_call(
        functools.partial(
            hop_kernel, which, base, head_dim ** (-0.5), head_dim, bool(more), turn, turned_in
        ),
        grid_spec=pltpu.PrefetchScalarGridSpec(
            num_scalar_prefetch=3,
            in_specs=[vmem, hbm] + [vmem] * len(more) + [pl.BlockSpec(memory_space=pl.ANY)] * len(after),
            out_specs=vmem,
            scratch_shapes=[
                pltpu.VMEM((cap, width, length), jnp.bfloat16),
                pltpu.VMEM((half, width, length), jnp.float32),
                pltpu.SemaphoreType.DMA((cap,)),
            ],
        ),
        out_shape=jax.ShapeDtypeStruct(out, jnp.bfloat16),
        compiler_params=params(56),
        cost_estimate=pl.CostEstimate(
            flops=4 * cap * width * length,
            bytes_accessed=2 * (cap + 3 * half) * width * length,
            transcendentals=0,
        ),
    )(unit_x, starts, counts, scale, dq, *more, *after)


def sum_kernel(base, factor, y_ref, s_ref, n_ref, *refs):
    scales, dks, dvs = refs[0:2], refs[2:4], refs[4:6]
    out_ref, sk, sv = refs[6:]
    sk[...] = jnp.zeros_like(sk)
    sv[...] = jnp.zeros_like(sv)
    lists = n_ref.shape[0]
    totals = (
        s_ref[lists - 3] + n_ref[lists - 3],
        n_ref[lists - 2] + n_ref[lists - 1],
    )
    for scale_ref, dk_ref, dv_ref, total, at in zip(scales, dks, dvs, totals, (0, base)):
        repeat = dk_ref.shape[2] // scale_ref.shape[1]

        def visit(u, carry):
            y = y_ref[at + u]
            g = jnp.concatenate([scale_ref[pl.ds(u, 1), :]] * repeat, axis=1)
            sk[y] += (g * factor) * dk_ref[u].astype(jnp.float32)
            sv[y] += g * dv_ref[u].astype(jnp.float32)
            return carry

        lax.fori_loop(0, total, visit, 0)
    out_ref[:, 1] = sk[...].astype(jnp.bfloat16)
    out_ref[:, 2] = sv[...].astype(jnp.bfloat16)


def run_sums(base, mols, factor, lists, scales, dks, dvs):
    _, unit_y, _, starts, counts = lists
    _, length, width = dks[0].shape
    units = dks[0].shape[0] + dks[1].shape[0]

    def rows(a):
        return pl.BlockSpec((a.shape[0], row_block, width), lambda i, y, s, n: (0, i, 0))

    def whole(a):
        return pl.BlockSpec(a.shape, lambda i, y, s, n: (0, 0))

    return pl.pallas_call(
        functools.partial(sum_kernel, base, factor),
        grid_spec=pltpu.PrefetchScalarGridSpec(
            num_scalar_prefetch=3,
            grid=(length // row_block,),
            in_specs=[whole(a) for a in scales] + [rows(a) for a in (*dks, *dvs)],
            out_specs=pl.BlockSpec((mols, 3, row_block, width), lambda i, y, s, n: (0, 0, i, 0)),
            scratch_shapes=[pltpu.VMEM((mols, row_block, width), jnp.float32)] * 2,
        ),
        out_shape=jax.ShapeDtypeStruct((mols, 3, length, width), jnp.bfloat16),
        compiler_params=params(56, dimension_semantics=("arbitrary",)),
        cost_estimate=pl.CostEstimate(
            flops=4 * units * length * width,
            bytes_accessed=4 * (2 * units + 3 * mols) * length * width,
            transcendentals=0,
        ),
    )(unit_y, starts, counts, *scales, *dks, *dvs)


def final_kernel(half, low_ref, high_ref, low_last_ref, high_last_ref, _, out_ref):
    low = pl.program_id(0) * out_ref.shape[0] < half
    before = jnp.where(low, low_ref[...], high_ref[...]).astype(jnp.float32)
    last = jnp.where(low, low_last_ref[...], high_last_ref[...]).astype(jnp.float32)
    out_ref[:, 0] = (before + last).astype(jnp.bfloat16)


def run_final(half, before, last, grads):
    mols, _, length, width = grads.shape
    each = half // 2
    low = pl.BlockSpec((each, length, width), lambda i: (jnp.minimum(i, 1), 0, 0))
    high = pl.BlockSpec((each, length, width), lambda i: (jnp.maximum(i - 2, 0), 0, 0))
    return pl.pallas_call(
        functools.partial(final_kernel, half),
        grid=(mols // each,),
        in_specs=[low, high, low, high, pl.BlockSpec(memory_space=pl.ANY)],
        out_specs=pl.BlockSpec((each, 1, length, width), lambda i: (i, 0, 0, 0)),
        out_shape=jax.ShapeDtypeStruct(grads.shape, jnp.bfloat16),
        input_output_aliases={4: 0},
        compiler_params=params(56, dimension_semantics=("arbitrary",)),
        cost_estimate=pl.CostEstimate(
            flops=mols * width * length, bytes_accessed=6 * mols * width * length, transcendentals=0
        ),
    )(*before, *last, grads)


def local(mol_qkv, pair_list, head_proj, head_out, labels):
    groups = lax.axis_size("group")
    shards = lax.axis_size("fsdp")
    me = lax.axis_index("group")
    mols_here, length, _, _ = mol_qkv.shape
    heads, head_dim, inner = head_proj.shape
    total_pairs = pair_list.shape[0]
    per_owner = total_pairs // groups
    cap_pair = 2 * per_owner // groups
    cap = 2 * cap_pair
    most = per_owner + groups * cap_pair
    base = -(-most // 8) * 8
    extra = -(-cap // 8) * 8
    half = mols_here // 2
    far = groups // 2
    factor = head_dim ** (-0.5)
    ring = ring_of(groups)
    forth = [(ring[i], ring[(i + 1) % groups]) for i in range(groups)]
    back = [(b, a) for a, b in forth]

    mols = jnp.transpose(mol_qkv, (0, 2, 1, 3))
    own = [mols[:half, 0], mols[half:, 0]]

    lists = make_lists(
        me.reshape(1).astype(jnp.int32), pair_list, groups, half, base, base + extra, per_owner
    )
    turned_kv = turn(mols, heads, head_dim)
    proj = head_proj * jnp.bfloat16(0.5)
    weights = (
        proj,
        jnp.transpose(proj, (0, 2, 1)),
        jnp.broadcast_to(head_out[:, :, None], (heads, inner, length)),
    )
    pairs = jnp.arange(total_pairs, dtype=jnp.int32)
    hot = (lists[2][:, None] == pairs[None, :]).astype(jnp.float32)
    targets = lax.dynamic_update_slice_in_dim(
        jnp.zeros((1, total_pairs), jnp.float32),
        labels.astype(jnp.float32)[None, :] * (lax.axis_index("fsdp") == 0),
        me * per_owner,
        1,
    )

    def units(event, q0, q1, held, after=()):
        at, room = (base, extra) if event == groups - 1 else (0, base)
        return run_units(
            event, at, room, lists, q0, q1, mols, turned_kv, weights, held, after
        )

    held = units(0, own[0], own[1], None)
    up, down = list(own), list(own)
    for event in range(1, groups):
        c = (event + 1) % 2
        up[c] = lax.ppermute(up[c], "group", forth)
        down[1 - c] = lax.ppermute(down[1 - c], "group", back)
        if event < groups - 1:
            held = units(event, up[c], down[1 - c], held)
    part, dq, dk, dv = held
    logits, scale = run_logits(0, length, part, hot[:base], targets, groups, shards)

    def hop(which, scales, terms, arrived, turn=False, turned_in=False, after=()):
        at = base if which >= 2 * (groups - 1) else 0
        return run_hop(
            which, at, cap, half, head_dim, lists, scales, terms, arrived, turn, turned_in, after
        )

    early = [
        hop(ahead_list(far - 1, 1, groups), scale, dq, None, turn=far == 2),
        hop(behind_list(far - 1, 0, groups), scale, dq, None, turn=far == 2),
    ]
    streams = {
        ("up", 1): lax.ppermute(early[0], "group", forth),
        ("down", 0): lax.ppermute(early[1], "group", back),
    }
    last_part, last_dq, last_dk, last_dv = units(groups - 1, up[0], down[1], None, early)
    last_logits, last_scale = run_logits(
        1, length, last_part, hot[base:], targets, groups, shards
    )
    opposite = [
        hop(ahead_list(far, 0, groups), last_scale, last_dq, None, after=(streams["up", 1],)),
        hop(behind_list(far, 1, groups), last_scale, last_dq, None, after=(streams["down", 0],)),
    ]
    streams["up", 0] = lax.ppermute(opposite[0], "group", forth)
    streams["down", 1] = lax.ppermute(opposite[1], "group", back)

    latest = {"up": opposite[0], "down": opposite[1]}

    def send(way, c, d):
        find, perm = (ahead_list, forth) if way == "up" else (behind_list, back)
        mine = hop(
            find(d, c, groups), scale, dq, streams[way, c], turn=d == 1, after=(latest[way],)
        )
        latest[way] = mine
        streams[way, c] = lax.ppermute(mine, "group", perm)

    for d in range(far - 1, 0, -1):
        if d > 1:
            send("up", 1, d - 1)
            send("down", 0, d - 1)
        send("up", 0, d)
        send("down", 1, d)
    grads = run_sums(
        base, mols_here, factor, lists, (scale, last_scale), (dk, last_dk), (dv, last_dv)
    )
    before = [
        hop(0, scale, dq, streams["down", 0], turn=True, turned_in=True),
        hop(1, scale, dq, streams["up", 1], turn=True, turned_in=True),
    ]
    grads = run_final(half, before, [streams["up", 0], streams["down", 1]], grads)
    mol_grad = jnp.transpose(grads, (0, 2, 1, 3))

    rows = logits[0] + last_logits[0]
    answers = logits[1]
    mean_loss = jnp.sum(jax.nn.softplus(rows) - answers * rows) / total_pairs
    own_logits = lax.dynamic_slice_in_dim(rows, me * per_owner, per_owner)
    return (mol_grad, own_logits, mean_loss)


def solution(mesh):
    placed = (
        P("group", None, None, "fsdp"),
        P(),
        P("fsdp", None, None),
        P("fsdp", None),
        P("group"),
    )
    return jax.shard_map(
        local,
        mesh=mesh,
        in_specs=placed,
        out_specs=(P("group", None, None, "fsdp"), P("group"), P()),
        check_vma=False,
    )
```

```python
import functools

import jax
import jax.numpy as jnp
from jax import lax
from jax.experimental import pallas as pl
from jax.experimental.pallas import tpu as pltpu
from jax.sharding import PartitionSpec as P

MESH = pl.DeviceIdType.MESH
loss_scale = 8192.0
row_block = 16

NN = (((1,), (0,)), ((), ()))
NT = (((1,), (1,)), ((), ()))


def mm(a, b, dims=NN):
    return lax.dot_general(a, b, dims, preferred_element_type=jnp.float32)


def params(mib, **more):
    return pltpu.CompilerParams(vmem_limit_bytes=mib * 1024 * 1024, **more)


def ring_of(groups):
    return list(range(0, groups, 2)) + list(range(groups - 1, 0, -2))


def place_of(group, groups):
    return jnp.where(group % 2 == 0, group // 2, groups - 1 - group // 2)


def behind_list(d, c, groups):
    if 2 * d == groups:
        return 2 * (groups - 1) + c
    return 2 * (2 * d - 1 + c)


def ahead_list(d, c, groups):
    if 2 * d == groups:
        return 2 * (groups - 1) + c
    return 2 * (2 * d - c) + 1


def list_kernel(groups, half, per_owner, me_ref, pairs_ref, x_ref, y_ref, p_ref, s_ref, n_ref, found):
    me = me_ref[0]
    my_place = place_of(me, groups)
    lists = 2 * groups

    def clear(i, carry):
        x_ref[i] = 0
        y_ref[i] = 0
        p_ref[i] = -1
        return carry

    lax.fori_loop(0, x_ref.shape[0], clear, 0)
    for i in range(lists):
        n_ref[i] = 0

    def note(i, group, x, y, p):
        c = (x >= half).astype(jnp.int32)
        behind = my_place - place_of(group, groups)
        behind = jnp.where(behind < 0, behind + groups, behind)
        from_behind = 2 * (2 * behind - 1 + c)
        from_ahead = 2 * (2 * (groups - behind) - c) + 1
        at = jnp.where(behind * 2 < groups, from_behind, from_ahead)
        at = jnp.where(behind * 2 == groups, 2 * (groups - 1) + c, at)
        at = jnp.where(behind == 0, c, at)
        found[0, i] = at
        found[1, i] = x - half * c
        found[2, i] = y
        found[3, i] = p
        n_ref[at] = n_ref[at] + 1

    def mine(i, carry):
        p = me * per_owner + i
        note(i, pairs_ref[3 * p + 1], pairs_ref[3 * p + 2], pairs_ref[3 * p], p)
        return carry

    lax.fori_loop(0, per_owner, mine, 0)

    def theirs(group, many):
        def visit(i, many):
            p = group * per_owner + i
            here = pairs_ref[3 * p + 1] == me

            @pl.when(here)
            def _():
                note(many, group, pairs_ref[3 * p], pairs_ref[3 * p + 2], p)

            return many + here.astype(jnp.int32)

        return lax.fori_loop(0, per_owner, visit, many)

    many = lax.fori_loop(0, groups, theirs, jnp.int32(per_owner))
    here = jnp.int32(0)
    for i in range(lists):
        s_ref[i] = here
        here = here + n_ref[i]
        n_ref[i] = 0

    def fill(i, carry):
        at = found[0, i]
        spot = s_ref[at] + n_ref[at]
        x_ref[spot] = found[1, i]
        y_ref[spot] = found[2, i]
        p_ref[spot] = found[3, i]
        n_ref[at] = n_ref[at] + 1
        return carry

    lax.fori_loop(0, many, fill, 0)


def make_lists(me, pair_list, groups, half, size, per_owner):
    smem = pl.BlockSpec(memory_space=pltpu.SMEM)
    table = jax.ShapeDtypeStruct((size,), jnp.int32)
    short = jax.ShapeDtypeStruct((2 * groups,), jnp.int32)
    return pl.pallas_call(
        functools.partial(list_kernel, groups, half, per_owner),
        in_specs=[smem, smem],
        out_specs=[smem] * 5,
        out_shape=[table, table, table, short, short],
        scratch_shapes=[pltpu.SMEM((4, size), jnp.int32)],
        cost_estimate=pl.CostEstimate(flops=1000, bytes_accessed=4000, transcendentals=0),
    )(me, pair_list.reshape(-1))


def turn_kernel(head_dim, k_ref, v_ref, kt_ref, vt_ref):
    for h in range(kt_ref.shape[1]):
        cols = slice(h * head_dim, (h + 1) * head_dim)
        kt_ref[0, h] = k_ref[0, 0, :, cols].T
        vt_ref[0, h] = v_ref[0, 0, :, cols].T


def turn(mols, heads, head_dim):
    count, _, length, width = mols.shape
    out = jax.ShapeDtypeStruct((count, heads, head_dim, length), jnp.bfloat16)
    out_spec = pl.BlockSpec((1, heads, head_dim, length), lambda i: (i, 0, 0, 0))
    return pl.pallas_call(
        functools.partial(turn_kernel, head_dim),
        grid=(count,),
        in_specs=[
            pl.BlockSpec((1, 1, length, width), lambda i: (i, 1, 0, 0)),
            pl.BlockSpec((1, 1, length, width), lambda i: (i, 2, 0, 0)),
        ],
        out_specs=[out_spec, out_spec],
        out_shape=[out, out],
        compiler_params=params(56),
        cost_estimate=pl.CostEstimate(
            flops=8 * count * length * width,
            bytes_accessed=8 * count * length * width,
            transcendentals=0,
        ),
    )(mols, mols)


def unit_body(head_dim, use_low, refs):
    q0_ref, q1_ref, k_ref, v_ref, kt_ref, vt_ref = refs[:6]
    proj_ref, turned_ref, out_ref = refs[6:9]
    part_ref, dq_ref, dk_ref, dv_ref = refs[9:]
    coef = 1.4426950408889634 * head_dim ** (-0.5)
    length = k_ref.shape[2]
    total = jnp.zeros((8, length), jnp.float32)
    hs = range(proj_ref.shape[0])

    def col(h):
        return slice(h * head_dim, (h + 1) * head_dim)

    q = [jnp.where(use_low, q0_ref[0, :, col(h)], q1_ref[0, :, col(h)]) for h in hs]
    s = [mm(k_ref[0, 0, :, col(h)], q[h], NT) for h in hs]
    w = [jnp.exp2((a - jnp.max(a, axis=0, keepdims=True)) * coef) for a in s]
    w = [a * (1.0 / jnp.sum(a, axis=0, keepdims=True)) for a in w]
    wb = [a.astype(jnp.bfloat16) for a in w]
    context = [mm(vt_ref[0, h], wb[h]).astype(jnp.bfloat16) for h in hs]
    dhidden = []
    for h in hs:
        hidden = mm(turned_ref[h], context[h])
        bend = jnp.tanh(hidden)
        first = (1.0 + bend) * out_ref[h]
        silu = hidden * first
        total += jnp.sum(silu.reshape(-1, 8, length), axis=0)
        dhidden.append((first + silu * (1.0 - bend)).astype(jnp.bfloat16))
    dcontext = [mm(proj_ref[h], dhidden[h]).astype(jnp.bfloat16) for h in hs]
    dw = [mm(v_ref[0, 0, :, col(h)], dcontext[h]) for h in hs]
    for h in hs:
        dv_ref[0, :, col(h)] = mm(wb[h], dcontext[h], NT).astype(jnp.bfloat16)
    ds = []
    for h in hs:
        inner = jnp.sum(dw[h] * w[h], axis=0, keepdims=True)
        ds.append((w[h] * (dw[h] - inner)).astype(jnp.bfloat16))
    for h in hs:
        dq_ref[0, col(h)] = mm(kt_ref[0, h], ds[h]).astype(jnp.bfloat16)
        dk_ref[0, :, col(h)] = mm(ds[h], q[h]).astype(jnp.bfloat16)
    part_ref[0] = total


def unit_kernel(head_dim, event, x_ref, y_ref, s_ref, n_ref, *refs):
    sources = refs[:5]
    weights = refs[5:8]
    results = refs[-5:-1]
    turns = refs[-1]
    heads = weights[0].shape[0]
    length, width = sources[0].shape[1:]
    low = n_ref[2 * event]
    total = low + n_ref[2 * event + 1]
    start = s_ref[2 * event]

    def low_map(u):
        return (x_ref[start + jnp.maximum(jnp.minimum(u, low - 1), 0)], 0, 0)

    def high_map(u):
        return (x_ref[start + jnp.minimum(jnp.maximum(u, low), total - 1)], 0, 0)

    def kv_map(u):
        return (y_ref[start + u], 0, 0, 0)

    def row_map(u):
        return (start + u, 0, 0)

    turns[0] = 0

    def step(*blocks):
        u = turns[0]
        turns[0] = u + 1
        unit_body(head_dim, u < low, (*blocks[:6], *weights, *blocks[6:]))

    kv_spec = pl.BlockSpec((1, heads, head_dim, length), kv_map)
    row_spec = pl.BlockSpec((1, length, width), row_map)

    @pl.when(total > 0)
    def _():
        pltpu.emit_pipeline(
            step,
            grid=(total,),
            in_specs=[
                pl.BlockSpec((1, length, width), low_map),
                pl.BlockSpec((1, length, width), high_map),
                pl.BlockSpec((1, 1, length, width), lambda u: (y_ref[start + u], 1, 0, 0)),
                pl.BlockSpec((1, 1, length, width), lambda u: (y_ref[start + u], 2, 0, 0)),
                kv_spec,
                kv_spec,
            ],
            out_specs=[
                pl.BlockSpec((1, 8, length), row_map),
                pl.BlockSpec((1, width, length), row_map),
                row_spec,
                row_spec,
            ],
        )(sources[0], sources[1], sources[2], sources[2], *sources[3:], *results)


def run_units(event, room, lists, q0, q1, mols, turned_kv, weights, held):
    unit_x, unit_y, _, starts, counts = lists
    proj, turned, readout = weights
    heads, head_dim, inner = proj.shape
    _, _, length, width = mols.shape
    rows = jax.ShapeDtypeStruct((room, length, width), jnp.bfloat16)
    hbm = pl.BlockSpec(memory_space=pltpu.HBM)
    vmem = pl.BlockSpec(memory_space=pltpu.VMEM)
    operands = [q0, q1, mols, *turned_kv, proj, turned, readout]
    in_specs = [pl.BlockSpec(memory_space=pl.ANY)] * 2 + [hbm] * 3 + [vmem] * 3
    aliases = {}
    if held is not None:
        aliases = {4 + len(operands) + i: i for i in range(4)}
        in_specs += [hbm] * 4
        operands += list(held)
    return pl.pallas_call(
        functools.partial(unit_kernel, head_dim, event),
        grid_spec=pltpu.PrefetchScalarGridSpec(
            num_scalar_prefetch=4,
            in_specs=in_specs,
            out_specs=[hbm] * 4,
            scratch_shapes=[pltpu.SMEM((1,), jnp.int32)],
        ),
        out_shape=[
            jax.ShapeDtypeStruct((room, 8, length), jnp.float32),
            jax.ShapeDtypeStruct((room, width, length), jnp.bfloat16),
            rows,
            rows,
        ],
        input_output_aliases=aliases,
        compiler_params=params(56),
        cost_estimate=pl.CostEstimate(
            flops=640 * heads * length * length * head_dim,
            bytes_accessed=48 * length * width,
            transcendentals=4 * heads * length * (length + inner),
        ),
    )(unit_x, unit_y, starts, counts, *operands)


def logit_kernel(length, groups, shards, part_ref, hot_ref, targets_ref, *refs):
    logits_ref, scale_ref, rows, send_sem, recv_sem = refs
    me = lax.axis_index("group") * shards + lax.axis_index("fsdp")
    devices = groups * shards
    few = devices <= 32

    def each(visit):
        def body(d, carry):
            other = lax.rem(me + d, devices)
            visit(d - 1, {"group": other // shards, "fsdp": lax.rem(other, shards)})
            return carry

        lax.fori_loop(1, devices, body, 0, unroll=few)

    barrier = pltpu.get_barrier_semaphore()

    def greet(i, device):
        pl.semaphore_signal(barrier, inc=1, device_id=device, device_id_type=MESH)

    each(greet)
    hot = hot_ref[...]
    mine = jnp.sum(part_ref[...], axis=1)
    used = jnp.max(hot, axis=1, keepdims=True) > 0.0
    mine = jnp.sum(jnp.where(used, mine, 0.0), axis=1, keepdims=True)
    terms = jnp.sum(mine * hot, axis=0, keepdims=True) * (1.0 / length)
    row = lax.broadcasted_iota(jnp.int32, rows.shape[1:], 0)
    rows[me] = jnp.where(row == 0, terms, targets_ref[...])

    def copy(i, device):
        return pltpu.make_async_remote_copy(
            src_ref=rows.at[me],
            dst_ref=rows.at[me],
            send_sem=send_sem.at[i],
            recv_sem=recv_sem.at[i],
            device_id=device,
            device_id_type=MESH,
        )

    pl.semaphore_wait(barrier, devices - 1)
    each(lambda i, device: copy(i, device).start())
    each(lambda i, device: copy(i, device).wait())
    both = jnp.sum(rows[...], axis=0)
    logits_ref[...] = both
    logits, targets = both[0:1], both[1:2]
    grad = (jax.nn.sigmoid(logits) - targets) * (loss_scale / length)
    scale_ref[...] = jnp.broadcast_to(
        jnp.sum(hot * grad, axis=1, keepdims=True), scale_ref.shape
    )


def run_logits(length, part, hot, targets, groups, shards):
    units, total = hot.shape
    devices = groups * shards
    vmem = pl.BlockSpec(memory_space=pltpu.VMEM)
    return pl.pallas_call(
        functools.partial(logit_kernel, length, groups, shards),
        in_specs=[vmem] * 3,
        out_specs=[vmem] * 2,
        out_shape=[
            jax.ShapeDtypeStruct((2, total), jnp.float32),
            jax.ShapeDtypeStruct((units, length), jnp.float32),
        ],
        scratch_shapes=[
            pltpu.VMEM((devices, 2, total), jnp.float32),
            pltpu.SemaphoreType.DMA((devices - 1,)),
            pltpu.SemaphoreType.DMA((devices - 1,)),
        ],
        compiler_params=params(56, collective_id=0, has_side_effects=True),
        cost_estimate=pl.CostEstimate(
            flops=6_000_000_000, bytes_accessed=4 * part.size, transcendentals=1000
        ),
    )(part, hot, targets)


def turn_heads(a, head_dim):
    return jnp.concatenate(
        [a[h : h + head_dim].T for h in range(0, a.shape[0], head_dim)], axis=1
    )


def hop_kernel(which, factor, head_dim, has_in, turn, turned_in, x_ref, s_ref, n_ref, *refs):
    scale_ref, dq_ref = refs[:2]
    out_ref, buf, acc, sems = refs[-4:]
    arrived = refs[2] if has_in else None
    count = n_ref[which]
    start = s_ref[which]

    def copy(i):
        return pltpu.make_async_copy(dq_ref.at[start + i], buf.at[i], sems.at[i])

    def begin(i, carry):
        copy(i).start()
        return carry

    lax.fori_loop(0, count, begin, 0)
    if arrived is None or turned_in:
        acc[...] = jnp.zeros_like(acc)
    else:
        acc[...] = arrived[...].astype(jnp.float32)

    def visit(i, carry):
        copy(i).wait()
        g = scale_ref[pl.ds(start + i, 1), :] * factor
        acc[x_ref[start + i]] += g * buf[i].astype(jnp.float32)
        return carry

    lax.fori_loop(0, count, visit, 0)
    if not turn:
        out_ref[...] = acc[...].astype(jnp.bfloat16)
        return
    for m in range(acc.shape[0]):
        if turned_in:
            for h in range(0, acc.shape[1], head_dim):
                cols = slice(h, h + head_dim)
                mine = acc[m, cols].T + arrived[m, :, cols].astype(jnp.float32)
                out_ref[m, :, cols] = mine.astype(jnp.bfloat16)
        else:
            out_ref[m] = turn_heads(acc[m].astype(jnp.bfloat16), head_dim)


def run_hop(which, cap, half, head_dim, lists, scale, dq, arrived, turn, turned_in, after):
    unit_x, _, _, starts, counts = lists
    _, width, length = dq.shape
    vmem = pl.BlockSpec(memory_space=pltpu.VMEM)
    hbm = pl.BlockSpec(memory_space=pltpu.HBM)
    more = [] if arrived is None else [arrived]
    out = (half, length, width) if turn else (half, width, length)
    return pl.pallas_call(
        functools.partial(
            hop_kernel, which, head_dim ** (-0.5), head_dim, bool(more), turn, turned_in
        ),
        grid_spec=pltpu.PrefetchScalarGridSpec(
            num_scalar_prefetch=3,
            in_specs=[vmem, hbm] + [vmem] * len(more) + [pl.BlockSpec(memory_space=pl.ANY)] * len(after),
            out_specs=vmem,
            scratch_shapes=[
                pltpu.VMEM((cap, width, length), jnp.bfloat16),
                pltpu.VMEM((half, width, length), jnp.float32),
                pltpu.SemaphoreType.DMA((cap,)),
            ],
        ),
        out_shape=jax.ShapeDtypeStruct(out, jnp.bfloat16),
        compiler_params=params(56),
        cost_estimate=pl.CostEstimate(
            flops=4 * cap * width * length,
            bytes_accessed=2 * (cap + 3 * half) * width * length,
            transcendentals=0,
        ),
    )(unit_x, starts, counts, scale, dq, *more, *after)


def sum_kernel(factor, y_ref, s_ref, n_ref, scale_ref, dk_ref, dv_ref, out_ref, sk, sv):
    sk[...] = jnp.zeros_like(sk)
    sv[...] = jnp.zeros_like(sv)
    last = n_ref.shape[0] - 1
    repeat = dk_ref.shape[2] // scale_ref.shape[1]

    def visit(u, carry):
        y = y_ref[u]
        g = jnp.concatenate([scale_ref[pl.ds(u, 1), :]] * repeat, axis=1)
        sk[y] += (g * factor) * dk_ref[u].astype(jnp.float32)
        sv[y] += g * dv_ref[u].astype(jnp.float32)
        return carry

    lax.fori_loop(0, s_ref[last] + n_ref[last], visit, 0)
    out_ref[:, 1] = sk[...].astype(jnp.bfloat16)
    out_ref[:, 2] = sv[...].astype(jnp.bfloat16)


def run_sums(mols, factor, lists, scale, dk, dv):
    _, unit_y, _, starts, counts = lists
    units, length, width = dk.shape
    rows = pl.BlockSpec((units, row_block, width), lambda i, y, s, n: (0, i, 0))
    return pl.pallas_call(
        functools.partial(sum_kernel, factor),
        grid_spec=pltpu.PrefetchScalarGridSpec(
            num_scalar_prefetch=3,
            grid=(length // row_block,),
            in_specs=[pl.BlockSpec(scale.shape, lambda i, y, s, n: (0, 0)), rows, rows],
            out_specs=pl.BlockSpec((mols, 3, row_block, width), lambda i, y, s, n: (0, 0, i, 0)),
            scratch_shapes=[pltpu.VMEM((mols, row_block, width), jnp.float32)] * 2,
        ),
        out_shape=jax.ShapeDtypeStruct((mols, 3, length, width), jnp.bfloat16),
        compiler_params=params(56, dimension_semantics=("arbitrary",)),
        cost_estimate=pl.CostEstimate(
            flops=4 * units * length * width,
            bytes_accessed=4 * (2 * units + 3 * mols) * length * width,
            transcendentals=0,
        ),
    )(unit_y, starts, counts, scale, dk, dv)


def final_kernel(half, low_ref, high_ref, low_last_ref, high_last_ref, _, out_ref):
    low = pl.program_id(0) * out_ref.shape[0] < half
    before = jnp.where(low, low_ref[...], high_ref[...]).astype(jnp.float32)
    last = jnp.where(low, low_last_ref[...], high_last_ref[...]).astype(jnp.float32)
    out_ref[:, 0] = (before + last).astype(jnp.bfloat16)


def run_final(half, before, last, grads):
    mols, _, length, width = grads.shape
    each = half // 2
    low = pl.BlockSpec((each, length, width), lambda i: (jnp.minimum(i, 1), 0, 0))
    high = pl.BlockSpec((each, length, width), lambda i: (jnp.maximum(i - 2, 0), 0, 0))
    return pl.pallas_call(
        functools.partial(final_kernel, half),
        grid=(mols // each,),
        in_specs=[low, high, low, high, pl.BlockSpec(memory_space=pl.ANY)],
        out_specs=pl.BlockSpec((each, 1, length, width), lambda i: (i, 0, 0, 0)),
        out_shape=jax.ShapeDtypeStruct(grads.shape, jnp.bfloat16),
        input_output_aliases={4: 0},
        compiler_params=params(56, dimension_semantics=("arbitrary",)),
        cost_estimate=pl.CostEstimate(
            flops=mols * width * length, bytes_accessed=6 * mols * width * length, transcendentals=0
        ),
    )(*before, *last, grads)


def local(mol_qkv, pair_list, head_proj, head_out, labels):
    groups = lax.axis_size("group")
    shards = lax.axis_size("fsdp")
    me = lax.axis_index("group")
    mols_here, length, _, _ = mol_qkv.shape
    heads, head_dim, inner = head_proj.shape
    total_pairs = pair_list.shape[0]
    per_owner = total_pairs // groups
    cap_pair = 2 * per_owner // groups
    cap = 2 * cap_pair
    most = per_owner + groups * cap_pair
    room = -(-most // 8) * 8
    half = mols_here // 2
    far = groups // 2
    factor = head_dim ** (-0.5)
    ring = ring_of(groups)
    forth = [(ring[i], ring[(i + 1) % groups]) for i in range(groups)]
    back = [(b, a) for a, b in forth]

    mols = jnp.transpose(mol_qkv, (0, 2, 1, 3))
    own = [mols[:half, 0], mols[half:, 0]]

    lists = make_lists(
        me.reshape(1).astype(jnp.int32), pair_list, groups, half, room, per_owner
    )
    turned_kv = turn(mols, heads, head_dim)
    proj = head_proj * jnp.bfloat16(0.5)
    weights = (
        proj,
        jnp.transpose(proj, (0, 2, 1)),
        jnp.broadcast_to(head_out[:, :, None], (heads, inner, length)),
    )
    pairs = jnp.arange(total_pairs, dtype=jnp.int32)
    hot = (lists[2][:, None] == pairs[None, :]).astype(jnp.float32)
    targets = lax.dynamic_update_slice_in_dim(
        jnp.zeros((1, total_pairs), jnp.float32),
        labels.astype(jnp.float32)[None, :] * (lax.axis_index("fsdp") == 0),
        me * per_owner,
        1,
    )

    def units(event, q0, q1, held):
        return run_units(event, room, lists, q0, q1, mols, turned_kv, weights, held)

    held = units(0, own[0], own[1], None)
    up, down = list(own), list(own)
    for event in range(1, groups):
        c = (event + 1) % 2
        up[c] = lax.ppermute(up[c], "group", forth)
        down[1 - c] = lax.ppermute(down[1 - c], "group", back)
        held = units(event, up[c], down[1 - c], held)
    part, dq, dk, dv = held
    logits, scale = run_logits(length, part, hot, targets, groups, shards)

    def hop(which, arrived, turn=False, turned_in=False, after=()):
        return run_hop(
            which, cap, half, head_dim, lists, scale, dq, arrived, turn, turned_in, after
        )

    streams, latest = {}, {}

    def send(way, c, d):
        find, perm = (ahead_list, forth) if way == "up" else (behind_list, back)
        after = (latest[way],) if way in latest else ()
        mine = hop(find(d, c, groups), streams.get((way, c)), turn=d == 1, after=after)
        latest[way] = mine
        streams[way, c] = lax.ppermute(mine, "group", perm)

    for d in range(far, 0, -1):
        send("up", 0, d)
        send("down", 1, d)
        if d > 1:
            send("up", 1, d - 1)
            send("down", 0, d - 1)
    grads = run_sums(mols_here, factor, lists, scale, dk, dv)
    before = [
        hop(0, streams["down", 0], turn=True, turned_in=True),
        hop(1, streams["up", 1], turn=True, turned_in=True),
    ]
    grads = run_final(half, before, [streams["up", 0], streams["down", 1]], grads)
    mol_grad = jnp.transpose(grads, (0, 2, 1, 3))

    rows = logits[0]
    answers = logits[1]
    mean_loss = jnp.sum(jax.nn.softplus(rows) - answers * rows) / total_pairs
    own_logits = lax.dynamic_slice_in_dim(rows, me * per_owner, per_owner)
    return (mol_grad, own_logits, mean_loss)


def solution(mesh):
    placed = (
        P("group", None, None, "fsdp"),
        P(),
        P("fsdp", None, None),
        P("fsdp", None),
        P("group"),
    )
    return jax.shard_map(
        local,
        mesh=mesh,
        in_specs=placed,
        out_specs=(P("group", None, None, "fsdp"), P("group"), P()),
        check_vma=False,
    )
```

```python
import functools

import jax
import jax.numpy as jnp
from jax import lax
from jax.experimental import pallas as pl
from jax.experimental.pallas import tpu as pltpu
from jax.sharding import PartitionSpec as P

MESH = pl.DeviceIdType.MESH
loss_scale = 8192.0
row_block = 16

NN = (((1,), (0,)), ((), ()))
NT = (((1,), (1,)), ((), ()))


def mm(a, b, dims=NN):
    return lax.dot_general(a, b, dims, preferred_element_type=jnp.float32)


def params(mib, **more):
    return pltpu.CompilerParams(vmem_limit_bytes=mib * 1024 * 1024, **more)


def ring_of(groups):
    return list(range(0, groups, 2)) + list(range(groups - 1, 0, -2))


def place_of(group, groups):
    return jnp.where(group % 2 == 0, group // 2, groups - 1 - group // 2)


def behind_list(d, c, groups):
    if 2 * d == groups:
        return 2 * (groups - 1) + c
    return 2 * (2 * d - 1 + c)


def ahead_list(d, c, groups):
    if 2 * d == groups:
        return 2 * (groups - 1) + c
    return 2 * (2 * d - c) + 1


def list_kernel(groups, half, per_owner, me_ref, pairs_ref, x_ref, y_ref, p_ref, s_ref, n_ref, found):
    me = me_ref[0]
    my_place = place_of(me, groups)
    lists = 2 * groups

    def clear(i, carry):
        x_ref[i] = 0
        y_ref[i] = 0
        p_ref[i] = -1
        return carry

    lax.fori_loop(0, x_ref.shape[0], clear, 0)
    for i in range(lists):
        n_ref[i] = 0

    def note(i, group, x, y, p):
        c = (x >= half).astype(jnp.int32)
        behind = my_place - place_of(group, groups)
        behind = jnp.where(behind < 0, behind + groups, behind)
        from_behind = 2 * (2 * behind - 1 + c)
        from_ahead = 2 * (2 * (groups - behind) - c) + 1
        at = jnp.where(behind * 2 < groups, from_behind, from_ahead)
        at = jnp.where(behind * 2 == groups, 2 * (groups - 1) + c, at)
        at = jnp.where(behind == 0, c, at)
        found[0, i] = at
        found[1, i] = x - half * c
        found[2, i] = y
        found[3, i] = p
        n_ref[at] = n_ref[at] + 1

    def mine(i, carry):
        p = me * per_owner + i
        note(i, pairs_ref[3 * p + 1], pairs_ref[3 * p + 2], pairs_ref[3 * p], p)
        return carry

    lax.fori_loop(0, per_owner, mine, 0)

    def theirs(group, many):
        def visit(i, many):
            p = group * per_owner + i
            here = pairs_ref[3 * p + 1] == me

            @pl.when(here)
            def _():
                note(many, group, pairs_ref[3 * p], pairs_ref[3 * p + 2], p)

            return many + here.astype(jnp.int32)

        return lax.fori_loop(0, per_owner, visit, many)

    many = lax.fori_loop(0, groups, theirs, jnp.int32(per_owner))
    here = jnp.int32(0)
    for i in range(lists):
        s_ref[i] = here
        here = here + n_ref[i]
        n_ref[i] = 0

    def fill(i, carry):
        at = found[0, i]
        spot = s_ref[at] + n_ref[at]
        x_ref[spot] = found[1, i]
        y_ref[spot] = found[2, i]
        p_ref[spot] = found[3, i]
        n_ref[at] = n_ref[at] + 1
        return carry

    lax.fori_loop(0, many, fill, 0)


def make_lists(me, pair_list, groups, half, size, per_owner):
    smem = pl.BlockSpec(memory_space=pltpu.SMEM)
    table = jax.ShapeDtypeStruct((size,), jnp.int32)
    short = jax.ShapeDtypeStruct((2 * groups,), jnp.int32)
    return pl.pallas_call(
        functools.partial(list_kernel, groups, half, per_owner),
        in_specs=[smem, smem],
        out_specs=[smem] * 5,
        out_shape=[table, table, table, short, short],
        scratch_shapes=[pltpu.SMEM((4, size), jnp.int32)],
        cost_estimate=pl.CostEstimate(flops=1000, bytes_accessed=4000, transcendentals=0),
    )(me, pair_list.reshape(-1))


def turn_kernel(head_dim, half, q_ref, k_ref, v_ref, kt_ref, vt_ref, low_ref, high_ref):
    for h in range(kt_ref.shape[1]):
        cols = slice(h * head_dim, (h + 1) * head_dim)
        kt_ref[0, h] = k_ref[0, 0, :, cols].T
        vt_ref[0, h] = v_ref[0, 0, :, cols].T

    @pl.when(pl.program_id(0) < half)
    def _():
        low_ref[...] = q_ref[:, 0]

    @pl.when(pl.program_id(0) >= half)
    def _():
        high_ref[...] = q_ref[:, 0]


def turn(mols, heads, head_dim):
    count, _, length, width = mols.shape
    half = count // 2
    out = jax.ShapeDtypeStruct((count, heads, head_dim, length), jnp.bfloat16)
    part = jax.ShapeDtypeStruct((half, length, width), jnp.bfloat16)
    out_spec = pl.BlockSpec((1, heads, head_dim, length), lambda i: (i, 0, 0, 0))

    def rows(c):
        return pl.BlockSpec((1, 1, length, width), lambda i: (i, c, 0, 0))

    return pl.pallas_call(
        functools.partial(turn_kernel, head_dim, half),
        grid=(count,),
        in_specs=[rows(0), rows(1), rows(2)],
        out_specs=[
            out_spec,
            out_spec,
            pl.BlockSpec((1, length, width), lambda i: (jnp.minimum(i, half - 1), 0, 0)),
            pl.BlockSpec((1, length, width), lambda i: (jnp.maximum(i - half, 0), 0, 0)),
        ],
        out_shape=[out, out, part, part],
        compiler_params=params(63),
        cost_estimate=pl.CostEstimate(
            flops=4_000_000_000,
            bytes_accessed=12 * count * length * width,
            transcendentals=0,
        ),
    )(mols, mols, mols)


def unit_body(head_dim, use_low, refs):
    q0_ref, q1_ref, k_ref, v_ref, kt_ref, vt_ref = refs[:6]
    proj_ref, turned_ref, out_ref = refs[6:9]
    part_ref, dq_ref, dk_ref, dv_ref = refs[9:]
    coef = 1.4426950408889634 * head_dim ** (-0.5)
    length = k_ref.shape[2]
    total = jnp.zeros((8, length), jnp.float32)
    hs = range(proj_ref.shape[0])

    def col(h):
        return slice(h * head_dim, (h + 1) * head_dim)

    q = [jnp.where(use_low, q0_ref[0, :, col(h)], q1_ref[0, :, col(h)]) for h in hs]
    s = [mm(k_ref[0, 0, :, col(h)], q[h], NT) for h in hs]
    w = [jnp.exp2((a - jnp.max(a, axis=0, keepdims=True)) * coef) for a in s]
    w = [a * (1.0 / jnp.sum(a, axis=0, keepdims=True)) for a in w]
    wb = [a.astype(jnp.bfloat16) for a in w]
    context = [mm(vt_ref[0, h], wb[h]).astype(jnp.bfloat16) for h in hs]
    dhidden = []
    for h in hs:
        hidden = mm(turned_ref[h], context[h])
        bend = jnp.tanh(hidden)
        first = (1.0 + bend) * out_ref[h]
        silu = hidden * first
        total += jnp.sum(silu.reshape(-1, 8, length), axis=0)
        dhidden.append((first + silu * (1.0 - bend)).astype(jnp.bfloat16))
    dcontext = [mm(proj_ref[h], dhidden[h]).astype(jnp.bfloat16) for h in hs]
    dw = [mm(v_ref[0, 0, :, col(h)], dcontext[h]) for h in hs]
    for h in hs:
        dv_ref[0, :, col(h)] = mm(wb[h], dcontext[h], NT).astype(jnp.bfloat16)
    ds = []
    for h in hs:
        inner = jnp.sum(dw[h] * w[h], axis=0, keepdims=True)
        ds.append((w[h] * (dw[h] - inner)).astype(jnp.bfloat16))
    for h in hs:
        dq_ref[0, col(h)] = mm(kt_ref[0, h], ds[h]).astype(jnp.bfloat16)
        dk_ref[0, :, col(h)] = mm(ds[h], q[h]).astype(jnp.bfloat16)
    part_ref[0] = total


def unit_kernel(head_dim, event, x_ref, y_ref, s_ref, n_ref, *refs):
    sources = refs[:5]
    weights = refs[5:8]
    results = refs[-5:-1]
    turns = refs[-1]
    heads = weights[0].shape[0]
    length, width = sources[0].shape[1:]
    low = n_ref[2 * event]
    total = low + n_ref[2 * event + 1]
    start = s_ref[2 * event]

    def low_map(u):
        return (x_ref[start + jnp.maximum(jnp.minimum(u, low - 1), 0)], 0, 0)

    def high_map(u):
        return (x_ref[start + jnp.minimum(jnp.maximum(u, low), total - 1)], 0, 0)

    def kv_map(u):
        return (y_ref[start + u], 0, 0, 0)

    def row_map(u):
        return (start + u, 0, 0)

    turns[0] = 0

    def step(*blocks):
        u = turns[0]
        turns[0] = u + 1
        unit_body(head_dim, u < low, (*blocks[:6], *weights, *blocks[6:]))

    kv_spec = pl.BlockSpec((1, heads, head_dim, length), kv_map)
    row_spec = pl.BlockSpec((1, length, width), row_map)

    @pl.when(total > 0)
    def _():
        pltpu.emit_pipeline(
            step,
            grid=(total,),
            in_specs=[
                pl.BlockSpec((1, length, width), low_map),
                pl.BlockSpec((1, length, width), high_map),
                pl.BlockSpec((1, 1, length, width), lambda u: (y_ref[start + u], 1, 0, 0)),
                pl.BlockSpec((1, 1, length, width), lambda u: (y_ref[start + u], 2, 0, 0)),
                kv_spec,
                kv_spec,
            ],
            out_specs=[
                pl.BlockSpec((1, 8, length), row_map),
                pl.BlockSpec((1, width, length), row_map),
                row_spec,
                row_spec,
            ],
        )(sources[0], sources[1], sources[2], sources[2], *sources[3:], *results)


def run_units(event, room, lists, q0, q1, mols, turned_kv, weights, held):
    unit_x, unit_y, _, starts, counts = lists
    proj, turned, readout = weights
    heads, head_dim, inner = proj.shape
    _, _, length, width = mols.shape
    rows = jax.ShapeDtypeStruct((room, length, width), jnp.bfloat16)
    hbm = pl.BlockSpec(memory_space=pltpu.HBM)
    vmem = pl.BlockSpec(memory_space=pltpu.VMEM)
    operands = [q0, q1, mols, *turned_kv, proj, turned, readout]
    in_specs = [pl.BlockSpec(memory_space=pl.ANY)] * 2 + [hbm] * 3 + [vmem] * 3
    aliases = {}
    if held is not None:
        aliases = {4 + len(operands) + i: i for i in range(4)}
        in_specs += [hbm] * 4
        operands += list(held)
    return pl.pallas_call(
        functools.partial(unit_kernel, head_dim, event),
        grid_spec=pltpu.PrefetchScalarGridSpec(
            num_scalar_prefetch=4,
            in_specs=in_specs,
            out_specs=[hbm] * 4,
            scratch_shapes=[pltpu.SMEM((1,), jnp.int32)],
        ),
        out_shape=[
            jax.ShapeDtypeStruct((room, 8, length), jnp.float32),
            jax.ShapeDtypeStruct((room, width, length), jnp.bfloat16),
            rows,
            rows,
        ],
        input_output_aliases=aliases,
        compiler_params=params(63),
        cost_estimate=pl.CostEstimate(
            flops=640 * heads * length * length * head_dim,
            bytes_accessed=48 * length * width,
            transcendentals=4 * heads * length * (length + inner),
        ),
    )(unit_x, unit_y, starts, counts, *operands)


def logit_kernel(length, groups, shards, part_ref, hot_ref, targets_ref, *refs):
    logits_ref, scale_ref, rows, send_sem, recv_sem = refs
    me = lax.axis_index("group") * shards + lax.axis_index("fsdp")
    devices = groups * shards
    few = devices <= 32

    def each(visit):
        def body(d, carry):
            other = lax.rem(me + d, devices)
            visit(d - 1, {"group": other // shards, "fsdp": lax.rem(other, shards)})
            return carry

        lax.fori_loop(1, devices, body, 0, unroll=few)

    barrier = pltpu.get_barrier_semaphore()

    def greet(i, device):
        pl.semaphore_signal(barrier, inc=1, device_id=device, device_id_type=MESH)

    each(greet)
    hot = hot_ref[...]
    mine = jnp.sum(part_ref[...], axis=1)
    used = jnp.max(hot, axis=1, keepdims=True) > 0.0
    mine = jnp.sum(jnp.where(used, mine, 0.0), axis=1, keepdims=True)
    terms = jnp.sum(mine * hot, axis=0, keepdims=True) * (1.0 / length)
    row = lax.broadcasted_iota(jnp.int32, rows.shape[1:], 0)
    rows[me] = jnp.where(row == 0, terms, targets_ref[...])

    def copy(i, device):
        return pltpu.make_async_remote_copy(
            src_ref=rows.at[me],
            dst_ref=rows.at[me],
            send_sem=send_sem.at[i],
            recv_sem=recv_sem.at[i],
            device_id=device,
            device_id_type=MESH,
        )

    pl.semaphore_wait(barrier, devices - 1)
    each(lambda i, device: copy(i, device).start())
    each(lambda i, device: copy(i, device).wait())
    both = jnp.sum(rows[...], axis=0)
    logits_ref[...] = both
    logits, targets = both[0:1], both[1:2]
    grad = (jax.nn.sigmoid(logits) - targets) * (loss_scale / length)
    scale_ref[...] = jnp.broadcast_to(
        jnp.sum(hot * grad, axis=1, keepdims=True), scale_ref.shape
    )


def run_logits(length, part, hot, targets, groups, shards):
    units, total = hot.shape
    devices = groups * shards
    vmem = pl.BlockSpec(memory_space=pltpu.VMEM)
    return pl.pallas_call(
        functools.partial(logit_kernel, length, groups, shards),
        in_specs=[vmem] * 3,
        out_specs=[vmem] * 2,
        out_shape=[
            jax.ShapeDtypeStruct((2, total), jnp.float32),
            jax.ShapeDtypeStruct((units, length), jnp.float32),
        ],
        scratch_shapes=[
            pltpu.VMEM((devices, 2, total), jnp.float32),
            pltpu.SemaphoreType.DMA((devices - 1,)),
            pltpu.SemaphoreType.DMA((devices - 1,)),
        ],
        compiler_params=params(63, collective_id=0, has_side_effects=True),
        cost_estimate=pl.CostEstimate(
            flops=6_000_000_000, bytes_accessed=4 * part.size, transcendentals=1000
        ),
    )(part, hot, targets)


def turn_heads(a, head_dim):
    return jnp.concatenate(
        [a[h : h + head_dim].T for h in range(0, a.shape[0], head_dim)], axis=1
    )


def hop_kernel(which, factor, head_dim, has_in, turn, turned_in, x_ref, s_ref, n_ref, *refs):
    scale_ref, dq_ref = refs[:2]
    arrived_ref = refs[2] if has_in else None
    out_ref, scales, terms, before, result, acc, sems = refs[-7:]
    half, cap = acc.shape[0], terms.shape[0]
    count = n_ref[which]
    start = s_ref[which]

    def copy(i):
        return pltpu.make_async_copy(dq_ref.at[start + i], terms.at[i], sems.at[i])

    def begin(i, carry):
        copy(i).start()
        return carry

    get_scales = pltpu.make_async_copy(scale_ref, scales, sems.at[cap])
    get_scales.start()
    lax.fori_loop(0, count, begin, 0)
    arrivals = []
    for m in range(half if has_in else 0):
        arrivals.append(
            pltpu.make_async_copy(arrived_ref.at[m], before.at[m], sems.at[cap + 1 + m])
        )
        arrivals[m].start()
    acc[...] = jnp.zeros_like(acc)
    get_scales.wait()

    def visit(i, carry):
        copy(i).wait()
        g = scales[pl.ds(start + i, 1), :] * factor
        acc[x_ref[start + i]] += g * terms[i].astype(jnp.float32)
        return carry

    lax.fori_loop(0, count, visit, 0)
    results = []
    for m in range(half):
        if has_in:
            arrivals[m].wait()
        if turned_in:
            for h in range(0, acc.shape[1], head_dim):
                cols = slice(h, h + head_dim)
                mine = acc[m, cols].T + before[m, :, cols].astype(jnp.float32)
                result[m, :, cols] = mine.astype(jnp.bfloat16)
        else:
            mine = acc[m]
            if has_in:
                mine = mine + before[m].astype(jnp.float32)
            mine = mine.astype(jnp.bfloat16)
            result[m] = turn_heads(mine, head_dim) if turn else mine
        results.append(
            pltpu.make_async_copy(result.at[m], out_ref.at[m], sems.at[cap + 1 + half + m])
        )
        results[m].start()
    for put in results:
        put.wait()


def run_hop(which, cap, half, head_dim, lists, scale, dq, arrived, turn, turned_in, after):
    unit_x, _, _, starts, counts = lists
    _, width, length = dq.shape
    hbm = pl.BlockSpec(memory_space=pltpu.HBM)
    anywhere = pl.BlockSpec(memory_space=pl.ANY)
    more = [] if arrived is None else [arrived]
    flat, turned = (half, width, length), (half, length, width)
    out = turned if turn else flat
    return pl.pallas_call(
        functools.partial(
            hop_kernel, which, head_dim ** (-0.5), head_dim, bool(more), turn, turned_in
        ),
        grid_spec=pltpu.PrefetchScalarGridSpec(
            num_scalar_prefetch=3,
            in_specs=[anywhere, hbm] + [anywhere] * (len(more) + len(after)),
            out_specs=anywhere,
            scratch_shapes=[
                pltpu.VMEM(scale.shape, jnp.float32),
                pltpu.VMEM((cap, width, length), jnp.bfloat16),
                pltpu.VMEM(turned if turned_in else flat, jnp.bfloat16),
                pltpu.VMEM(out, jnp.bfloat16),
                pltpu.VMEM(flat, jnp.float32),
                pltpu.SemaphoreType.DMA((cap + 1 + 2 * half,)),
            ],
        ),
        out_shape=jax.ShapeDtypeStruct(out, jnp.bfloat16),
        compiler_params=params(63),
        cost_estimate=pl.CostEstimate(
            flops=4 * cap * width * length,
            bytes_accessed=2 * (cap + 3 * half) * width * length,
            transcendentals=0,
        ),
    )(unit_x, starts, counts, scale, dq, *more, *after)


def sum_kernel(factor, y_ref, s_ref, n_ref, scale_ref, dk_ref, dv_ref, out_ref, sk, sv):
    sk[...] = jnp.zeros_like(sk)
    sv[...] = jnp.zeros_like(sv)
    last = n_ref.shape[0] - 1
    repeat = dk_ref.shape[2] // scale_ref.shape[1]

    def visit(u, carry):
        y = y_ref[u]
        g = jnp.concatenate([scale_ref[pl.ds(u, 1), :]] * repeat, axis=1)
        sk[y] += (g * factor) * dk_ref[u].astype(jnp.float32)
        sv[y] += g * dv_ref[u].astype(jnp.float32)
        return carry

    lax.fori_loop(0, s_ref[last] + n_ref[last], visit, 0)
    out_ref[:, 1] = sk[...].astype(jnp.bfloat16)
    out_ref[:, 2] = sv[...].astype(jnp.bfloat16)


def run_sums(mols, factor, lists, scale, dk, dv):
    _, unit_y, _, starts, counts = lists
    units, length, width = dk.shape
    rows = pl.BlockSpec((units, row_block, width), lambda i, y, s, n: (0, i, 0))
    return pl.pallas_call(
        functools.partial(sum_kernel, factor),
        grid_spec=pltpu.PrefetchScalarGridSpec(
            num_scalar_prefetch=3,
            grid=(length // row_block,),
            in_specs=[pl.BlockSpec(scale.shape, lambda i, y, s, n: (0, 0)), rows, rows],
            out_specs=pl.BlockSpec((mols, 3, row_block, width), lambda i, y, s, n: (0, 0, i, 0)),
            scratch_shapes=[pltpu.VMEM((mols, row_block, width), jnp.float32)] * 2,
        ),
        out_shape=jax.ShapeDtypeStruct((mols, 3, length, width), jnp.bfloat16),
        compiler_params=params(63, dimension_semantics=("arbitrary",)),
        cost_estimate=pl.CostEstimate(
            flops=4 * units * length * width,
            bytes_accessed=4 * (2 * units + 3 * mols) * length * width,
            transcendentals=0,
        ),
    )(unit_y, starts, counts, scale, dk, dv)


def final_kernel(half, low_ref, high_ref, low_last_ref, high_last_ref, _, out_ref):
    low = pl.program_id(0) * out_ref.shape[0] < half
    before = jnp.where(low, low_ref[...], high_ref[...]).astype(jnp.float32)
    last = jnp.where(low, low_last_ref[...], high_last_ref[...]).astype(jnp.float32)
    out_ref[:, 0] = (before + last).astype(jnp.bfloat16)


def run_final(half, before, last, grads):
    mols, _, length, width = grads.shape
    each = half // 2
    low = pl.BlockSpec((each, length, width), lambda i: (jnp.minimum(i, 1), 0, 0))
    high = pl.BlockSpec((each, length, width), lambda i: (jnp.maximum(i - 2, 0), 0, 0))
    return pl.pallas_call(
        functools.partial(final_kernel, half),
        grid=(mols // each,),
        in_specs=[low, high, low, high, pl.BlockSpec(memory_space=pl.ANY)],
        out_specs=pl.BlockSpec((each, 1, length, width), lambda i: (i, 0, 0, 0)),
        out_shape=jax.ShapeDtypeStruct(grads.shape, jnp.bfloat16),
        input_output_aliases={4: 0},
        compiler_params=params(63, dimension_semantics=("arbitrary",)),
        cost_estimate=pl.CostEstimate(
            flops=mols * width * length, bytes_accessed=6 * mols * width * length, transcendentals=0
        ),
    )(*before, *last, grads)


def local(mol_qkv, pair_list, head_proj, head_out, labels):
    groups = lax.axis_size("group")
    shards = lax.axis_size("fsdp")
    me = lax.axis_index("group")
    mols_here, length, _, _ = mol_qkv.shape
    heads, head_dim, inner = head_proj.shape
    total_pairs = pair_list.shape[0]
    per_owner = total_pairs // groups
    cap_pair = 2 * per_owner // groups
    cap = 2 * cap_pair
    most = per_owner + groups * cap_pair
    room = -(-most // 8) * 8
    half = mols_here // 2
    far = groups // 2
    factor = head_dim ** (-0.5)
    ring = ring_of(groups)
    forth = [(ring[i], ring[(i + 1) % groups]) for i in range(groups)]
    back = [(b, a) for a, b in forth]

    mols = jnp.transpose(mol_qkv, (0, 2, 1, 3))
    own = [mols[:half, 0], mols[half:, 0]]

    lists = make_lists(
        me.reshape(1).astype(jnp.int32), pair_list, groups, half, room, per_owner
    )
    *turned_kv, late_low, late_high = turn(mols, heads, head_dim)
    proj = head_proj * jnp.bfloat16(0.5)
    weights = (
        proj,
        jnp.transpose(proj, (0, 2, 1)),
        jnp.broadcast_to(head_out[:, :, None], (heads, inner, length)),
    )
    pairs = jnp.arange(total_pairs, dtype=jnp.int32)
    hot = (lists[2][:, None] == pairs[None, :]).astype(jnp.float32)
    targets = lax.dynamic_update_slice_in_dim(
        jnp.zeros((1, total_pairs), jnp.float32),
        labels.astype(jnp.float32)[None, :] * (lax.axis_index("fsdp") == 0),
        me * per_owner,
        1,
    )

    def units(event, q0, q1, held):
        return run_units(event, room, lists, q0, q1, mols, turned_kv, weights, held)

    held = units(0, own[0], own[1], None)
    up, down = [own[0], late_high], [late_low, own[1]]
    for event in range(1, groups):
        c = (event + 1) % 2
        up[c] = lax.ppermute(up[c], "group", forth)
        down[1 - c] = lax.ppermute(down[1 - c], "group", back)
        held = units(event, up[c], down[1 - c], held)
    part, dq, dk, dv = held
    logits, scale = run_logits(length, part, hot, targets, groups, shards)

    def hop(which, arrived, turn=False, turned_in=False, after=()):
        return run_hop(
            which, cap, half, head_dim, lists, scale, dq, arrived, turn, turned_in, after
        )

    streams, latest = {}, {}

    def send(way, c, d):
        find, perm = (ahead_list, forth) if way == "up" else (behind_list, back)
        after = (latest[way],) if way in latest else ()
        mine = hop(find(d, c, groups), streams.get((way, c)), turn=d == 1, after=after)
        latest[way] = mine
        streams[way, c] = lax.ppermute(mine, "group", perm)

    for d in range(far, 0, -1):
        send("up", 0, d)
        send("down", 1, d)
        if d > 1:
            send("up", 1, d - 1)
            send("down", 0, d - 1)
    grads = run_sums(mols_here, factor, lists, scale, dk, dv)
    before = [
        hop(0, streams["down", 0], turn=True, turned_in=True),
        hop(1, streams["up", 1], turn=True, turned_in=True),
    ]
    grads = run_final(half, before, [streams["up", 0], streams["down", 1]], grads)
    mol_grad = jnp.transpose(grads, (0, 2, 1, 3))

    rows = logits[0]
    answers = logits[1]
    mean_loss = jnp.sum(jax.nn.softplus(rows) - answers * rows) / total_pairs
    own_logits = lax.dynamic_slice_in_dim(rows, me * per_owner, per_owner)
    return (mol_grad, own_logits, mean_loss)


def solution(mesh):
    placed = (
        P("group", None, None, "fsdp"),
        P(),
        P("fsdp", None, None),
        P("fsdp", None),
        P("group"),
    )
    return jax.shard_map(
        local,
        mesh=mesh,
        in_specs=placed,
        out_specs=(P("group", None, None, "fsdp"), P("group"), P()),
        check_vma=False,
    )
```

```python
import functools

import jax
import jax.numpy as jnp
from jax import lax
from jax.experimental import pallas as pl
from jax.experimental.pallas import tpu as pltpu
from jax.sharding import PartitionSpec as P

MESH = pl.DeviceIdType.MESH
loss_scale = 8192.0
row_block = 16

NN = (((1,), (0,)), ((), ()))
NT = (((1,), (1,)), ((), ()))


def mm(a, b, dims=NN):
    return lax.dot_general(a, b, dims, preferred_element_type=jnp.float32)


def params(mib, **more):
    return pltpu.CompilerParams(vmem_limit_bytes=mib * 1024 * 1024, **more)


def ring_of(groups):
    return list(range(0, groups, 2)) + list(range(groups - 1, 0, -2))


def place_of(group, groups):
    return jnp.where(group % 2 == 0, group // 2, groups - 1 - group // 2)


def group_at(place, groups):
    return jnp.where(place < groups // 2, 2 * place, 2 * (groups - 1 - place) + 1)


def behind_list(d, c, groups):
    if 2 * d == groups:
        return 2 * (groups - 1) + c
    return 2 * (2 * d - 1 + c)


def ahead_list(d, c, groups):
    if 2 * d == groups:
        return 2 * (groups - 1) + c
    return 2 * (2 * d - c) + 1


def list_kernel(groups, half, base, extra, per_owner, me_ref, pairs_ref, x_ref, y_ref, p_ref, s_ref, n_ref, found):
    me = me_ref[0]
    my_place = place_of(me, groups)
    lists = 2 * groups

    def clear(i, carry):
        x_ref[i] = 0
        y_ref[i] = 0
        p_ref[i] = -1
        return carry

    lax.fori_loop(0, x_ref.shape[0], clear, 0)
    for i in range(lists):
        n_ref[i] = 0

    def note(i, group, x, y, p):
        c = (x >= half).astype(jnp.int32)
        behind = my_place - place_of(group, groups)
        behind = jnp.where(behind < 0, behind + groups, behind)
        from_behind = 2 * (2 * behind - 1 + c)
        from_ahead = 2 * (2 * (groups - behind) - c) + 1
        at = jnp.where(behind * 2 < groups, from_behind, from_ahead)
        at = jnp.where(behind * 2 == groups, 2 * (groups - 1) + c, at)
        at = jnp.where(behind == 0, c, at)
        found[0, i] = at
        found[1, i] = x - half * c
        found[2, i] = y
        found[3, i] = p
        n_ref[at] = n_ref[at] + 1

    def mine(i, carry):
        p = me * per_owner + i
        note(i, pairs_ref[3 * p + 1], pairs_ref[3 * p + 2], pairs_ref[3 * p], p)
        return carry

    lax.fori_loop(0, per_owner, mine, 0)

    def theirs(group, many):
        def visit(i, many):
            p = group * per_owner + i
            here = pairs_ref[3 * p + 1] == me

            @pl.when(here)
            def _():
                note(many, group, pairs_ref[3 * p], pairs_ref[3 * p + 2], p)

            return many + here.astype(jnp.int32)

        return lax.fori_loop(0, per_owner, visit, many)

    many = lax.fori_loop(0, groups, theirs, jnp.int32(per_owner))
    here = jnp.int32(0)
    for i in range(lists):
        if i == lists - 2:
            here = jnp.int32(base)
        s_ref[i] = here
        here = here + n_ref[i]
        n_ref[i] = 0

    def fill(i, carry):
        at = found[0, i]
        spot = s_ref[at] + n_ref[at]
        x_ref[spot] = found[1, i]
        y_ref[spot] = found[2, i]
        p_ref[spot] = found[3, i]
        n_ref[at] = n_ref[at] + 1
        return carry

    lax.fori_loop(0, many, fill, 0)

    for way in range(2):
        near = group_at(lax.rem(my_place + (groups - 1, 1)[way], groups), groups)
        across = group_at(lax.rem(place_of(near, groups) + groups // 2, groups), groups)
        row = base + extra + way * extra
        got = jnp.int32(0)
        for c in range(2):
            for owner, holder, column in ((near, across, 2), (across, near, 0)):

                def look(i, got, c=c, owner=owner, holder=holder, column=column, row=row):
                    p = owner * per_owner + i
                    x = pairs_ref[3 * p + column]
                    match = (pairs_ref[3 * p + 1] == holder) & ((x >= half) == (c == 1))

                    @pl.when(match)
                    def _():
                        x_ref[row + got] = x - half * c
                        y_ref[row + got] = c
                        p_ref[row + got] = p

                    return got + match.astype(jnp.int32)

                got = lax.fori_loop(0, per_owner, look, got)
        n_ref[lists + way] = got


def make_lists(me, pair_list, groups, half, base, extra, per_owner):
    size = base + 3 * extra
    smem = pl.BlockSpec(memory_space=pltpu.SMEM)
    table = jax.ShapeDtypeStruct((size,), jnp.int32)
    return pl.pallas_call(
        functools.partial(list_kernel, groups, half, base, extra, per_owner),
        in_specs=[smem, smem],
        out_specs=[smem] * 5,
        out_shape=[
            table,
            table,
            table,
            jax.ShapeDtypeStruct((2 * groups,), jnp.int32),
            jax.ShapeDtypeStruct((2 * groups + 2,), jnp.int32),
        ],
        scratch_shapes=[pltpu.SMEM((4, size), jnp.int32)],
        cost_estimate=pl.CostEstimate(flops=1000, bytes_accessed=4000, transcendentals=0),
    )(me, pair_list.reshape(-1))


def turn_kernel(head_dim, half, q_ref, k_ref, v_ref, kt_ref, vt_ref, low_ref, high_ref):
    for h in range(kt_ref.shape[1]):
        cols = slice(h * head_dim, (h + 1) * head_dim)
        kt_ref[0, h] = k_ref[0, 0, :, cols].T
        vt_ref[0, h] = v_ref[0, 0, :, cols].T

    @pl.when(pl.program_id(0) < half)
    def _():
        low_ref[...] = q_ref[:, 0]

    @pl.when(pl.program_id(0) >= half)
    def _():
        high_ref[...] = q_ref[:, 0]


def turn(mols, heads, head_dim):
    count, _, length, width = mols.shape
    half = count // 2
    out = jax.ShapeDtypeStruct((count, heads, head_dim, length), jnp.bfloat16)
    part = jax.ShapeDtypeStruct((half, length, width), jnp.bfloat16)
    out_spec = pl.BlockSpec((1, heads, head_dim, length), lambda i: (i, 0, 0, 0))

    def rows(c):
        return pl.BlockSpec((1, 1, length, width), lambda i: (i, c, 0, 0))

    return pl.pallas_call(
        functools.partial(turn_kernel, head_dim, half),
        grid=(count,),
        in_specs=[rows(0), rows(1), rows(2)],
        out_specs=[
            out_spec,
            out_spec,
            pl.BlockSpec((1, length, width), lambda i: (jnp.minimum(i, half - 1), 0, 0)),
            pl.BlockSpec((1, length, width), lambda i: (jnp.maximum(i - half, 0), 0, 0)),
        ],
        out_shape=[out, out, part, part],
        compiler_params=params(63),
        cost_estimate=pl.CostEstimate(
            flops=4_000_000_000,
            bytes_accessed=12 * count * length * width,
            transcendentals=0,
        ),
    )(mols, mols, mols)


def unit_body(head_dim, use_low, refs):
    q0_ref, q1_ref, k_ref, v_ref, kt_ref, vt_ref = refs[:6]
    proj_ref, turned_ref, out_ref = refs[6:9]
    part_ref, dq_ref, dk_ref, dv_ref = refs[9:]
    coef = 1.4426950408889634 * head_dim ** (-0.5)
    length = k_ref.shape[2]
    total = jnp.zeros((8, length), jnp.float32)
    hs = range(proj_ref.shape[0])

    def col(h):
        return slice(h * head_dim, (h + 1) * head_dim)

    q = [jnp.where(use_low, q0_ref[0, :, col(h)], q1_ref[0, :, col(h)]) for h in hs]
    s = [mm(k_ref[0, 0, :, col(h)], q[h], NT) for h in hs]
    w = [jnp.exp2((a - jnp.max(a, axis=0, keepdims=True)) * coef) for a in s]
    w = [a * (1.0 / jnp.sum(a, axis=0, keepdims=True)) for a in w]
    wb = [a.astype(jnp.bfloat16) for a in w]
    context = [mm(vt_ref[0, h], wb[h]).astype(jnp.bfloat16) for h in hs]
    dhidden = []
    for h in hs:
        hidden = mm(turned_ref[h], context[h])
        bend = jnp.tanh(hidden)
        first = (1.0 + bend) * out_ref[h]
        silu = hidden * first
        total += jnp.sum(silu.reshape(-1, 8, length), axis=0)
        dhidden.append((first + silu * (1.0 - bend)).astype(jnp.bfloat16))
    dcontext = [mm(proj_ref[h], dhidden[h]).astype(jnp.bfloat16) for h in hs]
    dw = [mm(v_ref[0, 0, :, col(h)], dcontext[h]) for h in hs]
    for h in hs:
        dv_ref[0, :, col(h)] = mm(wb[h], dcontext[h], NT).astype(jnp.bfloat16)
    ds = []
    for h in hs:
        inner = jnp.sum(dw[h] * w[h], axis=0, keepdims=True)
        ds.append((w[h] * (dw[h] - inner)).astype(jnp.bfloat16))
    for h in hs:
        dq_ref[0, col(h)] = mm(kt_ref[0, h], ds[h]).astype(jnp.bfloat16)
        dk_ref[0, :, col(h)] = mm(ds[h], q[h]).astype(jnp.bfloat16)
    part_ref[0] = total


def unit_kernel(head_dim, event, base, x_ref, y_ref, s_ref, n_ref, *refs):
    sources = refs[:5]
    weights = refs[5:8]
    results = refs[-5:-1]
    turns = refs[-1]
    heads = weights[0].shape[0]
    length, width = sources[0].shape[1:]
    low = n_ref[2 * event]
    total = low + n_ref[2 * event + 1]
    start = s_ref[2 * event]

    def low_map(u):
        return (x_ref[start + jnp.maximum(jnp.minimum(u, low - 1), 0)], 0, 0)

    def high_map(u):
        return (x_ref[start + jnp.minimum(jnp.maximum(u, low), total - 1)], 0, 0)

    def kv_map(u):
        return (y_ref[start + u], 0, 0, 0)

    def row_map(u):
        return (start - base + u, 0, 0)

    turns[0] = 0

    def step(*blocks):
        u = turns[0]
        turns[0] = u + 1
        unit_body(head_dim, u < low, (*blocks[:6], *weights, *blocks[6:]))

    kv_spec = pl.BlockSpec((1, heads, head_dim, length), kv_map)
    row_spec = pl.BlockSpec((1, length, width), row_map)

    @pl.when(total > 0)
    def _():
        pltpu.emit_pipeline(
            step,
            grid=(total,),
            in_specs=[
                pl.BlockSpec((1, length, width), low_map),
                pl.BlockSpec((1, length, width), high_map),
                pl.BlockSpec((1, 1, length, width), lambda u: (y_ref[start + u], 1, 0, 0)),
                pl.BlockSpec((1, 1, length, width), lambda u: (y_ref[start + u], 2, 0, 0)),
                kv_spec,
                kv_spec,
            ],
            out_specs=[
                pl.BlockSpec((1, 8, length), row_map),
                pl.BlockSpec((1, width, length), row_map),
                row_spec,
                row_spec,
            ],
        )(sources[0], sources[1], sources[2], sources[2], *sources[3:], *results)


def run_units(event, base, room, lists, q0, q1, mols, turned_kv, weights, held, after):
    unit_x, unit_y, _, starts, counts = lists
    proj, turned, readout = weights
    heads, head_dim, inner = proj.shape
    _, _, length, width = mols.shape
    rows = jax.ShapeDtypeStruct((room, length, width), jnp.bfloat16)
    hbm = pl.BlockSpec(memory_space=pltpu.HBM)
    vmem = pl.BlockSpec(memory_space=pltpu.VMEM)
    operands = [q0, q1, mols, *turned_kv, proj, turned, readout]
    in_specs = [pl.BlockSpec(memory_space=pl.ANY)] * 2 + [hbm] * 3 + [vmem] * 3
    aliases = {}
    if held is not None:
        aliases = {4 + len(operands) + i: i for i in range(4)}
        in_specs += [hbm] * 4
        operands += list(held)
    in_specs += [pl.BlockSpec(memory_space=pl.ANY)] * len(after)
    operands += list(after)
    return pl.pallas_call(
        functools.partial(unit_kernel, head_dim, event, base),
        grid_spec=pltpu.PrefetchScalarGridSpec(
            num_scalar_prefetch=4,
            in_specs=in_specs,
            out_specs=[hbm] * 4,
            scratch_shapes=[pltpu.SMEM((1,), jnp.int32)],
        ),
        out_shape=[
            jax.ShapeDtypeStruct((room, 8, length), jnp.float32),
            jax.ShapeDtypeStruct((room, width, length), jnp.bfloat16),
            rows,
            rows,
        ],
        input_output_aliases=aliases,
        compiler_params=params(63),
        cost_estimate=pl.CostEstimate(
            flops=640 * heads * length * length * head_dim,
            bytes_accessed=48 * length * width,
            transcendentals=4 * heads * length * (length + inner),
        ),
    )(unit_x, unit_y, starts, counts, *operands)


def logit_kernel(length, groups, shards, part_ref, last_ref, hot_ref, targets_ref, *refs):
    logits_ref, scale_ref, rows, send_sem, recv_sem = refs
    me = lax.axis_index("group") * shards + lax.axis_index("fsdp")
    devices = groups * shards
    few = devices <= 32

    def each(visit):
        def body(d, carry):
            other = lax.rem(me + d, devices)
            visit(d - 1, {"group": other // shards, "fsdp": lax.rem(other, shards)})
            return carry

        lax.fori_loop(1, devices, body, 0, unroll=few)

    barrier = pltpu.get_barrier_semaphore()

    def greet(i, device):
        pl.semaphore_signal(barrier, inc=1, device_id=device, device_id_type=MESH)

    each(greet)
    hot = hot_ref[...]
    terms, at = 0.0, 0
    for ref in (part_ref, last_ref):
        sums = jnp.sum(ref[...], axis=1)
        where = hot[at : at + ref.shape[0]]
        at += ref.shape[0]
        used = jnp.max(where, axis=1, keepdims=True) > 0.0
        sums = jnp.sum(jnp.where(used, sums, 0.0), axis=1, keepdims=True)
        terms += jnp.sum(sums * where, axis=0, keepdims=True) * (1.0 / length)
    row = lax.broadcasted_iota(jnp.int32, rows.shape[1:], 0)
    rows[me] = jnp.where(row == 0, terms, targets_ref[...])

    def copy(i, device):
        return pltpu.make_async_remote_copy(
            src_ref=rows.at[me],
            dst_ref=rows.at[me],
            send_sem=send_sem.at[i],
            recv_sem=recv_sem.at[i],
            device_id=device,
            device_id_type=MESH,
        )

    pl.semaphore_wait(barrier, devices - 1)
    each(lambda i, device: copy(i, device).start())
    each(lambda i, device: copy(i, device).wait())
    both = jnp.sum(rows[...], axis=0)
    logits_ref[...] = both
    logits, targets = both[0:1], both[1:2]
    grad = (jax.nn.sigmoid(logits) - targets) * (loss_scale / length)
    scale_ref[...] = jnp.broadcast_to(
        jnp.sum(hot * grad, axis=1, keepdims=True), scale_ref.shape
    )


def run_logits(length, part, last_part, hot, targets, groups, shards):
    units, total = hot.shape
    devices = groups * shards
    vmem = pl.BlockSpec(memory_space=pltpu.VMEM)
    return pl.pallas_call(
        functools.partial(logit_kernel, length, groups, shards),
        in_specs=[vmem] * 4,
        out_specs=[vmem] * 2,
        out_shape=[
            jax.ShapeDtypeStruct((2, total), jnp.float32),
            jax.ShapeDtypeStruct((units, length), jnp.float32),
        ],
        scratch_shapes=[
            pltpu.VMEM((devices, 2, total), jnp.float32),
            pltpu.SemaphoreType.DMA((devices - 1,)),
            pltpu.SemaphoreType.DMA((devices - 1,)),
        ],
        compiler_params=params(63, collective_id=0, has_side_effects=True),
        cost_estimate=pl.CostEstimate(
            flops=6_000_000_000, bytes_accessed=4 * part.size, transcendentals=1000
        ),
    )(part, last_part, hot, targets)


def turn_heads(a, head_dim):
    return jnp.concatenate(
        [a[h : h + head_dim].T for h in range(0, a.shape[0], head_dim)], axis=1
    )


def hop_kernel(which, factor, head_dim, has_in, turn, turned_in, raw, x_ref, y_ref, s_ref, n_ref, *refs):
    scale_ref, dq_ref = refs[:2]
    arrived_ref = refs[2] if has_in else None
    raw_ref = None if raw is None else refs[2]
    out_ref, scales, terms, before, result, acc, sems = refs[-7:]
    half, cap = acc.shape[0], terms.shape[0]
    count = n_ref[which]
    start = s_ref[which]

    def copy(i):
        return pltpu.make_async_copy(dq_ref.at[start + i], terms.at[i], sems.at[i])

    def begin(i, carry):
        copy(i).start()
        return carry

    get_scales = pltpu.make_async_copy(scale_ref, scales, sems.at[cap])
    get_scales.start()
    lax.fori_loop(0, count, begin, 0)
    arrivals = []
    for m in range(half if has_in else 0):
        arrivals.append(
            pltpu.make_async_copy(arrived_ref.at[m], before.at[m], sems.at[cap + 1 + m])
        )
        arrivals[m].start()
    raws = []
    if raw is not None:
        many = raw_ref.shape[0]
        for i in range(many):
            raws.append(
                pltpu.make_async_copy(raw_ref.at[i], before.at[i], sems.at[cap + 1 + i])
            )
            raws[i].start()
    acc[...] = jnp.zeros_like(acc)
    get_scales.wait()

    def visit(i, carry):
        copy(i).wait()
        g = scales[pl.ds(start + i, 1), :] * factor
        acc[x_ref[start + i]] += g * terms[i].astype(jnp.float32)
        return carry

    lax.fori_loop(0, count, visit, 0)
    for i in range(len(raws)):
        raws[i].wait()
        way, c, first = raw
        row = first + way * many + i

        @pl.when((way * many + i < n_ref[s_ref.shape[0] + way]) & (y_ref[row] == c))
        def _(i=i, row=row):
            g = scales[row : row + 1, :] * factor
            acc[x_ref[row]] += g * before[i].astype(jnp.float32)

    results = []
    for m in range(half):
        if has_in:
            arrivals[m].wait()
        if turned_in:
            for h in range(0, acc.shape[1], head_dim):
                cols = slice(h, h + head_dim)
                mine = acc[m, cols].T + before[m, :, cols].astype(jnp.float32)
                result[m, :, cols] = mine.astype(jnp.bfloat16)
        else:
            mine = acc[m]
            if has_in:
                mine = mine + before[m].astype(jnp.float32)
            mine = mine.astype(jnp.bfloat16)
            result[m] = turn_heads(mine, head_dim) if turn else mine
        results.append(
            pltpu.make_async_copy(result.at[m], out_ref.at[m], sems.at[cap + 1 + before.shape[0] + m])
        )
        results[m].start()
    for put in results:
        put.wait()


def run_hop(which, cap, half, head_dim, lists, scale, dq, arrived, turn, turned_in, after, raw, raw_units):
    unit_x, unit_y, _, starts, counts = lists
    _, width, length = dq.shape
    hbm = pl.BlockSpec(memory_space=pltpu.HBM)
    anywhere = pl.BlockSpec(memory_space=pl.ANY)
    more = [a for a in (arrived, raw_units) if a is not None]
    many = half if raw is None else raw_units.shape[0]
    flat, turned = (half, width, length), (half, length, width)
    out = turned if turn else flat
    return pl.pallas_call(
        functools.partial(
            hop_kernel, which, head_dim ** (-0.5), head_dim, arrived is not None, turn, turned_in, raw
        ),
        grid_spec=pltpu.PrefetchScalarGridSpec(
            num_scalar_prefetch=4,
            in_specs=[anywhere, hbm] + [anywhere] * (len(more) + len(after)),
            out_specs=anywhere,
            scratch_shapes=[
                pltpu.VMEM(scale.shape, jnp.float32),
                pltpu.VMEM((cap, width, length), jnp.bfloat16),
                pltpu.VMEM(turned if turned_in else (many, width, length), jnp.bfloat16),
                pltpu.VMEM(out, jnp.bfloat16),
                pltpu.VMEM(flat, jnp.float32),
                pltpu.SemaphoreType.DMA((cap + 1 + many + half,)),
            ],
        ),
        out_shape=jax.ShapeDtypeStruct(out, jnp.bfloat16),
        compiler_params=params(63),
        cost_estimate=pl.CostEstimate(
            flops=4 * cap * width * length,
            bytes_accessed=2 * (cap + 3 * half) * width * length,
            transcendentals=0,
        ),
    )(unit_x, unit_y, starts, counts, scale, dq, *more, *after)


def sum_kernel(base, factor, y_ref, s_ref, n_ref, scale_ref, *refs):
    dks, dvs = refs[0:2], refs[2:4]
    out_ref, sk, sv = refs[4:]
    sk[...] = jnp.zeros_like(sk)
    sv[...] = jnp.zeros_like(sv)
    lists = s_ref.shape[0]
    totals = (
        s_ref[lists - 3] + n_ref[lists - 3],
        n_ref[lists - 2] + n_ref[lists - 1],
    )
    for dk_ref, dv_ref, total, at in zip(dks, dvs, totals, (0, base)):
        repeat = dk_ref.shape[2] // scale_ref.shape[1]

        def visit(u, carry, dk_ref=dk_ref, dv_ref=dv_ref, at=at, repeat=repeat):
            y = y_ref[at + u]
            g = jnp.concatenate([scale_ref[pl.ds(at + u, 1), :]] * repeat, axis=1)
            sk[y] += (g * factor) * dk_ref[u].astype(jnp.float32)
            sv[y] += g * dv_ref[u].astype(jnp.float32)
            return carry

        lax.fori_loop(0, total, visit, 0)
    out_ref[:, 1] = sk[...].astype(jnp.bfloat16)
    out_ref[:, 2] = sv[...].astype(jnp.bfloat16)


def run_sums(base, mols, factor, lists, scale, dks, dvs):
    _, unit_y, _, starts, counts = lists
    _, length, width = dks[0].shape
    units = dks[0].shape[0] + dks[1].shape[0]

    def rows(a):
        return pl.BlockSpec((a.shape[0], row_block, width), lambda i, y, s, n: (0, i, 0))

    return pl.pallas_call(
        functools.partial(sum_kernel, base, factor),
        grid_spec=pltpu.PrefetchScalarGridSpec(
            num_scalar_prefetch=3,
            grid=(length // row_block,),
            in_specs=[pl.BlockSpec(scale.shape, lambda i, y, s, n: (0, 0))]
            + [rows(a) for a in (*dks, *dvs)],
            out_specs=pl.BlockSpec((mols, 3, row_block, width), lambda i, y, s, n: (0, 0, i, 0)),
            scratch_shapes=[pltpu.VMEM((mols, row_block, width), jnp.float32)] * 2,
        ),
        out_shape=jax.ShapeDtypeStruct((mols, 3, length, width), jnp.bfloat16),
        compiler_params=params(63, dimension_semantics=("arbitrary",)),
        cost_estimate=pl.CostEstimate(
            flops=4 * units * length * width,
            bytes_accessed=4 * (2 * units + 3 * mols) * length * width,
            transcendentals=0,
        ),
    )(unit_y, starts, counts, scale, *dks, *dvs)


def final_kernel(half, low_ref, high_ref, low_last_ref, high_last_ref, _, out_ref):
    low = pl.program_id(0) * out_ref.shape[0] < half
    before = jnp.where(low, low_ref[...], high_ref[...]).astype(jnp.float32)
    last = jnp.where(low, low_last_ref[...], high_last_ref[...]).astype(jnp.float32)
    out_ref[:, 0] = (before + last).astype(jnp.bfloat16)


def run_final(half, before, last, grads):
    mols, _, length, width = grads.shape
    each = half // 2
    low = pl.BlockSpec((each, length, width), lambda i: (jnp.minimum(i, 1), 0, 0))
    high = pl.BlockSpec((each, length, width), lambda i: (jnp.maximum(i - 2, 0), 0, 0))
    return pl.pallas_call(
        functools.partial(final_kernel, half),
        grid=(mols // each,),
        in_specs=[low, high, low, high, pl.BlockSpec(memory_space=pl.ANY)],
        out_specs=pl.BlockSpec((each, 1, length, width), lambda i: (i, 0, 0, 0)),
        out_shape=jax.ShapeDtypeStruct(grads.shape, jnp.bfloat16),
        input_output_aliases={4: 0},
        compiler_params=params(63, dimension_semantics=("arbitrary",)),
        cost_estimate=pl.CostEstimate(
            flops=mols * width * length, bytes_accessed=6 * mols * width * length, transcendentals=0
        ),
    )(*before, *last, grads)


def local(mol_qkv, pair_list, head_proj, head_out, labels):
    groups = lax.axis_size("group")
    shards = lax.axis_size("fsdp")
    me = lax.axis_index("group")
    mols_here, length, _, _ = mol_qkv.shape
    heads, head_dim, inner = head_proj.shape
    total_pairs = pair_list.shape[0]
    per_owner = total_pairs // groups
    cap_pair = 2 * per_owner // groups
    cap = 2 * cap_pair
    most = per_owner + groups * cap_pair
    base = -(-most // 8) * 8
    extra = -(-cap // 8) * 8
    half = mols_here // 2
    far = groups // 2
    factor = head_dim ** (-0.5)
    ring = ring_of(groups)
    forth = [(ring[i], ring[(i + 1) % groups]) for i in range(groups)]
    back = [(b, a) for a, b in forth]

    mols = jnp.transpose(mol_qkv, (0, 2, 1, 3))
    own = [mols[:half, 0], mols[half:, 0]]

    lists = make_lists(
        me.reshape(1).astype(jnp.int32), pair_list, groups, half, base, extra, per_owner
    )
    *turned_kv, late_low, late_high = turn(mols, heads, head_dim)
    proj = head_proj * jnp.bfloat16(0.5)
    weights = (
        proj,
        jnp.transpose(proj, (0, 2, 1)),
        jnp.broadcast_to(head_out[:, :, None], (heads, inner, length)),
    )
    pairs = jnp.arange(total_pairs, dtype=jnp.int32)
    hot = (lists[2][:, None] == pairs[None, :]).astype(jnp.float32)
    targets = lax.dynamic_update_slice_in_dim(
        jnp.zeros((1, total_pairs), jnp.float32),
        labels.astype(jnp.float32)[None, :] * (lax.axis_index("fsdp") == 0),
        me * per_owner,
        1,
    )

    def units(event, q0, q1, held, after=()):
        at, room = (base, extra) if event == groups - 1 else (0, base)
        return run_units(
            event, at, room, lists, q0, q1, mols, turned_kv, weights, held, after
        )

    held = units(0, own[0], own[1], None)
    up, down = [own[0], late_high], [late_low, own[1]]
    for event in range(1, groups):
        c = (event + 1) % 2
        up[c] = lax.ppermute(up[c], "group", forth)
        down[1 - c] = lax.ppermute(down[1 - c], "group", back)
        if event < groups - 1:
            held = units(event, up[c], down[1 - c], held)
    part, dq, dk, dv = held
    last_part, last_dq, last_dk, last_dv = units(groups - 1, up[0], down[1], None, (part,))
    raw = {
        "up": lax.ppermute(last_dq[: extra // 2], "group", forth),
        "down": lax.ppermute(last_dq[extra // 2 :], "group", back),
    }
    logits, scale = run_logits(length, part, last_part, hot, targets, groups, shards)

    def hop(which, arrived, turn=False, turned_in=False, after=(), raw=None, raw_units=None):
        return run_hop(
            which, cap, half, head_dim, lists, scale, dq, arrived, turn, turned_in, after,
            raw, raw_units,
        )

    streams, latest = {}, {}

    def send(way, c, d):
        find, perm = (ahead_list, forth) if way == "up" else (behind_list, back)
        after = (latest[way],) if way in latest else ()
        got, units_got = None, None
        if d == far - 1:
            got, units_got = (int(way == "down"), c, base + extra), raw[way]
            if way == "down":
                got = (1, c, base + 2 * extra)
        mine = hop(
            find(d, c, groups), streams.get((way, c)), turn=d == 1, after=after,
            raw=got, raw_units=units_got,
        )
        latest[way] = mine
        streams[way, c] = lax.ppermute(mine, "group", perm)

    for d in range(far - 1, 0, -1):
        send("up", 0, d)
        send("down", 1, d)
        send("up", 1, d)
        send("down", 0, d)
    grads = run_sums(base, mols_here, factor, lists, scale, (dk, last_dk), (dv, last_dv))
    before = [
        hop(0, streams["up", 0], turn=True, turned_in=True),
        hop(1, streams["down", 1], turn=True, turned_in=True),
    ]
    arrived = [streams["down", 0], streams["up", 1]]
    grads = run_final(half, before, arrived, grads)
    mol_grad = jnp.transpose(grads, (0, 2, 1, 3))

    rows = logits[0]
    answers = logits[1]
    mean_loss = jnp.sum(jax.nn.softplus(rows) - answers * rows) / total_pairs
    own_logits = lax.dynamic_slice_in_dim(rows, me * per_owner, per_owner)
    return (mol_grad, own_logits, mean_loss)


def solution(mesh):
    placed = (
        P("group", None, None, "fsdp"),
        P(),
        P("fsdp", None, None),
        P("fsdp", None),
        P("group"),
    )
    return jax.shard_map(
        local,
        mesh=mesh,
        in_specs=placed,
        out_specs=(P("group", None, None, "fsdp"), P("group"), P()),
        check_vma=False,
    )
```

```python
import functools

import jax
import jax.numpy as jnp
from jax import lax
from jax.experimental import pallas as pl
from jax.experimental.pallas import tpu as pltpu
from jax.sharding import PartitionSpec as P

MESH = pl.DeviceIdType.MESH
loss_scale = 8192.0
row_block = 16

NN = (((1,), (0,)), ((), ()))
NT = (((1,), (1,)), ((), ()))


def mm(a, b, dims=NN):
    return lax.dot_general(a, b, dims, preferred_element_type=jnp.float32)


def params(mib, **more):
    return pltpu.CompilerParams(vmem_limit_bytes=mib * 1024 * 1024, **more)


def ring_of(groups):
    return list(range(0, groups, 2)) + list(range(groups - 1, 0, -2))


def place_of(group, groups):
    return jnp.where(group % 2 == 0, group // 2, groups - 1 - group // 2)


def behind_list(d, c, groups):
    if 2 * d == groups:
        return 2 * (groups - 1) + 2 * c
    return 2 * (2 * d - 1 + c)


def ahead_list(d, c, groups):
    if 2 * d == groups:
        return 2 * (groups - 1) + 2 * c
    return 2 * (2 * d - c) + 1


def list_kernel(groups, half, per_owner, me_ref, pairs_ref, x_ref, y_ref, p_ref, s_ref, n_ref, found):
    me = me_ref[0]
    my_place = place_of(me, groups)
    lists = 2 * groups + 2

    def clear(i, carry):
        x_ref[i] = 0
        y_ref[i] = 0
        p_ref[i] = -1
        return carry

    lax.fori_loop(0, x_ref.shape[0], clear, 0)
    for i in range(lists):
        n_ref[i] = 0

    def note(i, group, x, y, p):
        c = (x >= half).astype(jnp.int32)
        behind = my_place - place_of(group, groups)
        behind = jnp.where(behind < 0, behind + groups, behind)
        from_behind = 2 * (2 * behind - 1 + c)
        from_ahead = 2 * (2 * (groups - behind) - c) + 1
        at = jnp.where(behind * 2 < groups, from_behind, from_ahead)
        later = (x - half * c >= half // 2).astype(jnp.int32)
        at = jnp.where(behind * 2 == groups, 2 * (groups - 1) + 2 * c + later, at)
        at = jnp.where(behind == 0, c, at)
        found[0, i] = at
        found[1, i] = x - half * c
        found[2, i] = y
        found[3, i] = p
        n_ref[at] = n_ref[at] + 1

    def mine(i, carry):
        p = me * per_owner + i
        note(i, pairs_ref[3 * p + 1], pairs_ref[3 * p + 2], pairs_ref[3 * p], p)
        return carry

    lax.fori_loop(0, per_owner, mine, 0)

    def theirs(group, many):
        def visit(i, many):
            p = group * per_owner + i
            here = pairs_ref[3 * p + 1] == me

            @pl.when(here)
            def _():
                note(many, group, pairs_ref[3 * p], pairs_ref[3 * p + 2], p)

            return many + here.astype(jnp.int32)

        return lax.fori_loop(0, per_owner, visit, many)

    many = lax.fori_loop(0, groups, theirs, jnp.int32(per_owner))
    here = jnp.int32(0)
    for i in range(lists):
        s_ref[i] = here
        here = here + n_ref[i]
        n_ref[i] = 0

    def fill(i, carry):
        at = found[0, i]
        spot = s_ref[at] + n_ref[at]
        x_ref[spot] = found[1, i]
        y_ref[spot] = found[2, i]
        p_ref[spot] = found[3, i]
        n_ref[at] = n_ref[at] + 1
        return carry

    lax.fori_loop(0, many, fill, 0)


def make_lists(me, pair_list, groups, half, size, per_owner):
    smem = pl.BlockSpec(memory_space=pltpu.SMEM)
    table = jax.ShapeDtypeStruct((size,), jnp.int32)
    short = jax.ShapeDtypeStruct((2 * groups + 2,), jnp.int32)
    return pl.pallas_call(
        functools.partial(list_kernel, groups, half, per_owner),
        in_specs=[smem, smem],
        out_specs=[smem] * 5,
        out_shape=[table, table, table, short, short],
        scratch_shapes=[pltpu.SMEM((4, size), jnp.int32)],
        cost_estimate=pl.CostEstimate(flops=1000, bytes_accessed=4000, transcendentals=0),
    )(me, pair_list.reshape(-1))


def turn_kernel(head_dim, half, q_ref, k_ref, v_ref, kt_ref, vt_ref, low_ref, high_ref):
    for h in range(kt_ref.shape[1]):
        cols = slice(h * head_dim, (h + 1) * head_dim)
        kt_ref[0, h] = k_ref[0, 0, :, cols].T
        vt_ref[0, h] = v_ref[0, 0, :, cols].T

    @pl.when(pl.program_id(0) < half)
    def _():
        low_ref[...] = q_ref[:, 0]

    @pl.when(pl.program_id(0) >= half)
    def _():
        high_ref[...] = q_ref[:, 0]


def turn(mols, heads, head_dim):
    count, _, length, width = mols.shape
    half = count // 2
    out = jax.ShapeDtypeStruct((count, heads, head_dim, length), jnp.bfloat16)
    part = jax.ShapeDtypeStruct((half, length, width), jnp.bfloat16)
    out_spec = pl.BlockSpec((1, heads, head_dim, length), lambda i: (i, 0, 0, 0))

    def rows(c):
        return pl.BlockSpec((1, 1, length, width), lambda i: (i, c, 0, 0))

    return pl.pallas_call(
        functools.partial(turn_kernel, head_dim, half),
        grid=(count,),
        in_specs=[rows(0), rows(1), rows(2)],
        out_specs=[
            out_spec,
            out_spec,
            pl.BlockSpec((1, length, width), lambda i: (jnp.minimum(i, half - 1), 0, 0)),
            pl.BlockSpec((1, length, width), lambda i: (jnp.maximum(i - half, 0), 0, 0)),
        ],
        out_shape=[out, out, part, part],
        compiler_params=params(63),
        cost_estimate=pl.CostEstimate(
            flops=4_000_000_000,
            bytes_accessed=12 * count * length * width,
            transcendentals=0,
        ),
    )(mols, mols, mols)


def unit_body(head_dim, use_low, refs):
    q0_ref, q1_ref, k_ref, v_ref, kt_ref, vt_ref = refs[:6]
    proj_ref, turned_ref, out_ref = refs[6:9]
    part_ref, dq_ref, dk_ref, dv_ref = refs[9:]
    coef = 1.4426950408889634 * head_dim ** (-0.5)
    length = k_ref.shape[2]
    total = jnp.zeros((8, length), jnp.float32)
    hs = range(proj_ref.shape[0])

    def col(h):
        return slice(h * head_dim, (h + 1) * head_dim)

    q = [jnp.where(use_low, q0_ref[0, :, col(h)], q1_ref[0, :, col(h)]) for h in hs]
    s = [mm(k_ref[0, 0, :, col(h)], q[h], NT) for h in hs]
    w = [jnp.exp2((a - jnp.max(a, axis=0, keepdims=True)) * coef) for a in s]
    w = [a * (1.0 / jnp.sum(a, axis=0, keepdims=True)) for a in w]
    wb = [a.astype(jnp.bfloat16) for a in w]
    context = [mm(vt_ref[0, h], wb[h]).astype(jnp.bfloat16) for h in hs]
    dhidden = []
    for h in hs:
        hidden = mm(turned_ref[h], context[h])
        bend = jnp.tanh(hidden)
        first = (1.0 + bend) * out_ref[h]
        silu = hidden * first
        total += jnp.sum(silu.reshape(-1, 8, length), axis=0)
        dhidden.append((first + silu * (1.0 - bend)).astype(jnp.bfloat16))
    dcontext = [mm(proj_ref[h], dhidden[h]).astype(jnp.bfloat16) for h in hs]
    dw = [mm(v_ref[0, 0, :, col(h)], dcontext[h]) for h in hs]
    for h in hs:
        dv_ref[0, :, col(h)] = mm(wb[h], dcontext[h], NT).astype(jnp.bfloat16)
    ds = []
    for h in hs:
        inner = jnp.sum(dw[h] * w[h], axis=0, keepdims=True)
        ds.append((w[h] * (dw[h] - inner)).astype(jnp.bfloat16))
    for h in hs:
        dq_ref[0, col(h)] = mm(kt_ref[0, h], ds[h]).astype(jnp.bfloat16)
        dk_ref[0, :, col(h)] = mm(ds[h], q[h]).astype(jnp.bfloat16)
    part_ref[0] = total


def unit_kernel(head_dim, first, second, shift, x_ref, y_ref, s_ref, n_ref, *refs):
    sources = refs[:5]
    weights = refs[5:8]
    results = refs[-5:-1]
    turns = refs[-1]
    heads = weights[0].shape[0]
    length, width = sources[0].shape[1:]
    low = n_ref[first]
    total = low + n_ref[second]
    rows, last = sources[0].shape[0], x_ref.shape[0] - 1

    def spot(u):
        return jnp.where(u < low, s_ref[first] + u, s_ref[second] + u - low)

    def local_x(which, u):
        u = jnp.maximum(jnp.minimum(u, n_ref[which] - 1), 0)
        x = x_ref[jnp.minimum(s_ref[which] + u, last)] - shift
        return jnp.maximum(jnp.minimum(x, rows - 1), 0)

    def low_map(u):
        return (local_x(first, u), 0, 0)

    def high_map(u):
        return (local_x(second, u - low), 0, 0)

    def kv_map(u):
        return (y_ref[spot(u)], 0, 0, 0)

    def row_map(u):
        return (spot(u), 0, 0)

    turns[0] = 0

    def step(*blocks):
        u = turns[0]
        turns[0] = u + 1
        unit_body(head_dim, u < low, (*blocks[:6], *weights, *blocks[6:]))

    kv_spec = pl.BlockSpec((1, heads, head_dim, length), kv_map)
    row_spec = pl.BlockSpec((1, length, width), row_map)

    @pl.when(total > 0)
    def _():
        pltpu.emit_pipeline(
            step,
            grid=(total,),
            in_specs=[
                pl.BlockSpec((1, length, width), low_map),
                pl.BlockSpec((1, length, width), high_map),
                pl.BlockSpec((1, 1, length, width), lambda u: (y_ref[spot(u)], 1, 0, 0)),
                pl.BlockSpec((1, 1, length, width), lambda u: (y_ref[spot(u)], 2, 0, 0)),
                kv_spec,
                kv_spec,
            ],
            out_specs=[
                pl.BlockSpec((1, 8, length), row_map),
                pl.BlockSpec((1, width, length), row_map),
                row_spec,
                row_spec,
            ],
        )(sources[0], sources[1], sources[2], sources[2], *sources[3:], *results)


def run_units(which, room, lists, q0, q1, mols, turned_kv, weights, held):
    unit_x, unit_y, _, starts, counts = lists
    proj, turned, readout = weights
    heads, head_dim, inner = proj.shape
    _, _, length, width = mols.shape
    rows = jax.ShapeDtypeStruct((room, length, width), jnp.bfloat16)
    hbm = pl.BlockSpec(memory_space=pltpu.HBM)
    vmem = pl.BlockSpec(memory_space=pltpu.VMEM)
    operands = [q0, q1, mols, *turned_kv, proj, turned, readout]
    in_specs = [pl.BlockSpec(memory_space=pl.ANY)] * 2 + [hbm] * 3 + [vmem] * 3
    aliases = {}
    if held is not None:
        aliases = {4 + len(operands) + i: i for i in range(4)}
        in_specs += [hbm] * 4
        operands += list(held)
    return pl.pallas_call(
        functools.partial(unit_kernel, head_dim, *which),
        grid_spec=pltpu.PrefetchScalarGridSpec(
            num_scalar_prefetch=4,
            in_specs=in_specs,
            out_specs=[hbm] * 4,
            scratch_shapes=[pltpu.SMEM((1,), jnp.int32)],
        ),
        out_shape=[
            jax.ShapeDtypeStruct((room, 8, length), jnp.float32),
            jax.ShapeDtypeStruct((room, width, length), jnp.bfloat16),
            rows,
            rows,
        ],
        input_output_aliases=aliases,
        compiler_params=params(63),
        cost_estimate=pl.CostEstimate(
            flops=640 * heads * length * length * head_dim,
            bytes_accessed=48 * length * width,
            transcendentals=4 * heads * length * (length + inner),
        ),
    )(unit_x, unit_y, starts, counts, *operands)


def logit_kernel(length, groups, shards, part_ref, hot_ref, targets_ref, *refs):
    logits_ref, scale_ref, rows, send_sem, recv_sem = refs
    me = lax.axis_index("group") * shards + lax.axis_index("fsdp")
    devices = groups * shards
    few = devices <= 32

    def each(visit):
        def body(d, carry):
            other = lax.rem(me + d, devices)
            visit(d - 1, {"group": other // shards, "fsdp": lax.rem(other, shards)})
            return carry

        lax.fori_loop(1, devices, body, 0, unroll=few)

    barrier = pltpu.get_barrier_semaphore()

    def greet(i, device):
        pl.semaphore_signal(barrier, inc=1, device_id=device, device_id_type=MESH)

    each(greet)
    hot = hot_ref[...]
    mine = jnp.sum(part_ref[...], axis=1)
    used = jnp.max(hot, axis=1, keepdims=True) > 0.0
    mine = jnp.sum(jnp.where(used, mine, 0.0), axis=1, keepdims=True)
    terms = jnp.sum(mine * hot, axis=0, keepdims=True) * (1.0 / length)
    row = lax.broadcasted_iota(jnp.int32, rows.shape[1:], 0)
    rows[me] = jnp.where(row == 0, terms, targets_ref[...])

    def copy(i, device):
        return pltpu.make_async_remote_copy(
            src_ref=rows.at[me],
            dst_ref=rows.at[me],
            send_sem=send_sem.at[i],
            recv_sem=recv_sem.at[i],
            device_id=device,
            device_id_type=MESH,
        )

    pl.semaphore_wait(barrier, devices - 1)
    each(lambda i, device: copy(i, device).start())
    each(lambda i, device: copy(i, device).wait())
    both = jnp.sum(rows[...], axis=0)
    logits_ref[...] = both
    logits, targets = both[0:1], both[1:2]
    grad = (jax.nn.sigmoid(logits) - targets) * (loss_scale / length)
    scale_ref[...] = jnp.broadcast_to(
        jnp.sum(hot * grad, axis=1, keepdims=True), scale_ref.shape
    )


def run_logits(length, part, hot, targets, groups, shards):
    units, total = hot.shape
    devices = groups * shards
    vmem = pl.BlockSpec(memory_space=pltpu.VMEM)
    return pl.pallas_call(
        functools.partial(logit_kernel, length, groups, shards),
        in_specs=[vmem] * 3,
        out_specs=[vmem] * 2,
        out_shape=[
            jax.ShapeDtypeStruct((2, total), jnp.float32),
            jax.ShapeDtypeStruct((units, length), jnp.float32),
        ],
        scratch_shapes=[
            pltpu.VMEM((devices, 2, total), jnp.float32),
            pltpu.SemaphoreType.DMA((devices - 1,)),
            pltpu.SemaphoreType.DMA((devices - 1,)),
        ],
        compiler_params=params(63, collective_id=0, has_side_effects=True),
        cost_estimate=pl.CostEstimate(
            flops=6_000_000_000, bytes_accessed=4 * part.size, transcendentals=1000
        ),
    )(part, hot, targets)


def turn_heads(a, head_dim):
    return jnp.concatenate(
        [a[h : h + head_dim].T for h in range(0, a.shape[0], head_dim)], axis=1
    )


def hop_kernel(which, factor, head_dim, has_in, turn, turned_in, x_ref, s_ref, n_ref, *refs):
    scale_ref, dq_ref = refs[:2]
    arrived_ref = refs[2] if has_in else None
    out_ref, scales, terms, before, result, acc, sems = refs[-7:]
    half, cap = acc.shape[0], terms.shape[0]
    count = n_ref[which]
    if which >= n_ref.shape[0] - 4:
        count = count + n_ref[which + 1]
    start = s_ref[which]

    def copy(i):
        return pltpu.make_async_copy(dq_ref.at[start + i], terms.at[i], sems.at[i])

    def begin(i, carry):
        copy(i).start()
        return carry

    get_scales = pltpu.make_async_copy(scale_ref, scales, sems.at[cap])
    get_scales.start()
    lax.fori_loop(0, count, begin, 0)
    arrivals = []
    for m in range(half if has_in else 0):
        arrivals.append(
            pltpu.make_async_copy(arrived_ref.at[m], before.at[m], sems.at[cap + 1 + m])
        )
        arrivals[m].start()
    acc[...] = jnp.zeros_like(acc)
    get_scales.wait()

    def visit(i, carry):
        copy(i).wait()
        g = scales[pl.ds(start + i, 1), :] * factor
        acc[x_ref[start + i]] += g * terms[i].astype(jnp.float32)
        return carry

    lax.fori_loop(0, count, visit, 0)
    results = []
    for m in range(half):
        if has_in:
            arrivals[m].wait()
        if turned_in:
            for h in range(0, acc.shape[1], head_dim):
                cols = slice(h, h + head_dim)
                mine = acc[m, cols].T + before[m, :, cols].astype(jnp.float32)
                result[m, :, cols] = mine.astype(jnp.bfloat16)
        else:
            mine = acc[m]
            if has_in:
                mine = mine + before[m].astype(jnp.float32)
            mine = mine.astype(jnp.bfloat16)
            result[m] = turn_heads(mine, head_dim) if turn else mine
        results.append(
            pltpu.make_async_copy(result.at[m], out_ref.at[m], sems.at[cap + 1 + half + m])
        )
        results[m].start()
    for put in results:
        put.wait()


def run_hop(which, cap, half, head_dim, lists, scale, dq, arrived, turn, turned_in, after):
    unit_x, _, _, starts, counts = lists
    _, width, length = dq.shape
    hbm = pl.BlockSpec(memory_space=pltpu.HBM)
    anywhere = pl.BlockSpec(memory_space=pl.ANY)
    more = [] if arrived is None else [arrived]
    flat, turned = (half, width, length), (half, length, width)
    out = turned if turn else flat
    return pl.pallas_call(
        functools.partial(
            hop_kernel, which, head_dim ** (-0.5), head_dim, bool(more), turn, turned_in
        ),
        grid_spec=pltpu.PrefetchScalarGridSpec(
            num_scalar_prefetch=3,
            in_specs=[anywhere, hbm] + [anywhere] * (len(more) + len(after)),
            out_specs=anywhere,
            scratch_shapes=[
                pltpu.VMEM(scale.shape, jnp.float32),
                pltpu.VMEM((cap, width, length), jnp.bfloat16),
                pltpu.VMEM(turned if turned_in else flat, jnp.bfloat16),
                pltpu.VMEM(out, jnp.bfloat16),
                pltpu.VMEM(flat, jnp.float32),
                pltpu.SemaphoreType.DMA((cap + 1 + 2 * half,)),
            ],
        ),
        out_shape=jax.ShapeDtypeStruct(out, jnp.bfloat16),
        compiler_params=params(63),
        cost_estimate=pl.CostEstimate(
            flops=4 * cap * width * length,
            bytes_accessed=2 * (cap + 3 * half) * width * length,
            transcendentals=0,
        ),
    )(unit_x, starts, counts, scale, dq, *more, *after)


def sum_kernel(factor, y_ref, s_ref, n_ref, scale_ref, dk_ref, dv_ref, out_ref, sk, sv):
    sk[...] = jnp.zeros_like(sk)
    sv[...] = jnp.zeros_like(sv)
    last = n_ref.shape[0] - 1
    repeat = dk_ref.shape[2] // scale_ref.shape[1]

    def visit(u, carry):
        y = y_ref[u]
        g = jnp.concatenate([scale_ref[pl.ds(u, 1), :]] * repeat, axis=1)
        sk[y] += (g * factor) * dk_ref[u].astype(jnp.float32)
        sv[y] += g * dv_ref[u].astype(jnp.float32)
        return carry

    lax.fori_loop(0, s_ref[last] + n_ref[last], visit, 0)
    out_ref[:, 1] = sk[...].astype(jnp.bfloat16)
    out_ref[:, 2] = sv[...].astype(jnp.bfloat16)


def run_sums(mols, factor, lists, scale, dk, dv):
    _, unit_y, _, starts, counts = lists
    units, length, width = dk.shape
    rows = pl.BlockSpec((units, row_block, width), lambda i, y, s, n: (0, i, 0))
    return pl.pallas_call(
        functools.partial(sum_kernel, factor),
        grid_spec=pltpu.PrefetchScalarGridSpec(
            num_scalar_prefetch=3,
            grid=(length // row_block,),
            in_specs=[pl.BlockSpec(scale.shape, lambda i, y, s, n: (0, 0)), rows, rows],
            out_specs=pl.BlockSpec((mols, 3, row_block, width), lambda i, y, s, n: (0, 0, i, 0)),
            scratch_shapes=[pltpu.VMEM((mols, row_block, width), jnp.float32)] * 2,
        ),
        out_shape=jax.ShapeDtypeStruct((mols, 3, length, width), jnp.bfloat16),
        compiler_params=params(63, dimension_semantics=("arbitrary",)),
        cost_estimate=pl.CostEstimate(
            flops=4 * units * length * width,
            bytes_accessed=4 * (2 * units + 3 * mols) * length * width,
            transcendentals=0,
        ),
    )(unit_y, starts, counts, scale, dk, dv)


def final_kernel(half, low_ref, high_ref, low_last_ref, high_last_ref, _, out_ref):
    low = pl.program_id(0) * out_ref.shape[0] < half
    before = jnp.where(low, low_ref[...], high_ref[...]).astype(jnp.float32)
    last = jnp.where(low, low_last_ref[...], high_last_ref[...]).astype(jnp.float32)
    out_ref[:, 0] = (before + last).astype(jnp.bfloat16)


def run_final(half, before, last, grads):
    mols, _, length, width = grads.shape
    each = half // 2
    low = pl.BlockSpec((each, length, width), lambda i: (jnp.minimum(i, 1), 0, 0))
    high = pl.BlockSpec((each, length, width), lambda i: (jnp.maximum(i - 2, 0), 0, 0))
    return pl.pallas_call(
        functools.partial(final_kernel, half),
        grid=(mols // each,),
        in_specs=[low, high, low, high, pl.BlockSpec(memory_space=pl.ANY)],
        out_specs=pl.BlockSpec((each, 1, length, width), lambda i: (i, 0, 0, 0)),
        out_shape=jax.ShapeDtypeStruct(grads.shape, jnp.bfloat16),
        input_output_aliases={4: 0},
        compiler_params=params(63, dimension_semantics=("arbitrary",)),
        cost_estimate=pl.CostEstimate(
            flops=mols * width * length, bytes_accessed=6 * mols * width * length, transcendentals=0
        ),
    )(*before, *last, grads)


def local(mol_qkv, pair_list, head_proj, head_out, labels):
    groups = lax.axis_size("group")
    shards = lax.axis_size("fsdp")
    me = lax.axis_index("group")
    mols_here, length, _, _ = mol_qkv.shape
    heads, head_dim, inner = head_proj.shape
    total_pairs = pair_list.shape[0]
    per_owner = total_pairs // groups
    cap_pair = 2 * per_owner // groups
    cap = 2 * cap_pair
    most = per_owner + groups * cap_pair
    room = -(-most // 8) * 8
    half = mols_here // 2
    far = groups // 2
    factor = head_dim ** (-0.5)
    ring = ring_of(groups)
    forth = [(ring[i], ring[(i + 1) % groups]) for i in range(groups)]
    back = [(b, a) for a, b in forth]

    mols = jnp.transpose(mol_qkv, (0, 2, 1, 3))
    own = [mols[:half, 0], mols[half:, 0]]

    lists = make_lists(
        me.reshape(1).astype(jnp.int32), pair_list, groups, half, room, per_owner
    )
    *turned_kv, late_low, late_high = turn(mols, heads, head_dim)
    proj = head_proj * jnp.bfloat16(0.5)
    weights = (
        proj,
        jnp.transpose(proj, (0, 2, 1)),
        jnp.broadcast_to(head_out[:, :, None], (heads, inner, length)),
    )
    pairs = jnp.arange(total_pairs, dtype=jnp.int32)
    hot = (lists[2][:, None] == pairs[None, :]).astype(jnp.float32)
    targets = lax.dynamic_update_slice_in_dim(
        jnp.zeros((1, total_pairs), jnp.float32),
        labels.astype(jnp.float32)[None, :] * (lax.axis_index("fsdp") == 0),
        me * per_owner,
        1,
    )

    def units(which, q0, q1, held):
        return run_units(which, room, lists, q0, q1, mols, turned_kv, weights, held)

    held = units((0, 1, 0), own[0], own[1], None)
    up, down = [own[0], late_high], [late_low, own[1]]
    for event in range(1, groups - 1):
        c = (event + 1) % 2
        up[c] = lax.ppermute(up[c], "group", forth)
        down[1 - c] = lax.ppermute(down[1 - c], "group", back)
        held = units((2 * event, 2 * event + 1, 0), up[c], down[1 - c], held)
    quarter = half // 2
    for i in range(2):
        rows = slice(i * quarter, (i + 1) * quarter)
        low = lax.ppermute(up[0][rows], "group", forth)
        high = lax.ppermute(down[1][rows], "group", back)
        first = 2 * (groups - 1) + i
        held = units((first, first + 2, i * quarter), low, high, held)
    part, dq, dk, dv = held
    logits, scale = run_logits(length, part, hot, targets, groups, shards)

    def hop(which, arrived, turn=False, turned_in=False, after=()):
        return run_hop(
            which, cap, half, head_dim, lists, scale, dq, arrived, turn, turned_in, after
        )

    streams, latest = {}, {}

    def send(way, c, d):
        find, perm = (ahead_list, forth) if way == "up" else (behind_list, back)
        after = (latest[way],) if way in latest else ()
        mine = hop(find(d, c, groups), streams.get((way, c)), turn=d == 1, after=after)
        latest[way] = mine
        streams[way, c] = lax.ppermute(mine, "group", perm)

    for d in range(far, 0, -1):
        send("up", 0, d)
        send("down", 1, d)
        if d > 1:
            send("up", 1, d - 1)
            send("down", 0, d - 1)
    grads = run_sums(mols_here, factor, lists, scale, dk, dv)
    before = [
        hop(0, streams["down", 0], turn=True, turned_in=True),
        hop(1, streams["up", 1], turn=True, turned_in=True),
    ]
    grads = run_final(half, before, [streams["up", 0], streams["down", 1]], grads)
    mol_grad = jnp.transpose(grads, (0, 2, 1, 3))

    rows = logits[0]
    answers = logits[1]
    mean_loss = jnp.sum(jax.nn.softplus(rows) - answers * rows) / total_pairs
    own_logits = lax.dynamic_slice_in_dim(rows, me * per_owner, per_owner)
    return (mol_grad, own_logits, mean_loss)


def solution(mesh):
    placed = (
        P("group", None, None, "fsdp"),
        P(),
        P("fsdp", None, None),
        P("fsdp", None),
        P("group"),
    )
    return jax.shard_map(
        local,
        mesh=mesh,
        in_specs=placed,
        out_specs=(P("group", None, None, "fsdp"), P("group"), P()),
        check_vma=False,
    )
```
